32 devices in a mesh: seq: 8 (over y, x, core), head: 4 (over z).
Axes of the slice: x: 2, y: 2, z: 4, core: 2. Of those that a mesh axis runs over, the one named last changes fastest.
Arguments:
- tokens: bfloat16 [32, 1024, 768], P('seq', 'head'), may hold values from -6 to 6
- skip_values: bfloat16 [32, 1024, 384], P('seq', 'head'), may hold values from -6 to 6
- segments: int32 [32, 1024], P('seq', 'head'), may hold values from 0 to 3, as said below
- token_mask: int32 [32, 1024], P('seq', 'head'), may hold values 0 or 1
- attn_gain: bfloat16 [768], replicated, may hold values from 0.099609375 to 1.8984375
- attn_shift: bfloat16 [768], replicated, may hold values from -1.75 to 1.75
- w_qkv: bfloat16 [768, 1920], replicated, may hold values from -0.21875 to 0.21875
- q_bias: bfloat16 [768], replicated, may hold values from -3 to 3
- v_bias: bfloat16 [384], replicated, may hold values from -3 to 3
- w_out: bfloat16 [768, 768], replicated, may hold values from -0.875 to 0.875
- out_bias: bfloat16 [768], replicated, may hold values from -1.75 to 1.75
- mlp_gain: bfloat16 [768], replicated, may hold values from 0.099609375 to 1.8984375
- mlp_shift: bfloat16 [768], replicated, may hold values from -1.75 to 1.75
- w_up: bfloat16 [768, 3072], replicated, may hold values from -0.21875 to 0.21875
- up_bias: bfloat16 [3072], replicated, may hold values from -3 to 3
- w_down: bfloat16 [3072, 768], replicated, may hold values from -0.109375 to 0.109375
- down_bias: bfloat16 [768], replicated, may hold values from -1.75 to 1.75
- cotangent: bfloat16 [32, 1024, 768], P('seq', 'head'), may hold values from -6 to 6
Outputs:
- layer_out: bfloat16 [32, 1024, 768], P('seq', 'head')
- grad_tokens: float32 [32, 1024, 768], P('seq', 'head')
- grad_skip_values: float32 [32, 1024, 384], P('seq', 'head')
- grad_attn_gain: float32 [768], replicated
- grad_attn_shift: float32 [768], replicated
- grad_w_qkv: float32 [768, 1920], P('seq')
- grad_q_bias: float32 [768], replicated
- grad_v_bias: float32 [384], replicated
- grad_w_out: float32 [768, 768], P('seq')
- grad_out_bias: float32 [768], replicated
- grad_mlp_gain: float32 [768], replicated
- grad_mlp_shift: float32 [768], replicated
- grad_w_up: float32 [768, 3072], P('seq')
- grad_up_bias: float32 [3072], replicated
- grad_w_down: float32 [3072, 768], P('seq')
- grad_down_bias: float32 [768], replicated
The draws below stay inside these ranges and needn't reach their ends.
Inputs may be any that keep to these rules, and one draw needn't show every extreme that they name: `segments`: within each row the document numbers start at 0 and never fall; in each aligned group of 4 rows one row is a single document, and every other row holds exactly four documents.
All inputs are finite; a program needn't handle non-finite values. No bound on the sum of `token_mask` on one device may be relied on, other than what follows from the above.
Results may differ from the reference program's by a relative error of at most 0.017.
Values may be sent and summed in bfloat16 or wider, within the bound.
No kernel may reach another device: no remote copies, remote signals or barrier semaphores. Data moves between devices by JAX's collectives and lax.ppermute only.
A program may use at most 320 MiB of HBM per device.

```python
from functools import partial
import jax
import jax.numpy as jnp
from jax import lax

D = 768
HEADS = 12
HDIM = 64
FF = 3072
HALF = 384
LENGTH = 1024
ROWS_GRP = 4
ROWS = 32


def draw_segments(key, part):
    key_breaks = jax.random.fold_in(key, 11)
    key_whole = jax.random.fold_in(key, 23)
    row_keys = jax.random.split(key_breaks, ROWS)
    orders = jax.vmap(lambda row_key: jax.random.permutation(row_key, LENGTH - 1))(row_keys)
    places = orders[:, :3] + 1
    positions = jnp.arange(LENGTH)
    breaks = jnp.sum((positions[None, None, :] == places[:, :, None]).astype(jnp.int32), axis=1)
    chosen = jax.random.randint(key_whole, (ROWS // ROWS_GRP,), 0, ROWS_GRP)
    row_ids = jnp.arange(ROWS)
    whole_row = row_ids % ROWS_GRP == chosen[row_ids // ROWS_GRP]
    breaks = jnp.where(whole_row[:, None], 0, breaks)
    return jnp.cumsum(breaks, axis=1).astype(jnp.int32)


def with_ends(values, rng, least, high):
    longest = values.shape.index(max(values.shape))
    spots = []
    for shift in (0, 1):
        where = [jax.random.randint(jax.random.fold_in(rng, axis), (), 0, length) for axis, length in enumerate(values.shape)]
        where[longest] = (where[longest] + shift) % values.shape[longest]
        spots.append(tuple(where))
    return values.at[spots[0]].set(least).at[spots[1]].set(high)


def spiked(values, key, source, target, shards_of, factor):
    def block_of(axis_at):
        return (jnp.arange(values.shape[axis_at]) // (values.shape[axis_at] // shards_of)).reshape((-1,) + (1,) * (values.ndim - 1 - axis_at))

    first = jax.random.permutation(key, shards_of)[block_of(target)]
    second = (block_of(target) + shards_of // 2) % shards_of
    return jnp.where((block_of(source) == first) | (block_of(source) == second), factor * values, values)


def shard_levels(own_key, dims, pieces, low, largest):
    def one(dim, shards_of):
        heights = jax.random.uniform(jax.random.fold_in(jax.random.fold_in(own_key, 6), dim), (shards_of,), jnp.float32, low / len(pieces), largest / len(pieces))
        return jnp.repeat(jnp.exp(heights), dims[dim] // shards_of).reshape((-1,) + (1,) * (len(dims) - dim - 1))

    factor_of = one(*pieces[0])
    for cut in pieces[1:]:
        factor_of = factor_of * one(*cut)
    return factor_of


def bell_draw(own_key, dims, scale, limit, cuts=(), held_as=jnp.bfloat16):
    entries = scale * jax.random.normal(own_key, dims, jnp.float32)
    if cuts:
        entries = entries * shard_levels(own_key, dims, cuts, -0.22, 0.18)
    return jnp.clip(entries, -limit, limit).astype(held_as)


def noise_with(stream_key, extent, width, limit, pieces, heavy, held_as=jnp.bfloat16):
    drawn = width * jax.random.normal(stream_key, extent, jnp.float32)
    if pieces:
        drawn = drawn * shard_levels(stream_key, extent, pieces, -0.22, 0.18)
    return jnp.clip(spiked(drawn, jax.random.fold_in(stream_key, 3), *heavy), -limit, limit).astype(held_as)


def setup_inputs(seed: int = 0) -> dict:
    key_of = jax.random.split(jax.random.key(seed), 19)
    tokens = noise_with(key_of[0], (ROWS, LENGTH, D), 1.0, 6.0, ((0, 8), (1, 4)), (0, 2, 8, 2.0))
    skip_values = bell_draw(key_of[1], (ROWS, LENGTH, HALF), 1.0, 6.0, ((0, 8), (1, 4)))
    segments = draw_segments(jax.random.fold_in(key_of[18], 71), 0)
    token_mask = with_ends((jax.random.randint(key_of[3], (ROWS, LENGTH), 0, 8) < 7).astype(jnp.int32), jax.random.fold_in(key_of[3], 1), 0, 1)
    attn_gain = jnp.clip(1.0 + 0.18 * jax.random.normal(key_of[4], (D,), jnp.float32), 0.099609375, 1.8984375).astype(jnp.bfloat16)
    attn_shift = bell_draw(key_of[5], (D,), 0.3, 1.75)
    w_qkv = bell_draw(key_of[6], (D, 2 * D + HALF), D ** -0.5, 0.21875)
    q_bias = bell_draw(key_of[7], (D,), 0.5, 3.0)
    v_bias = bell_draw(key_of[8], (HALF,), 0.5, 3.0)
    w_out = bell_draw(key_of[9], (D, D), (D // 16) ** -0.5, 0.875)
    out_bias = bell_draw(key_of[10], (D,), 0.3, 1.75)
    mlp_gain = jnp.clip(1.0 + 0.18 * jax.random.normal(key_of[11], (D,), jnp.float32), 0.099609375, 1.8984375).astype(jnp.bfloat16)
    mlp_shift = bell_draw(key_of[12], (D,), 0.3, 1.75)
    w_up = bell_draw(key_of[13], (D, FF), D ** -0.5, 0.21875)
    up_bias = bell_draw(key_of[14], (FF,), 0.5, 3.0)
    w_down = bell_draw(key_of[15], (FF, D), FF ** -0.5, 0.109375)
    down_bias = bell_draw(key_of[16], (D,), 0.3, 1.75)
    cotangent = noise_with(key_of[17], (ROWS, LENGTH, D), 1.0, 6.0, ((0, 8), (1, 4)), (0, 2, 8, 2.0))
    return dict(tokens=tokens, skip_values=skip_values, segments=segments, token_mask=token_mask, attn_gain=attn_gain, attn_shift=attn_shift, w_qkv=w_qkv, q_bias=q_bias, v_bias=v_bias, w_out=w_out, out_bias=out_bias, mlp_gain=mlp_gain, mlp_shift=mlp_shift, w_up=w_up, up_bias=up_bias, w_down=w_down, down_bias=down_bias, cotangent=cotangent)


EPSILON = 1e-05
MASKED = -1e+30
HIGHEST = lax.Precision.HIGHEST

@jax.custom_vjp
def low(v):
    return lax.optimization_barrier(v.astype(jnp.bfloat16)).astype(jnp.float32)

@jax.custom_vjp
def low_back(v):
    return v

def low_keep(v):
    return (low(v), None)

def low_pass(kept, grad):
    return (grad,)

def back_keep(v):
    return (v, None)

def back_low(kept, grad):
    return (low(grad),)
low.defvjp(low_keep, low_pass)
low_back.defvjp(back_keep, back_low)

def layer_norm(inputs, norm_gain, norm_shift):
    center = inputs - lax.optimization_barrier(jnp.mean(inputs, axis=-1, keepdims=True))
    spread = lax.optimization_barrier(jnp.mean(center * center, axis=-1, keepdims=True))
    return center * lax.rsqrt(spread + EPSILON) * norm_gain + norm_shift

def matmul(left, right):
    return jnp.dot(left, right, precision=HIGHEST, preferred_element_type=jnp.float32)

def forward_row(params, row_tokens, row_skip, row_segments, row_mask):
    attn_gain, attn_shift, w_qkv, q_bias, v_bias, w_out, out_bias, mlp_gain, mlp_shift, w_up, up_bias, w_down, down_bias = params
    normed = low(layer_norm(row_tokens, attn_gain, attn_shift))
    project = matmul(normed, w_qkv)
    queries = low_back(low(project[:, :D] + q_bias))
    key_rows = low_back(low(project[:, D:2 * D]))
    fresh = low_back(low(project[:, 2 * D:] + v_bias))
    value_rows = jnp.concatenate([fresh, low_back(row_skip)], axis=1)
    head_shape = (LENGTH, HEADS, HDIM)
    raw = low_back(jnp.einsum('qhc,khc->hqk', queries.reshape(head_shape), key_rows.reshape(head_shape), precision=HIGHEST))
    position = jnp.arange(LENGTH)
    causal = position[None, :] <= position[:, None]
    diagonal = position[None, :] == position[:, None]
    allowed = (row_segments[:, None] == row_segments[None, :]) & causal & ((row_mask[None, :] == 1) | diagonal)
    scores = jnp.where(allowed[None], raw * float(HDIM) ** (-0.5), MASKED)
    row_max = lax.optimization_barrier(jnp.max(scores, axis=-1, keepdims=True))
    exp_scores = jnp.exp(scores - row_max)
    probs = low(exp_scores / lax.optimization_barrier(jnp.sum(exp_scores, axis=-1, keepdims=True)))
    mixed = jnp.einsum('hqk,khc->qhc', probs, value_rows.reshape(head_shape), precision=HIGHEST).reshape(LENGTH, D)
    mixed = low_back(low(mixed))
    attended = low_back(matmul(mixed, w_out) + out_bias)
    middle = row_tokens + attended
    normed_two = low(layer_norm(middle, mlp_gain, mlp_shift))
    hidden = low_back(matmul(normed_two, w_up) + up_bias)
    active = low(jax.nn.gelu(hidden, approximate=True))
    return middle + matmul(active, w_down) + down_bias

def reference(tokens, skip_values, segments, token_mask, attn_gain, attn_shift, w_qkv, q_bias, v_bias, w_out, out_bias, mlp_gain, mlp_shift, w_up, up_bias, w_down, down_bias, cotangent):
    params = tuple((entry.astype(jnp.float32) for entry in (attn_gain, attn_shift, w_qkv, q_bias, v_bias, w_out, out_bias, mlp_gain, mlp_shift, w_up, up_bias, w_down, down_bias)))

    def forward(all_tokens, all_skip, weights):
        row_func = jax.checkpoint(partial(forward_row, weights))

        def step(carry, inputs):
            return (carry, row_func(inputs[0], inputs[1], inputs[2], inputs[3]))
        start_carry = jnp.zeros((), jnp.float32)
        _, result = lax.scan(step, start_carry, (all_tokens, all_skip, segments, token_mask))
        return result
    output, backward = jax.vjp(forward, tokens.astype(jnp.float32), skip_values.astype(jnp.float32), params)
    grad_tokens, grad_skip, grads = backward(cotangent.astype(jnp.float32))
    return (output.astype(jnp.bfloat16), grad_tokens, grad_skip, grads[0], grads[1], grads[2], grads[3], grads[4], grads[5], grads[6], grads[7], grads[8], grads[9], grads[10], grads[11], grads[12])
```

```python
import functools
import jax, jax.numpy as jnp
from jax import lax
from jax.sharding import PartitionSpec as P
from jax.experimental import pallas as pl
from jax.experimental.pallas import tpu as pltpu
HDIM = 64
BLK = 256
LN2 = 0.6931471805599453
LOG2E = 1.4426950408889634
def nt(a,b): return lax.dot_general(a,b,(((1,),(1,)),((),())),preferred_element_type=jnp.float32)
def nn(a,b): return lax.dot_general(a,b,(((1,),(0,)),((),())),preferred_element_type=jnp.float32)

def fill_bias(code_ref, bias_ref):
    length = code_ref.shape[1]
    code = code_ref[...]
    col = jnp.transpose(jnp.broadcast_to(code, (128, length)))
    for i in range(length // BLK):
        q_doc = col[i*BLK:(i+1)*BLK, :1] >> 1
        for j in range(i + 1):
            k_code = code[:, j*BLK:(j+1)*BLK]
            same = q_doc == (k_code >> 1)
            real = (k_code & 1) == 1
            if i == j:
                rows = lax.broadcasted_iota(jnp.int32, (BLK, BLK), 0)
                cols = lax.broadcasted_iota(jnp.int32, (BLK, BLK), 1)
                ok = same & (cols <= rows) & (real | (cols == rows))
            else:
                ok = same & real
            bias_ref[i*BLK:(i+1)*BLK, j*BLK:(j+1)*BLK] = jnp.where(ok, 0.0, MASKED)

def fwd_kernel(code_ref, q_ref, k_ref, v_ref, o_ref, lse_ref, bias_ref):
    @pl.when(pl.program_id(0) == 0)
    def _(): fill_bias(code_ref, bias_ref)
    length = q_ref.shape[0]
    first = lax.broadcasted_iota(jnp.int32, (length, 2*HDIM), 1) < HDIM
    k_pair, v_pair = k_ref[...], v_ref[...]
    zero = jnp.zeros_like(k_pair); one = jnp.ones_like(v_pair)
    keys = (jnp.where(first, k_pair, zero), jnp.where(first, zero, k_pair))
    vals = (jnp.where(first, v_pair, one), jnp.where(first, one, v_pair))
    half = first[:BLK]
    for i in range(length // BLK):
        end = (i + 1) * BLK
        q = q_ref[i*BLK:end, :]
        outs, lses = [], []
        for h in range(2):
            s = nt(q, keys[h][:end]) + bias_ref[i*BLK:end, :end]
            top = jnp.max(s, axis=1, keepdims=True)
            p = jnp.exp2(s - top).astype(jnp.bfloat16)
            mixed = nn(p, vals[h][:end])
            total = pltpu.roll(mixed, HDIM, 1)
            outs.append(mixed / total)
            lses.append(top + jnp.log2(total))
        o_ref[i*BLK:end, :] = jnp.where(half, outs[0], outs[1]).astype(o_ref.dtype)
        lse_ref[i*BLK:end, :] = jnp.where(half, lses[0], lses[1])

def bwd_kernel(code_ref, q_ref, k_ref, v_ref, o_ref, do_ref, lse_ref, dq_ref, dk_ref, dv_ref, bias_ref, dkt_ref, dvt_ref):
    @pl.when(pl.program_id(0) == 0)
    def _(): fill_bias(code_ref, bias_ref)
    length = q_ref.shape[0]
    first = lax.broadcasted_iota(jnp.int32, (length, 2*HDIM), 1) < HDIM
    k_pair, v_pair = k_ref[...], v_ref[...]
    zero = jnp.zeros_like(k_pair)
    keys = (jnp.where(first, k_pair, zero), jnp.where(first, zero, k_pair))
    vals = (jnp.where(first, v_pair, zero), jnp.where(first, zero, v_pair))
    half = first[:BLK]
    count = length // BLK
    for i in reversed(range(count)):
        end = (i + 1) * BLK
        rows = slice(i*BLK, end)
        q, do = q_ref[rows, :], do_ref[rows, :]
        q_t, do_t = jnp.transpose(q), jnp.transpose(do)
        prod = do.astype(jnp.float32) * o_ref[rows, :].astype(jnp.float32)
        dq = None
        for h in range(2):
            lse = lse_ref[rows, h*HDIM:h*HDIM+1]
            mine = half if h == 0 else ~half
            delta = jnp.sum(jnp.where(mine, prod, 0.0), axis=1, keepdims=True)
            p = jnp.exp2(nt(q, keys[h][:end]) + bias_ref[rows, :end] - lse)
            dp = nt(do, vals[h][:end])
            ds = (p * (dp - delta)).astype(jnp.bfloat16)
            pb = p.astype(jnp.bfloat16)
            part = nn(ds, keys[h][:end])
            dq = part if dq is None else dq + part
            hs = slice(h*HDIM, (h+1)*HDIM)
            dv = nn(do_t[hs], pb)
            dk = nn(q_t[hs], ds)
            if i == count - 1:
                dvt_ref[hs, :] = dv
                dkt_ref[hs, :] = dk
            else:
                dvt_ref[hs, :end] += dv
                dkt_ref[hs, :end] += dk
        dq_ref[rows, :] = (dq * 0.125).astype(dq_ref.dtype)
    dk_ref[...] = jnp.transpose(dkt_ref[...] * LN2).astype(dk_ref.dtype)
    dv_ref[...] = jnp.transpose(dvt_ref[...]).astype(dv_ref.dtype)

def attn_fwd(code, proj, values, q0, k0, v0, pairs, name):
    length = proj.shape[0]
    w = 2*HDIM
    blk = lambda off: pl.BlockSpec((length, w), lambda p: (0, p + off))
    flops = pairs * 2 * 2 * 2 * length * length * 256
    return pl.pallas_call(fwd_kernel, grid=(pairs,), name=name,
        in_specs=[pl.BlockSpec((1, length), lambda p: (0, 0)), blk(q0), blk(k0), blk(v0)],
        out_specs=[blk(0), blk(0)],
        out_shape=[jax.ShapeDtypeStruct((length, pairs*w), jnp.bfloat16), jax.ShapeDtypeStruct((length, pairs*w), jnp.float32)],
        scratch_shapes=[pltpu.VMEM((length, length), jnp.float32)],
        cost_estimate=pl.CostEstimate(flops=flops, bytes_accessed=pairs*length*w*12, transcendentals=0),
        compiler_params=pltpu.CompilerParams(vmem_limit_bytes=48 << 20))(code, proj, proj, values)

def attn_bwd(code, proj, values, o, do, lse, q0, k0, v0, o0, do0, pairs, name):
    length = proj.shape[0]
    w = 2*HDIM
    blk = lambda off: pl.BlockSpec((length, w), lambda p: (0, p + off))
    flops = pairs * 2 * 5 * 2 * length * length * 256
    return pl.pallas_call(bwd_kernel, grid=(pairs,), name=name,
        in_specs=[pl.BlockSpec((1, length), lambda p: (0, 0)), blk(q0), blk(k0), blk(v0), blk(o0), blk(do0), blk(0)],
        out_specs=[blk(0)]*3,
        out_shape=[jax.ShapeDtypeStruct((length, pairs*w), jnp.bfloat16)]*3,
        scratch_shapes=[pltpu.VMEM((length, length), jnp.float32), pltpu.VMEM((w, length), jnp.float32), pltpu.VMEM((w, length), jnp.float32)],
        cost_estimate=pl.CostEstimate(flops=flops, bytes_accessed=pairs*length*w*18, transcendentals=0),
        compiler_params=pltpu.CompilerParams(vmem_limit_bytes=48 << 20))(code, proj, proj, values, o, do, lse)


QBLOCK = 512


EPSILON = 1e-05
MASKED = -1e30


def layer_norm(inputs, norm_gain, norm_shift):
    center = inputs - jnp.mean(inputs, axis=-1, keepdims=True)
    spread = jnp.mean(center * center, axis=-1, keepdims=True)
    return center * lax.rsqrt(spread + EPSILON) * norm_gain + norm_shift


def gelu_tanh(inputs):
    return jax.nn.gelu(inputs, approximate=True)


def split_pairs(array):
    return array.reshape(array.shape[0], array.shape[1], 2, array.shape[2] // 2)


def block_scores(q_block, k_block, seg_items, mask_items, q_start, k_end, factor):
    raw = jnp.einsum("iqhc,ikhc->ihqk", q_block, k_block, preferred_element_type=jnp.float32)
    q_pos = q_start + jnp.arange(q_block.shape[1])
    k_pos = jnp.arange(k_end)
    causal = k_pos[None, :] <= q_pos[:, None]
    diagonal = k_pos[None, :] == q_pos[:, None]
    same_doc = (
        seg_items[:, q_start : q_start + q_block.shape[1], None] == seg_items[:, None, :k_end]
    )
    allowed = same_doc & causal[None] & ((mask_items[:, None, :k_end] == 1) | diagonal[None])
    return jnp.where(allowed[:, None], raw * factor, MASKED)


def spread_body(
    tokens,
    skip_values,
    segments,
    token_mask,
    attn_gain,
    attn_shift,
    w_qkv,
    q_bias,
    v_bias,
    w_out,
    out_bias,
    mlp_gain,
    mlp_shift,
    w_up,
    up_bias,
    w_down,
    down_bias,
    cotangent,
):
    rows_here, seq_here, width = tokens.shape
    pair_width = 2 * HDIM
    pair_count = width // pair_width
    fresh_pairs = pair_count // 2
    factor = float(HDIM) ** (-0.5)
    tokens_f = tokens.astype(jnp.float32)
    normed_f, first_back = jax.vjp(
        layer_norm, tokens_f, attn_gain.astype(jnp.float32), attn_shift.astype(jnp.float32)
    )
    normed = normed_f.astype(jnp.bfloat16)
    w_pairs = w_qkv.reshape(width, 2 * pair_count + fresh_pairs, pair_width)
    project = jnp.einsum("rsd,dpc->rpsc", normed, w_pairs, preferred_element_type=jnp.float32)
    queries = (
        project[:, :pair_count] + q_bias.astype(jnp.float32).reshape(1, pair_count, 1, pair_width)
    ).astype(jnp.bfloat16)
    key_rows = project[:, pair_count : 2 * pair_count].astype(jnp.bfloat16)
    fresh = (
        project[:, 2 * pair_count :]
        + v_bias.astype(jnp.float32).reshape(1, fresh_pairs, 1, pair_width)
    ).astype(jnp.bfloat16)
    reused = skip_values.reshape(rows_here, seq_here, fresh_pairs, pair_width).transpose(0, 2, 1, 3)
    value_rows = jnp.concatenate([fresh, reused], axis=1)
    flat_shape = (rows_here * pair_count, seq_here, pair_width)
    q_items, k_items, v_items = (
        lax.all_to_all(
            queries.reshape(flat_shape), "head", split_axis=0, concat_axis=1, tiled=True
        ),
        lax.all_to_all(
            key_rows.reshape(flat_shape), "head", split_axis=0, concat_axis=1, tiled=True
        ),
        lax.all_to_all(
            value_rows.reshape(flat_shape), "head", split_axis=0, concat_axis=1, tiled=True
        ),
    )
    seg_rows, mask_rows = (
        lax.all_gather(segments, "head", axis=1, tiled=True),
        lax.all_gather(token_mask, "head", axis=1, tiled=True),
    )
    item_count = q_items.shape[0]
    length = q_items.shape[1]
    item_row = (lax.axis_index("head") * item_count + jnp.arange(item_count)) // pair_count
    picker = (item_row[:, None] == jnp.arange(rows_here)[None, :]).astype(jnp.int32)
    seg_items = jnp.sum(picker[:, :, None] * seg_rows[None], axis=1)
    mask_items = jnp.sum(picker[:, :, None] * mask_rows[None], axis=1)
    q_split = split_pairs(q_items)
    k_split = split_pairs(k_items)
    v_split = split_pairs(v_items)
    block_count = length // QBLOCK
    mixed_blocks = []
    log_sums = []
    for block_id in range(block_count):
        q_start = block_id * QBLOCK
        k_end = q_start + QBLOCK
        scores = block_scores(
            q_split[:, q_start:k_end],
            k_split[:, :k_end],
            seg_items,
            mask_items,
            q_start,
            k_end,
            factor,
        )
        row_max = jnp.max(scores, axis=-1, keepdims=True)
        exp_scores = jnp.exp(scores - row_max)
        row_sum = jnp.sum(exp_scores, axis=-1, keepdims=True)
        soft_probs = (exp_scores / row_sum).astype(jnp.bfloat16)
        mixed = jnp.einsum(
            "ihqk,ikhc->iqhc", soft_probs, v_split[:, :k_end], preferred_element_type=jnp.float32
        )
        mixed_blocks.append(mixed.astype(jnp.bfloat16).reshape(item_count, QBLOCK, pair_width))
        log_sums.append(row_max + jnp.log(row_sum))
    mixed_items = jnp.concatenate(mixed_blocks, axis=1)
    mixed_rows = lax.all_to_all(
        mixed_items, "head", split_axis=1, concat_axis=0, tiled=True
    ).reshape(rows_here, pair_count, seq_here, pair_width)
    w_out_pairs = w_out.reshape(pair_count, pair_width, width)
    attended = jnp.einsum(
        "rpsc,pcd->rsd", mixed_rows, w_out_pairs, preferred_element_type=jnp.float32
    ) + out_bias.astype(jnp.float32)
    middle = tokens_f + attended
    normed_mid, second_back = jax.vjp(
        layer_norm, middle, mlp_gain.astype(jnp.float32), mlp_shift.astype(jnp.float32)
    )
    normed_two = normed_mid.astype(jnp.bfloat16)
    hidden = jnp.einsum(
        "rsd,df->rsf", normed_two, w_up, preferred_element_type=jnp.float32
    ) + up_bias.astype(jnp.float32)
    active_f, gelu_back = jax.vjp(gelu_tanh, hidden)
    active = active_f.astype(jnp.bfloat16)
    result = (
        middle
        + jnp.einsum("rsf,fd->rsd", active, w_down, preferred_element_type=jnp.float32)
        + down_bias.astype(jnp.float32)
    )
    layer_out = result.astype(jnp.bfloat16)
    g_down = jnp.einsum("rsf,rsd->fd", active, cotangent, preferred_element_type=jnp.float32)
    g_down_bias = jnp.sum(cotangent, axis=(0, 1), dtype=jnp.float32)
    d_active = jnp.einsum("rsd,fd->rsf", cotangent, w_down, preferred_element_type=jnp.float32)
    d_hidden = gelu_back(d_active)[0].astype(jnp.bfloat16)
    g_up_bias = jnp.sum(d_hidden, axis=(0, 1), dtype=jnp.float32)
    g_up = jnp.einsum("rsd,rsf->df", normed_two, d_hidden, preferred_element_type=jnp.float32)
    d_normed_two = jnp.einsum("rsf,df->rsd", d_hidden, w_up, preferred_element_type=jnp.float32)
    d_mid_norm, g_mlp_gain, g_mlp_shift = second_back(d_normed_two)
    d_middle = cotangent.astype(jnp.float32) + d_mid_norm
    d_att = d_middle.astype(jnp.bfloat16)
    g_out_bias = jnp.sum(d_att, axis=(0, 1), dtype=jnp.float32)
    g_out = jnp.einsum(
        "rpsc,rsd->pcd", mixed_rows, d_att, preferred_element_type=jnp.float32
    ).reshape(width, width)
    d_mixed = (
        jnp.einsum("rsd,pcd->rpsc", d_att, w_out_pairs, preferred_element_type=jnp.float32)
        .astype(jnp.bfloat16)
        .reshape(flat_shape)
    )
    d_items = lax.all_to_all(d_mixed, "head", split_axis=0, concat_axis=1, tiled=True)
    d_split = split_pairs(d_items)
    dk_total = jnp.zeros((item_count, length, 2, HDIM), jnp.float32)
    dv_total = jnp.zeros((item_count, length, 2, HDIM), jnp.float32)
    dq_blocks = []
    for block_id in range(block_count):
        q_start = block_id * QBLOCK
        k_end = q_start + QBLOCK
        scores = block_scores(
            q_split[:, q_start:k_end],
            k_split[:, :k_end],
            seg_items,
            mask_items,
            q_start,
            k_end,
            factor,
        )
        soft = jnp.exp(scores - log_sums[block_id])
        d_block = d_split[:, q_start:k_end]
        d_probs = jnp.einsum(
            "iqhc,ikhc->ihqk", d_block, v_split[:, :k_end], preferred_element_type=jnp.float32
        )
        delta = jnp.sum(d_probs * soft, axis=-1, keepdims=True)
        d_raw = (soft * (d_probs - delta) * factor).astype(jnp.bfloat16)
        dq_blocks.append(
            jnp.einsum(
                "ihqk,ikhc->iqhc", d_raw, k_split[:, :k_end], preferred_element_type=jnp.float32
            )
        )
        dk_total = dk_total.at[:, :k_end].add(
            jnp.einsum(
                "ihqk,iqhc->ikhc",
                d_raw,
                q_split[:, q_start:k_end],
                preferred_element_type=jnp.float32,
            )
        )
        dv_total = dv_total.at[:, :k_end].add(
            jnp.einsum(
                "ihqk,iqhc->ikhc",
                soft.astype(jnp.bfloat16),
                d_block,
                preferred_element_type=jnp.float32,
            )
        )
    item_shape = (item_count, length, pair_width)
    dq_items = jnp.concatenate(dq_blocks, axis=1).astype(jnp.bfloat16).reshape(item_shape)
    dk_items = dk_total.astype(jnp.bfloat16).reshape(item_shape)
    dv_items = dv_total.astype(jnp.bfloat16).reshape(item_shape)
    dq_rows, dk_rows, dv_rows = (
        lax.all_to_all(dq_items, "head", split_axis=1, concat_axis=0, tiled=True),
        lax.all_to_all(dk_items, "head", split_axis=1, concat_axis=0, tiled=True),
        lax.all_to_all(dv_items, "head", split_axis=1, concat_axis=0, tiled=True),
    )
    row_shape = (rows_here, pair_count, seq_here, pair_width)
    dq_rows = dq_rows.reshape(row_shape)
    dk_rows = dk_rows.reshape(row_shape)
    dv_rows = dv_rows.reshape(row_shape)
    grad_skip = (
        dv_rows[:, fresh_pairs:]
        .transpose(0, 2, 1, 3)
        .reshape(rows_here, seq_here, fresh_pairs * pair_width)
        .astype(jnp.float32)
    )
    d_project = jnp.concatenate([dq_rows, dk_rows, dv_rows[:, :fresh_pairs]], axis=1)
    g_qkv = jnp.einsum(
        "rsd,rpsc->dpc", normed, d_project, preferred_element_type=jnp.float32
    ).reshape(width, -1)
    g_q_bias = jnp.sum(dq_rows, axis=(0, 2), dtype=jnp.float32).reshape(-1)
    g_v_bias = jnp.sum(dv_rows[:, :fresh_pairs], axis=(0, 2), dtype=jnp.float32).reshape(-1)
    d_normed = jnp.einsum("rpsc,dpc->rsd", d_project, w_pairs, preferred_element_type=jnp.float32)
    d_tok_norm, g_attn_gain, g_attn_shift = first_back(d_normed)
    grad_tokens = d_middle + d_tok_norm
    small_sums = lax.psum(
        (
            g_attn_gain,
            g_attn_shift,
            g_q_bias,
            g_v_bias,
            g_out_bias,
            g_mlp_gain,
            g_mlp_shift,
            g_up_bias,
            g_down_bias,
        ),
        ("seq", "head"),
    )
    shards = (
        lax.psum_scatter(g_qkv.astype(jnp.bfloat16), "seq", scatter_dimension=0, tiled=True).astype(
            jnp.float32
        ),
        lax.psum_scatter(g_out.astype(jnp.bfloat16), "seq", scatter_dimension=0, tiled=True).astype(
            jnp.float32
        ),
        lax.psum_scatter(g_up.astype(jnp.bfloat16), "seq", scatter_dimension=0, tiled=True).astype(
            jnp.float32
        ),
        lax.psum_scatter(
            g_down.astype(jnp.bfloat16), "seq", scatter_dimension=0, tiled=True
        ).astype(jnp.float32),
    )
    reduced = (
        lax.psum(shards[0].astype(jnp.bfloat16), "head").astype(jnp.float32),
        lax.psum(shards[1].astype(jnp.bfloat16), "head").astype(jnp.float32),
        lax.psum(shards[2].astype(jnp.bfloat16), "head").astype(jnp.float32),
        lax.psum(shards[3].astype(jnp.bfloat16), "head").astype(jnp.float32),
    )
    return (
        layer_out,
        grad_tokens,
        grad_skip,
        small_sums[0],
        small_sums[1],
        reduced[0],
        small_sums[2],
        small_sums[3],
        reduced[1],
        small_sums[4],
        small_sums[5],
        small_sums[6],
        reduced[2],
        small_sums[7],
        reduced[3],
        small_sums[8],
    )


Q_SCALE = LOG2E * HDIM ** -0.5


def fits(sizes):
    return sizes == (8, 4)


def pick(array, index):
    return lax.dynamic_index_in_dim(array, index, 0, keepdims=False)


def swap(array, axis, count, bit):
    return lax.ppermute(array, axis, [(i, i ^ bit) for i in range(count)])


def trade(blocks, me, count):
    return [
        pick(blocks, me) if d == 0 else swap(pick(blocks, me ^ d), "head", count, d)
        for d in range(count)
    ]


def settle(parts, me):
    whole = jnp.zeros((len(parts),) + parts[0].shape, parts[0].dtype)
    for d, part in enumerate(parts):
        whole = lax.dynamic_update_index_in_dim(whole, part, me ^ d, 0)
    return whole


def row_body(
    sizes,
    tokens,
    skip_values,
    segments,
    token_mask,
    attn_gain,
    attn_shift,
    w_qkv,
    q_bias,
    v_bias,
    w_out,
    out_bias,
    mlp_gain,
    mlp_shift,
    w_up,
    up_bias,
    w_down,
    down_bias,
    cotangent,
):
    n_head = sizes[1]
    f32 = jnp.float32
    me = lax.axis_index("head")
    rows, part, width = tokens.shape
    length = rows * part
    fresh = width // 2
    code = (segments * 2 + token_mask).reshape(rows, 1, part)
    code_row = settle(trade(code, me, n_head), me).reshape(1, length)
    x_row = settle(trade(tokens, me, n_head), me).reshape(length, width)
    skip_values, x_row = lax.optimization_barrier((skip_values, x_row))
    skip_row = settle(trade(skip_values, me, n_head), me).reshape(length, fresh)
    cotangent, skip_gate = lax.optimization_barrier((cotangent, skip_row))
    skip_row = skip_gate
    dy = settle(trade(cotangent, me, n_head), me).reshape(length, width)

    x_f = x_row.astype(f32)
    normed_f, first_back = jax.vjp(layer_norm, x_f, attn_gain.astype(f32), attn_shift.astype(f32))
    normed = normed_f.astype(jnp.bfloat16)
    qkv_bias = jnp.concatenate([q_bias, jnp.zeros_like(q_bias), v_bias]).astype(f32)
    scale = jnp.where(jnp.arange(w_qkv.shape[1]) < width, Q_SCALE, 1.0).astype(f32)
    proj = ((nn(normed, w_qkv) + qkv_bias) * scale).astype(jnp.bfloat16)
    o_a, lse_a = attn_fwd(code_row, proj, proj, 0, 6, 12, 3, "attn_fwd_a")
    o_b, lse_b = attn_fwd(code_row, proj, skip_row, 3, 9, 0, 3, "attn_fwd_b")
    mixed = jnp.concatenate([o_a, o_b], axis=1)
    middle = x_f + nn(mixed, w_out) + out_bias.astype(f32)
    normed_mid, second_back = jax.vjp(layer_norm, middle, mlp_gain.astype(f32), mlp_shift.astype(f32))
    normed_two = normed_mid.astype(jnp.bfloat16)
    hidden = nn(normed_two, w_up) + up_bias.astype(f32)
    active_f, gelu_back = jax.vjp(gelu_tanh, hidden)
    active = active_f.astype(jnp.bfloat16)
    result = (middle + nn(active, w_down) + down_bias.astype(f32)).astype(jnp.bfloat16)
    layer_out = settle(trade(result.reshape(rows, part, width), me, n_head), me)
    g_down = jnp.einsum("sf,sd->fd", active, dy, preferred_element_type=f32)
    g_down_bias = jnp.sum(dy, axis=0, dtype=f32)
    d_hidden = gelu_back(nt(dy, w_down))[0].astype(jnp.bfloat16)
    g_up_bias = jnp.sum(d_hidden, axis=0, dtype=f32)
    g_up = jnp.einsum("sd,sf->df", normed_two, d_hidden, preferred_element_type=f32)
    d_mid_norm, g_mlp_gain, g_mlp_shift = second_back(nt(d_hidden, w_up))
    d_middle = dy.astype(f32) + d_mid_norm
    d_att = d_middle.astype(jnp.bfloat16)
    g_out_bias = jnp.sum(d_att, axis=0, dtype=f32)
    g_out = jnp.einsum("sc,sd->cd", mixed, d_att, preferred_element_type=f32)
    d_mixed = nt(d_att, w_out).astype(jnp.bfloat16)
    dq_b, dk_b, dv_b = attn_bwd(
        code_row, proj, skip_row, o_b, d_mixed, lse_b, 3, 9, 0, 0, 3, 3, "attn_bwd_b"
    )
    grad_skip = settle(trade(dv_b.reshape(rows, part, fresh), me, n_head), me).astype(f32)
    dq_a, dk_a, dv_a = attn_bwd(
        code_row, proj, proj, o_a, d_mixed, lse_a, 0, 6, 12, 0, 0, 3, "attn_bwd_a"
    )
    d_proj = jnp.concatenate([dq_a, dq_b, dk_a, dk_b, dv_a], axis=1)
    d_normed = nt(d_proj, w_qkv)
    d_tok_norm, g_attn_gain, g_attn_shift = first_back(d_normed)
    grad_row = (d_middle + d_tok_norm).astype(jnp.bfloat16)
    grad_tokens = settle(trade(grad_row.reshape(rows, part, width), me, n_head), me).astype(f32)
    g_qkv = jnp.einsum("sd,sc->dc", normed, d_proj, preferred_element_type=f32)
    g_proj_bias = jnp.sum(d_proj, axis=0, dtype=f32)
    small = (
        g_attn_gain,
        g_attn_shift,
        g_proj_bias[:width],
        g_proj_bias[2 * width :],
        g_out_bias,
        g_mlp_gain,
        g_mlp_shift,
        g_up_bias,
        g_down_bias,
    )
    packed = lax.psum(jnp.concatenate(small), ("seq", "head"))
    sums = []
    for entry in small:
        sums.append(packed[: entry.shape[0]])
        packed = packed[entry.shape[0] :]

    def reduce(grad):
        shard = lax.psum_scatter(
            grad.astype(jnp.bfloat16), "seq", scatter_dimension=0, tiled=True
        )
        return lax.psum(shard, "head").astype(f32)

    r_down, r_up, r_out, r_qkv = reduce(g_down), reduce(g_up), reduce(g_out), reduce(g_qkv)
    return (
        layer_out,
        grad_tokens,
        grad_skip,
        sums[0],
        sums[1],
        r_qkv,
        sums[2],
        sums[3],
        r_out,
        sums[4],
        sums[5],
        sums[6],
        r_up,
        sums[7],
        r_down,
        sums[8],
    )


def solution(mesh):
    sizes = (mesh.shape["seq"], mesh.shape["head"])
    return jax.shard_map(
        functools.partial(row_body, sizes) if fits(sizes) else spread_body,
        mesh=mesh,
        in_specs=(
            P("seq", "head", None),
            P("seq", "head", None),
            P("seq", "head"),
            P("seq", "head"),
            P(),
            P(),
            P(),
            P(),
            P(),
            P(),
            P(),
            P(),
            P(),
            P(),
            P(),
            P(),
            P(),
            P("seq", "head", None),
        ),
        out_specs=(
            P("seq", "head", None),
            P("seq", "head", None),
            P("seq", "head", None),
            P(),
            P(),
            P("seq", None),
            P(),
            P(),
            P("seq", None),
            P(),
            P(),
            P(),
            P("seq", None),
            P(),
            P("seq", None),
            P(),
        ),
        check_vma=False,
    )
```

```python
import functools

import jax
import jax.numpy as jnp
from jax import lax
from jax.experimental import pallas as pl
from jax.experimental.pallas import tpu as pltpu
from jax.sharding import PartitionSpec as P

HDIM = 64
PAIR = 2 * HDIM
BLK = 256
LN2 = 0.6931471805599453
LOG2E = 1.4426950408889634
Q_SCALE = LOG2E * HDIM**-0.5
BF16 = jnp.bfloat16
F32 = jnp.float32
VMEM_BYTES = 56 << 20


def dot(left, right, left_dim, right_dim):
    return lax.dot_general(
        left, right, (((left_dim,), (right_dim,)), ((), ())), preferred_element_type=F32
    )


def nn(left, right):
    return dot(left, right, 1, 0)


def nt(left, right):
    return dot(left, right, 1, 1)


def tn(left, right):
    return dot(left, right, 0, 0)


def call(kernel, name, grid, in_specs, out_specs, out_shape, scratch=(), flops=0, moved=0, aliases=None):
    return pl.pallas_call(
        kernel,
        name=name,
        grid_spec=pltpu.PrefetchScalarGridSpec(
            num_scalar_prefetch=1,
            grid=grid,
            in_specs=in_specs,
            out_specs=out_specs,
            scratch_shapes=list(scratch),
        ),
        out_shape=out_shape,
        input_output_aliases=aliases or {},
        cost_estimate=pl.CostEstimate(flops=flops, bytes_accessed=moved, transcendentals=0),
        compiler_params=pltpu.CompilerParams(vmem_limit_bytes=VMEM_BYTES),
    )


def shape(dims, dtype=BF16):
    return jax.ShapeDtypeStruct(dims, dtype)


def whole(dims):
    return pl.BlockSpec(dims, lambda *_: (0,) * len(dims))


def standardize(values):
    center = values - jnp.mean(values, axis=1, keepdims=True)
    rate = lax.rsqrt(jnp.mean(center * center, axis=1, keepdims=True) + EPSILON)
    return center * rate, rate


def standardize_back(grad, unit, rate):
    mean_grad = jnp.mean(grad, axis=1, keepdims=True)
    mean_dot = jnp.mean(grad * unit, axis=1, keepdims=True)
    return rate * (grad - mean_grad - unit * mean_dot)


def column_sums(values):
    return jnp.sum(values, axis=0, keepdims=True)


def block_rows(place, d, size):
    return pl.ds(pl.multiple_of((place ^ d) * size, size), size)


def project_kernel(at_ref, x_ref, gain_ref, shift_ref, w_ref, bias_ref, scale_ref, *refs):
    row_ref, normed_ref, proj_ref = refs[-3:]
    unit, _ = standardize(x_ref[...].astype(F32))
    normed = (unit * gain_ref[...] + shift_ref[...]).astype(BF16)
    row_ref[...] = x_ref[...]
    normed_ref[...] = normed
    proj_ref[...] = ((nn(normed, w_ref[...]) + bias_ref[...]) * scale_ref[...]).astype(BF16)


def project(at, piece, gain, shift, w, bias, scale, length, so_far):
    part, width = piece.shape
    cols = w.shape[1]
    block = lambda n: pl.BlockSpec((part, n), lambda i, at: (at[0], 0))
    held = [pl.BlockSpec(memory_space=pl.ANY)] * len(so_far)
    return call(
        project_kernel,
        "project",
        (1,),
        [whole((part, width)), whole((1, width)), whole((1, width)), whole((width, cols)), whole((1, cols)), whole((1, cols))]
        + held,
        [block(width), block(width), block(cols)],
        [shape((length, width)), shape((length, width)), shape((length, cols))],
        flops=2 * part * width * cols,
        moved=2 * (part * (3 * width + cols) + width * cols),
        aliases={7 + n: n for n in range(len(so_far))},
    )(at, piece, gain, shift, w, bias, scale, *so_far)


def fill_bias(code_ref, bias_ref):
    length = code_ref.shape[1]
    code = code_ref[...]
    column = jnp.transpose(jnp.broadcast_to(code, (128, length)))
    for i in range(length // BLK):
        q_doc = column[i * BLK : (i + 1) * BLK, :1] >> 1
        for j in range(i + 1):
            k_code = code[:, j * BLK : (j + 1) * BLK]
            same = q_doc == (k_code >> 1)
            real = (k_code & 1) == 1
            if i == j:
                row_at = lax.broadcasted_iota(jnp.int32, (BLK, BLK), 0)
                col_at = lax.broadcasted_iota(jnp.int32, (BLK, BLK), 1)
                allowed = same & (col_at <= row_at) & (real | (col_at == row_at))
            else:
                allowed = same & real
            bias_ref[i * BLK : (i + 1) * BLK, j * BLK : (j + 1) * BLK] = jnp.where(allowed, 0.0, MASKED)


def halves(pair, other):
    first = lax.broadcasted_iota(jnp.int32, pair.shape, 1) < HDIM
    return jnp.where(first, pair, other), jnp.where(first, other, pair)


def gather_values(me_ref, v_refs, value_ref):
    if len(v_refs) == 1:
        return v_refs[0][...]
    for d, ref in enumerate(v_refs):
        value_ref[block_rows(me_ref[0], d, ref.shape[0]), :] = ref[...]
    return value_ref[...]


def forward_kernel(count, me_ref, code_ref, q_ref, k_ref, *refs):
    v_refs, (o_ref, lse_ref, bias_ref, value_ref) = refs[:count], refs[count:]

    @pl.when(pl.program_id(0) == 0)
    def _():
        fill_bias(code_ref, bias_ref)

    length = q_ref.shape[0]
    v_pair = gather_values(me_ref, v_refs, value_ref)
    k_pair = k_ref[...]
    keys = halves(k_pair, jnp.zeros_like(k_pair))
    vals = halves(v_pair, jnp.ones_like(v_pair))
    first = lax.broadcasted_iota(jnp.int32, (BLK, PAIR), 1) < HDIM
    for i in range(length // BLK):
        end = (i + 1) * BLK
        rows = slice(i * BLK, end)
        q = q_ref[rows, :]
        outs, lses = [], []
        for h in range(2):
            scores = nt(q, keys[h][:end]) + bias_ref[rows, :end]
            top = jnp.max(scores, axis=1, keepdims=True)
            weights = jnp.exp2(scores - top).astype(BF16)
            mixed = nn(weights, vals[h][:end])
            total = pltpu.roll(mixed, HDIM, 1)
            outs.append(mixed / total)
            lses.append(top + jnp.log2(total))
        o_ref[rows, :] = jnp.where(first, outs[0], outs[1]).astype(BF16)
        lse_ref[rows, :] = jnp.where(first, lses[0], lses[1])


def backward_kernel(count, me_ref, code_ref, q_ref, k_ref, *refs):
    v_refs = refs[:count]
    o_ref, do_ref, lse_ref = refs[count : count + 3]
    outs = refs[count + 3 :]
    d_ref = outs[0]
    piece_refs = outs[1 : len(outs) - 4]
    bias_ref, value_ref, dkt_ref, dvt_ref = outs[-4:]

    @pl.when(pl.program_id(0) == 0)
    def _():
        fill_bias(code_ref, bias_ref)

    length = q_ref.shape[0]
    v_pair = gather_values(me_ref, v_refs, value_ref)
    k_pair = k_ref[...]
    zero = jnp.zeros_like(k_pair)
    keys = halves(k_pair, zero)
    vals = halves(v_pair, zero)
    first = lax.broadcasted_iota(jnp.int32, (BLK, PAIR), 1) < HDIM
    blocks = length // BLK
    for i in reversed(range(blocks)):
        end = (i + 1) * BLK
        rows = slice(i * BLK, end)
        q, do = q_ref[rows, :], do_ref[rows, :]
        q_t, do_t = jnp.transpose(q), jnp.transpose(do)
        prod = do.astype(F32) * o_ref[rows, :].astype(F32)
        dq = None
        for h in range(2):
            head = slice(h * HDIM, (h + 1) * HDIM)
            lse = lse_ref[rows, h * HDIM : h * HDIM + 1]
            mine = first if h == 0 else ~first
            delta = jnp.sum(jnp.where(mine, prod, 0.0), axis=1, keepdims=True)
            probs = jnp.exp2(nt(q, keys[h][:end]) + bias_ref[rows, :end] - lse)
            d_scores = (probs * (nt(do, vals[h][:end]) - delta)).astype(BF16)
            part = nn(d_scores, keys[h][:end])
            dq = part if dq is None else dq + part
            dv = nn(do_t[head], probs.astype(BF16))
            dk = nn(q_t[head], d_scores)
            if i == blocks - 1:
                dvt_ref[head, :] = dv
                dkt_ref[head, :] = dk
            else:
                dvt_ref[head, :end] += dv
                dkt_ref[head, :end] += dk
        d_ref[0, rows, :] = (dq * HDIM**-0.5).astype(BF16)
    d_ref[1] = jnp.transpose(dkt_ref[...] * LN2).astype(BF16)
    dv = jnp.transpose(dvt_ref[...]).astype(BF16)
    if piece_refs:
        value_ref[...] = dv
        for d, ref in enumerate(piece_refs):
            ref[...] = value_ref[block_rows(me_ref[0], d, ref.shape[0]), :]
    else:
        d_ref[2] = dv


def pair_specs(length, offset):
    return pl.BlockSpec((length, PAIR), lambda p, me: (0, p + offset))


def value_specs(values, length, offset):
    if len(values) == 1:
        return [pair_specs(length, offset)]
    return [pl.BlockSpec((v.shape[0], PAIR), lambda p, me: (0, p)) for v in values]


def attend(me, code, proj, values, q_at, k_at, v_at, pairs, name):
    length = proj.shape[0]
    return call(
        functools.partial(forward_kernel, len(values)),
        name,
        (pairs,),
        [whole((1, length)), pair_specs(length, q_at), pair_specs(length, k_at)]
        + value_specs(values, length, v_at),
        [pair_specs(length, 0)] * 2,
        [shape((length, pairs * PAIR)), shape((length, pairs * PAIR), F32)],
        [pltpu.VMEM((length, length), F32), pltpu.VMEM((length, PAIR), BF16)],
        flops=pairs * 24 * length * length * PAIR,
        moved=pairs * length * PAIR * 12,
    )(me, code, proj, proj, *values)


def attend_back(me, code, proj, values, o, do, lse, q_at, k_at, v_at, do_at, pairs, name):
    length = proj.shape[0]
    split = len(values) > 1
    part = length // 4
    outs = [pl.BlockSpec((2 if split else 3, length, PAIR), lambda p, me: (0, 0, p))]
    shapes = [shape((2 if split else 3, length, pairs * PAIR))]
    if split:
        outs += [pl.BlockSpec((v.shape[0], PAIR), lambda p, me: (0, p)) for v in values]
        shapes += [shape((v.shape[0], pairs * PAIR)) for v in values]
    return call(
        functools.partial(backward_kernel, len(values)),
        name,
        (pairs,),
        [whole((1, length)), pair_specs(length, q_at), pair_specs(length, k_at)]
        + value_specs(values, length, v_at)
        + [pair_specs(length, 0), pair_specs(length, do_at), pair_specs(length, 0)],
        outs,
        shapes,
        [
            pltpu.VMEM((length, length), F32),
            pltpu.VMEM((length, PAIR), BF16),
            pltpu.VMEM((PAIR, length), F32),
            pltpu.VMEM((PAIR, length), F32),
        ],
        flops=pairs * 30 * length * length * PAIR,
        moved=pairs * length * PAIR * 18,
    )(me, code, proj, proj, *values, o, do, lse)


def mlp_kernel(
    me_ref, x_ref, oa_ref, ob_ref, wo_ref, ob_bias_ref, gain_ref, shift_ref, wu_ref, ub_ref, wd_ref, db_ref,
    middle_ref, normed_ref, act_ref, slope_ref, y0_ref, y1_ref, y2_ref, y3_ref, acc_ref,
):
    @pl.when(pl.program_id(0) == 0)
    def _():
        half = oa_ref.shape[1]
        middle = (
            x_ref[...].astype(F32)
            + nn(oa_ref[...], wo_ref[:half, :])
            + nn(ob_ref[...], wo_ref[half:, :])
            + ob_bias_ref[...]
        )
        middle_ref[...] = middle
        unit, _ = standardize(middle)
        normed_ref[...] = (unit * gain_ref[...] + shift_ref[...]).astype(BF16)
        acc_ref[...] = middle + db_ref[...]

    pre = nn(normed_ref[...], wu_ref[...]) + ub_ref[...]
    square = pre * pre
    curve = jnp.tanh(pre * (GELU_A + (GELU_A * GELU_B) * square))
    half_up = 0.5 + 0.5 * curve
    act = (pre * half_up).astype(BF16)
    act_ref[...] = act
    slope = half_up + 0.5 * pre * (1.0 - curve * curve) * (GELU_A + (3.0 * GELU_A * GELU_B) * square)
    slope_ref[...] = slope.astype(BF16)
    acc_ref[...] += nn(act, wd_ref[...])

    @pl.when(pl.program_id(0) == pl.num_programs(0) - 1)
    def _():
        for d, ref in enumerate((y0_ref, y1_ref, y2_ref, y3_ref)):
            ref[...] = acc_ref[block_rows(me_ref[0], d, ref.shape[0]), :].astype(BF16)


GELU_A = 0.7978845608028654
GELU_B = 0.044715


def mlp(me, x, o_a, o_b, w_out, out_bias, gain, shift, w_up, up_bias, w_down, down_bias, chunk):
    length, width = x.shape
    ff = w_up.shape[1]
    part = length // 4
    vec = whole((1, width))
    cols = pl.BlockSpec((length, chunk), lambda c, me: (0, c))
    return call(
        mlp_kernel,
        "mlp",
        (ff // chunk,),
        [
            whole((length, width)), whole(o_a.shape), whole(o_b.shape), whole((width, width)), vec, vec, vec,
            pl.BlockSpec((width, chunk), lambda c, me: (0, c)),
            pl.BlockSpec((1, chunk), lambda c, me: (0, c)),
            pl.BlockSpec((chunk, width), lambda c, me: (c, 0)),
            vec,
        ],
        [whole((length, width))] * 2 + [cols, cols] + [whole((part, width))] * 4,
        [shape((length, width), F32), shape((length, width)), shape((length, ff)), shape((length, ff))]
        + [shape((part, width))] * 4,
        [pltpu.VMEM((length, width), F32)],
        flops=2 * length * width * (width + 2 * ff),
        moved=length * (width * 12 + ff * 4) + 4 * width * ff,
    )(me, x, o_a, o_b, w_out, out_bias, gain, shift, w_up, up_bias, w_down, down_bias)


def step_chunk(step, core):
    return 2 * (step % 4) + jnp.where(step < 4, 1 - core, core)


def down_kernel(at_ref, d0_ref, d1_ref, d2_ref, d3_ref, act_ref, dy_ref, bias_ref, send_ref, keep_ref):
    @pl.when(pl.program_id(0) == 0)
    def _():
        for d, ref in enumerate((d0_ref, d1_ref, d2_ref, d3_ref)):
            dy_ref[block_rows(at_ref[0], d, ref.shape[0]), :] = ref[...]
        bias_ref[...] = column_sums(dy_ref[...].astype(F32))

    grad = tn(act_ref[...], dy_ref[...]).astype(BF16)

    @pl.when(pl.program_id(0) < 4)
    def _():
        send_ref[0] = grad

    @pl.when(pl.program_id(0) >= 4)
    def _():
        keep_ref[0] = grad


def down_grad(at, pieces, act):
    part, width = pieces[0].shape
    length, ff = act.shape
    chunk = ff // 8
    return call(
        down_kernel,
        "down_grad",
        (8,),
        [whole((part, width))] * 4
        + [pl.BlockSpec((length, chunk), lambda s, at: (0, step_chunk(s, at[1])))],
        [
            whole((length, width)),
            whole((1, width)),
            pl.BlockSpec((1, chunk, width), lambda s, at: (jnp.minimum(s, 3), 0, 0)),
            pl.BlockSpec((1, chunk, width), lambda s, at: (jnp.maximum(s - 4, 0), 0, 0)),
        ],
        [shape((length, width)), shape((1, width), F32), shape((4, chunk, width)), shape((4, chunk, width))],
        flops=2 * length * width * ff,
        moved=2 * (length * ff + 2 * length * width + width * ff),
    )(at, *pieces, act)


def split_store(grad, core, stage_ref, send_ref, keep_ref, lead):
    stage_ref[...] = grad.astype(BF16).reshape(stage_ref.shape)
    for j in range(4):
        send_ref[(j,) + lead] = stage_ref[j, 1 - core]
        keep_ref[(j,) + lead] = stage_ref[j, core]


def mlp_back_kernel(
    at_ref, dy_ref, normed_ref, act_slope_ref, wd_ref, wu_ref, middle_ref, gain_ref, oa_ref, ob_ref, wo_ref,
    up_bias_ref, send_ref, keep_ref, d_att_ref, d_o_ref, sums_ref, out_send_ref, out_keep_ref, acc_ref, stage_ref, out_stage_ref,
):
    step = pl.program_id(0)
    core = at_ref[1]
    d_pre = (nt(dy_ref[...], wd_ref[...]) * act_slope_ref[...].astype(F32)).astype(BF16)
    up_bias_ref[...] = column_sums(d_pre.astype(F32))
    split_store(tn(normed_ref[...], d_pre), core, stage_ref, send_ref, keep_ref, (0,))
    d_normed = nt(d_pre, wu_ref[...])

    @pl.when(step == 0)
    def _():
        acc_ref[...] = d_normed

    @pl.when(step > 0)
    def _():
        acc_ref[...] += d_normed

    @pl.when(step == pl.num_programs(0) - 1)
    def _():
        total = acc_ref[...]
        unit, rate = standardize(middle_ref[...])
        sums_ref[0:1, :] = column_sums(total * unit)
        sums_ref[1:2, :] = column_sums(total)
        d_middle = dy_ref[...].astype(F32) + standardize_back(total * gain_ref[...], unit, rate)
        d_att = d_middle.astype(BF16)
        d_att_ref[...] = d_att
        sums_ref[2:3, :] = column_sums(d_att.astype(F32))
        d_o_ref[...] = nt(d_att, wo_ref[...]).astype(BF16)
        grad = jnp.concatenate([tn(oa_ref[...], d_att), tn(ob_ref[...], d_att)], axis=0)
        split_store(grad, core, out_stage_ref, out_send_ref, out_keep_ref, ())


def mlp_back(at, dy, normed, slope, w_down, w_up, middle, gain, o_a, o_b, w_out):
    length, width = dy.shape
    ff = slope.shape[1]
    chunk = ff // 8
    rows = width // 8
    full = whole((length, width))
    shards = pl.BlockSpec((4, 1, rows, chunk), lambda c, at: (0, c, 0, 0))
    return call(
        mlp_back_kernel,
        "mlp_back",
        (8,),
        [
            full, full,
            pl.BlockSpec((length, chunk), lambda c, at: (0, c)),
            pl.BlockSpec((chunk, width), lambda c, at: (c, 0)),
            pl.BlockSpec((width, chunk), lambda c, at: (0, c)),
            full, whole((1, width)), whole(o_a.shape), whole(o_b.shape), whole((width, width)),
        ],
        [
            pl.BlockSpec((1, chunk), lambda c, at: (0, c)), shards, shards, full, full,
            whole((8, width)), whole((4, rows, width)), whole((4, rows, width)),
        ],
        [
            shape((1, ff), F32), shape((4, 8, rows, chunk)), shape((4, 8, rows, chunk)), shape((length, width)),
            shape((length, width)), shape((8, width), F32), shape((4, rows, width)), shape((4, rows, width)),
        ],
        [
            pltpu.VMEM((length, width), F32),
            pltpu.VMEM((4, 2, rows, chunk), BF16),
            pltpu.VMEM((4, 2, rows, width), BF16),
        ],
        flops=2 * length * width * (3 * ff + 2 * width),
        moved=2 * length * (6 * width + ff) + 6 * width * ff,
    )(at, dy, normed, slope, w_down, w_up, middle, gain, o_a, o_b, w_out)


def qkv_grad_kernel(at_ref, normed_ref, d_ref, bias_ref, send_ref, keep_ref, stage_ref):
    grad = d_ref[0]
    bias_ref[0] = column_sums(grad.astype(F32))
    split_store(tn(normed_ref[...], grad), at_ref[1], stage_ref, send_ref, keep_ref, (0,))


def qkv_grad(at, normed, d_heads, name):
    length, width = normed.shape
    count, _, chunk = d_heads.shape
    rows = width // 8
    shards = pl.BlockSpec((4, 1, rows, chunk), lambda c, at: (0, c, 0, 0))
    return call(
        qkv_grad_kernel,
        name,
        (count,),
        [whole((length, width)), pl.BlockSpec((1, length, chunk), lambda c, at: (c, 0, 0))],
        [pl.BlockSpec((1, 1, chunk), lambda c, at: (c, 0, 0)), shards, shards],
        [shape((count, 1, chunk), F32), shape((4, count, rows, chunk)), shape((4, count, rows, chunk))],
        [pltpu.VMEM((4, 2, rows, chunk), BF16)],
        flops=2 * count * length * width * chunk,
        moved=2 * (length * width + count * chunk * (length + width)),
    )(at, normed, d_heads)


def token_grad_kernel(at_ref, da_ref, db_ref, w_ref, x_ref, gain_ref, d_att_ref, sums_ref, y0_ref, y1_ref, y2_ref, y3_ref, acc_ref):
    step = pl.program_id(0)

    @pl.when(step == 0)
    def _():
        acc_ref[...] = nt(da_ref[0], w_ref[...])

    for s in range(1, 5):
        d_ref = da_ref if s % 2 == 0 else db_ref

        @pl.when(step == s)
        def _():
            acc_ref[...] += nt(d_ref[s // 2], w_ref[...])

    @pl.when(step == 4)
    def _():
        total = acc_ref[...]
        unit, rate = standardize(x_ref[...].astype(F32))
        sums_ref[0:1, :] = column_sums(total * unit)
        sums_ref[1:2, :] = column_sums(total)
        acc_ref[...] = d_att_ref[...].astype(F32) + standardize_back(total * gain_ref[...], unit, rate)
        for d, ref in enumerate((y0_ref, y1_ref, y2_ref, y3_ref)):
            ref[...] = acc_ref[block_rows(at_ref[0], d, ref.shape[0]), :].astype(BF16)


def token_grad(at, d_a, d_b, w_qkv, x, gain, d_att):
    length, width = x.shape
    chunk = d_a.shape[2]
    part = length // 4
    full = whole((length, width))
    return call(
        token_grad_kernel,
        "token_grad",
        (5,),
        [whole(d_a.shape), whole(d_b.shape), pl.BlockSpec((width, chunk), lambda c, at: (0, c)), full, whole((1, width)), full],
        [whole((8, width))] + [whole((part, width))] * 4,
        [shape((8, width), F32)] + [shape((part, width))] * 4,
        [pltpu.VMEM((length, width), F32)],
        flops=10 * length * width * chunk,
        moved=2 * length * (5 * chunk + 3 * width) + 10 * width * chunk,
    )(at, d_a, d_b, w_qkv, x, gain, d_att)


def settle_kernel(at_ref, *refs):
    out_ref = refs[-1]
    for d, ref in enumerate(refs[:-1]):
        out_ref[at_ref[0] ^ d] = ref[...].astype(out_ref.dtype)


def settle(at, pieces, dtype, name):
    part, width = pieces[0].shape
    rows = part // 4
    return call(
        settle_kernel,
        name,
        (4,),
        [pl.BlockSpec((rows, width), lambda i, at: (i, 0))] * 4,
        pl.BlockSpec((4, rows, width), lambda i, at: (0, i, 0)),
        shape((4, part, width), dtype),
        moved=4 * part * width * 6,
    )(at, *pieces)


QBLOCK = 512


EPSILON = 1e-05
MASKED = -1e30


def layer_norm(inputs, norm_gain, norm_shift):
    center = inputs - jnp.mean(inputs, axis=-1, keepdims=True)
    spread = jnp.mean(center * center, axis=-1, keepdims=True)
    return center * lax.rsqrt(spread + EPSILON) * norm_gain + norm_shift


def gelu_tanh(inputs):
    return jax.nn.gelu(inputs, approximate=True)


def split_pairs(array):
    return array.reshape(array.shape[0], array.shape[1], 2, array.shape[2] // 2)


def block_scores(q_block, k_block, seg_items, mask_items, q_start, k_end, factor):
    raw = jnp.einsum("iqhc,ikhc->ihqk", q_block, k_block, preferred_element_type=jnp.float32)
    q_pos = q_start + jnp.arange(q_block.shape[1])
    k_pos = jnp.arange(k_end)
    causal = k_pos[None, :] <= q_pos[:, None]
    diagonal = k_pos[None, :] == q_pos[:, None]
    same_doc = (
        seg_items[:, q_start : q_start + q_block.shape[1], None] == seg_items[:, None, :k_end]
    )
    allowed = same_doc & causal[None] & ((mask_items[:, None, :k_end] == 1) | diagonal[None])
    return jnp.where(allowed[:, None], raw * factor, MASKED)


def spread_body(
    tokens,
    skip_values,
    segments,
    token_mask,
    attn_gain,
    attn_shift,
    w_qkv,
    q_bias,
    v_bias,
    w_out,
    out_bias,
    mlp_gain,
    mlp_shift,
    w_up,
    up_bias,
    w_down,
    down_bias,
    cotangent,
):
    rows_here, seq_here, width = tokens.shape
    pair_width = 2 * HDIM
    pair_count = width // pair_width
    fresh_pairs = pair_count // 2
    factor = float(HDIM) ** (-0.5)
    tokens_f = tokens.astype(jnp.float32)
    normed_f, first_back = jax.vjp(
        layer_norm, tokens_f, attn_gain.astype(jnp.float32), attn_shift.astype(jnp.float32)
    )
    normed = normed_f.astype(jnp.bfloat16)
    w_pairs = w_qkv.reshape(width, 2 * pair_count + fresh_pairs, pair_width)
    project = jnp.einsum("rsd,dpc->rpsc", normed, w_pairs, preferred_element_type=jnp.float32)
    queries = (
        project[:, :pair_count] + q_bias.astype(jnp.float32).reshape(1, pair_count, 1, pair_width)
    ).astype(jnp.bfloat16)
    key_rows = project[:, pair_count : 2 * pair_count].astype(jnp.bfloat16)
    fresh = (
        project[:, 2 * pair_count :]
        + v_bias.astype(jnp.float32).reshape(1, fresh_pairs, 1, pair_width)
    ).astype(jnp.bfloat16)
    reused = skip_values.reshape(rows_here, seq_here, fresh_pairs, pair_width).transpose(0, 2, 1, 3)
    value_rows = jnp.concatenate([fresh, reused], axis=1)
    flat_shape = (rows_here * pair_count, seq_here, pair_width)
    q_items, k_items, v_items = (
        lax.all_to_all(
            queries.reshape(flat_shape), "head", split_axis=0, concat_axis=1, tiled=True
        ),
        lax.all_to_all(
            key_rows.reshape(flat_shape), "head", split_axis=0, concat_axis=1, tiled=True
        ),
        lax.all_to_all(
            value_rows.reshape(flat_shape), "head", split_axis=0, concat_axis=1, tiled=True
        ),
    )
    seg_rows, mask_rows = (
        lax.all_gather(segments, "head", axis=1, tiled=True),
        lax.all_gather(token_mask, "head", axis=1, tiled=True),
    )
    item_count = q_items.shape[0]
    length = q_items.shape[1]
    item_row = (lax.axis_index("head") * item_count + jnp.arange(item_count)) // pair_count
    picker = (item_row[:, None] == jnp.arange(rows_here)[None, :]).astype(jnp.int32)
    seg_items = jnp.sum(picker[:, :, None] * seg_rows[None], axis=1)
    mask_items = jnp.sum(picker[:, :, None] * mask_rows[None], axis=1)
    q_split = split_pairs(q_items)
    k_split = split_pairs(k_items)
    v_split = split_pairs(v_items)
    block_count = length // QBLOCK
    mixed_blocks = []
    log_sums = []
    for block_id in range(block_count):
        q_start = block_id * QBLOCK
        k_end = q_start + QBLOCK
        scores = block_scores(
            q_split[:, q_start:k_end],
            k_split[:, :k_end],
            seg_items,
            mask_items,
            q_start,
            k_end,
            factor,
        )
        row_max = jnp.max(scores, axis=-1, keepdims=True)
        exp_scores = jnp.exp(scores - row_max)
        row_sum = jnp.sum(exp_scores, axis=-1, keepdims=True)
        soft_probs = (exp_scores / row_sum).astype(jnp.bfloat16)
        mixed = jnp.einsum(
            "ihqk,ikhc->iqhc", soft_probs, v_split[:, :k_end], preferred_element_type=jnp.float32
        )
        mixed_blocks.append(mixed.astype(jnp.bfloat16).reshape(item_count, QBLOCK, pair_width))
        log_sums.append(row_max + jnp.log(row_sum))
    mixed_items = jnp.concatenate(mixed_blocks, axis=1)
    mixed_rows = lax.all_to_all(
        mixed_items, "head", split_axis=1, concat_axis=0, tiled=True
    ).reshape(rows_here, pair_count, seq_here, pair_width)
    w_out_pairs = w_out.reshape(pair_count, pair_width, width)
    attended = jnp.einsum(
        "rpsc,pcd->rsd", mixed_rows, w_out_pairs, preferred_element_type=jnp.float32
    ) + out_bias.astype(jnp.float32)
    middle = tokens_f + attended
    normed_mid, second_back = jax.vjp(
        layer_norm, middle, mlp_gain.astype(jnp.float32), mlp_shift.astype(jnp.float32)
    )
    normed_two = normed_mid.astype(jnp.bfloat16)
    hidden = jnp.einsum(
        "rsd,df->rsf", normed_two, w_up, preferred_element_type=jnp.float32
    ) + up_bias.astype(jnp.float32)
    active_f, gelu_back = jax.vjp(gelu_tanh, hidden)
    active = active_f.astype(jnp.bfloat16)
    result = (
        middle
        + jnp.einsum("rsf,fd->rsd", active, w_down, preferred_element_type=jnp.float32)
        + down_bias.astype(jnp.float32)
    )
    layer_out = result.astype(jnp.bfloat16)
    g_down = jnp.einsum("rsf,rsd->fd", active, cotangent, preferred_element_type=jnp.float32)
    g_down_bias = jnp.sum(cotangent, axis=(0, 1), dtype=jnp.float32)
    d_active = jnp.einsum("rsd,fd->rsf", cotangent, w_down, preferred_element_type=jnp.float32)
    d_hidden = gelu_back(d_active)[0].astype(jnp.bfloat16)
    g_up_bias = jnp.sum(d_hidden, axis=(0, 1), dtype=jnp.float32)
    g_up = jnp.einsum("rsd,rsf->df", normed_two, d_hidden, preferred_element_type=jnp.float32)
    d_normed_two = jnp.einsum("rsf,df->rsd", d_hidden, w_up, preferred_element_type=jnp.float32)
    d_mid_norm, g_mlp_gain, g_mlp_shift = second_back(d_normed_two)
    d_middle = cotangent.astype(jnp.float32) + d_mid_norm
    d_att = d_middle.astype(jnp.bfloat16)
    g_out_bias = jnp.sum(d_att, axis=(0, 1), dtype=jnp.float32)
    g_out = jnp.einsum(
        "rpsc,rsd->pcd", mixed_rows, d_att, preferred_element_type=jnp.float32
    ).reshape(width, width)
    d_mixed = (
        jnp.einsum("rsd,pcd->rpsc", d_att, w_out_pairs, preferred_element_type=jnp.float32)
        .astype(jnp.bfloat16)
        .reshape(flat_shape)
    )
    d_items = lax.all_to_all(d_mixed, "head", split_axis=0, concat_axis=1, tiled=True)
    d_split = split_pairs(d_items)
    dk_total = jnp.zeros((item_count, length, 2, HDIM), jnp.float32)
    dv_total = jnp.zeros((item_count, length, 2, HDIM), jnp.float32)
    dq_blocks = []
    for block_id in range(block_count):
        q_start = block_id * QBLOCK
        k_end = q_start + QBLOCK
        scores = block_scores(
            q_split[:, q_start:k_end],
            k_split[:, :k_end],
            seg_items,
            mask_items,
            q_start,
            k_end,
            factor,
        )
        soft = jnp.exp(scores - log_sums[block_id])
        d_block = d_split[:, q_start:k_end]
        d_probs = jnp.einsum(
            "iqhc,ikhc->ihqk", d_block, v_split[:, :k_end], preferred_element_type=jnp.float32
        )
        delta = jnp.sum(d_probs * soft, axis=-1, keepdims=True)
        d_raw = (soft * (d_probs - delta) * factor).astype(jnp.bfloat16)
        dq_blocks.append(
            jnp.einsum(
                "ihqk,ikhc->iqhc", d_raw, k_split[:, :k_end], preferred_element_type=jnp.float32
            )
        )
        dk_total = dk_total.at[:, :k_end].add(
            jnp.einsum(
                "ihqk,iqhc->ikhc",
                d_raw,
                q_split[:, q_start:k_end],
                preferred_element_type=jnp.float32,
            )
        )
        dv_total = dv_total.at[:, :k_end].add(
            jnp.einsum(
                "ihqk,iqhc->ikhc",
                soft.astype(jnp.bfloat16),
                d_block,
                preferred_element_type=jnp.float32,
            )
        )
    item_shape = (item_count, length, pair_width)
    dq_items = jnp.concatenate(dq_blocks, axis=1).astype(jnp.bfloat16).reshape(item_shape)
    dk_items = dk_total.astype(jnp.bfloat16).reshape(item_shape)
    dv_items = dv_total.astype(jnp.bfloat16).reshape(item_shape)
    dq_rows, dk_rows, dv_rows = (
        lax.all_to_all(dq_items, "head", split_axis=1, concat_axis=0, tiled=True),
        lax.all_to_all(dk_items, "head", split_axis=1, concat_axis=0, tiled=True),
        lax.all_to_all(dv_items, "head", split_axis=1, concat_axis=0, tiled=True),
    )
    row_shape = (rows_here, pair_count, seq_here, pair_width)
    dq_rows = dq_rows.reshape(row_shape)
    dk_rows = dk_rows.reshape(row_shape)
    dv_rows = dv_rows.reshape(row_shape)
    grad_skip = (
        dv_rows[:, fresh_pairs:]
        .transpose(0, 2, 1, 3)
        .reshape(rows_here, seq_here, fresh_pairs * pair_width)
        .astype(jnp.float32)
    )
    d_project = jnp.concatenate([dq_rows, dk_rows, dv_rows[:, :fresh_pairs]], axis=1)
    g_qkv = jnp.einsum(
        "rsd,rpsc->dpc", normed, d_project, preferred_element_type=jnp.float32
    ).reshape(width, -1)
    g_q_bias = jnp.sum(dq_rows, axis=(0, 2), dtype=jnp.float32).reshape(-1)
    g_v_bias = jnp.sum(dv_rows[:, :fresh_pairs], axis=(0, 2), dtype=jnp.float32).reshape(-1)
    d_normed = jnp.einsum("rpsc,dpc->rsd", d_project, w_pairs, preferred_element_type=jnp.float32)
    d_tok_norm, g_attn_gain, g_attn_shift = first_back(d_normed)
    grad_tokens = d_middle + d_tok_norm
    small_sums = lax.psum(
        (
            g_attn_gain,
            g_attn_shift,
            g_q_bias,
            g_v_bias,
            g_out_bias,
            g_mlp_gain,
            g_mlp_shift,
            g_up_bias,
            g_down_bias,
        ),
        ("seq", "head"),
    )
    shards = (
        lax.psum_scatter(g_qkv.astype(jnp.bfloat16), "seq", scatter_dimension=0, tiled=True).astype(
            jnp.float32
        ),
        lax.psum_scatter(g_out.astype(jnp.bfloat16), "seq", scatter_dimension=0, tiled=True).astype(
            jnp.float32
        ),
        lax.psum_scatter(g_up.astype(jnp.bfloat16), "seq", scatter_dimension=0, tiled=True).astype(
            jnp.float32
        ),
        lax.psum_scatter(
            g_down.astype(jnp.bfloat16), "seq", scatter_dimension=0, tiled=True
        ).astype(jnp.float32),
    )
    reduced = (
        lax.psum(shards[0].astype(jnp.bfloat16), "head").astype(jnp.float32),
        lax.psum(shards[1].astype(jnp.bfloat16), "head").astype(jnp.float32),
        lax.psum(shards[2].astype(jnp.bfloat16), "head").astype(jnp.float32),
        lax.psum(shards[3].astype(jnp.bfloat16), "head").astype(jnp.float32),
    )
    return (
        layer_out,
        grad_tokens,
        grad_skip,
        small_sums[0],
        small_sums[1],
        reduced[0],
        small_sums[2],
        small_sums[3],
        reduced[1],
        small_sums[4],
        small_sums[5],
        small_sums[6],
        reduced[2],
        small_sums[7],
        reduced[3],
        small_sums[8],
    )


def pick(array, index):
    return lax.dynamic_index_in_dim(array, index, 0, keepdims=False)


def swap(array, axis, count, bit):
    return lax.ppermute(array, axis, [(i, i ^ bit) for i in range(count)])


def trade(pieces):
    return [pieces[0]] + [swap(pieces[d], "head", 4, d) for d in (1, 2, 3)]


def deal(array, me):
    return [pick(array, me ^ d) for d in range(4)]


def arrange(pieces, me):
    return [lax.select_n(me, *(pieces[q ^ m] for m in range(4))) for q in range(4)]


def add_up(parts):
    total = parts[0].astype(F32)
    for part in parts[1:]:
        total = total + part.astype(F32)
    return total.astype(BF16)


def across_cores(send):
    return swap(send, "seq", 8, 1)


def plane_pieces(pairs, plane):
    return [
        jnp.concatenate([add_up([pick(a, plane ^ d), pick(b, plane ^ d)]) for a, b in pairs], axis=0)
        for d in range(4)
    ]


def across_plane(pieces):
    return [pieces[0]] + [swap(pieces[d], "seq", 8, 2 * d) for d in (1, 2, 3)]


def gate(first, second):
    return lax.optimization_barrier((first, second))


def fits(sizes):
    return sizes == (8, 4)


def row_body(
    tokens,
    skip_values,
    segments,
    token_mask,
    attn_gain,
    attn_shift,
    w_qkv,
    q_bias,
    v_bias,
    w_out,
    out_bias,
    mlp_gain,
    mlp_shift,
    w_up,
    up_bias,
    w_down,
    down_bias,
    cotangent,
):
    me = lax.axis_index("head")
    seq = lax.axis_index("seq")
    core, plane = seq & 1, seq >> 1
    at = jnp.stack([me, core]).astype(jnp.int32)
    rows, part, width = tokens.shape
    length = rows * part
    fresh = width // 2
    ff = w_up.shape[1]
    row = lambda v: v.astype(F32).reshape(1, -1)
    qkv_bias = row(jnp.concatenate([q_bias, jnp.zeros_like(q_bias), v_bias]))
    scale = row(jnp.where(jnp.arange(w_qkv.shape[1]) < width, Q_SCALE, 1.0))

    code = (segments * 2 + token_mask).reshape(rows, 1, part)
    strip = width // 8

    x_pieces = trade(deal(tokens, me))
    so_far = ()
    for d in range(4):
        so_far = project(
            (me ^ d)[None], x_pieces[d], row(attn_gain), row(attn_shift), w_qkv, qkv_bias, scale, length, so_far
        )
    x, normed, proj = so_far
    (code, skip_values), x_pieces = gate((code, skip_values), x_pieces)
    code_row = jnp.concatenate(arrange(trade(deal(code, me)), me), axis=1)
    skip = trade(deal(skip_values, me))

    o_a, lse_a = attend(at, code_row, proj, [proj], 0, 6, 12, 3, "attend_a")
    (o_a, skip), cotangent = gate((o_a, skip), cotangent)
    dy_pieces = trade(deal(cotangent, me))
    o_b, lse_b = attend(at, code_row, proj, skip, 3, 9, 0, 3, "attend_b")
    middle, normed_two, act, slope, *y_pieces = mlp(
        at, x, o_a, o_b, w_out, row(out_bias), row(mlp_gain), row(mlp_shift), w_up, row(up_bias), w_down, row(down_bias), 384
    )
    dy_pieces, y_pieces = gate(dy_pieces, y_pieces)
    y_got = trade(y_pieces)
    dy, g_down_bias, down_send, down_keep = down_grad(at, dy_pieces, act)
    dy, down_send = gate(dy, down_send)
    down_got = across_cores(down_send)
    g_up_bias, up_send, up_keep, d_att, d_o, mlp_sums, out_send, out_keep = mlp_back(
        at, dy, normed_two, slope, w_down, w_up, middle, row(mlp_gain), o_a, o_b, w_out
    )
    down_pieces = plane_pieces([(down_got, down_keep)], plane)
    (d_o, up_send, out_send), (down_pieces, y_got) = gate((d_o, up_send, out_send), (down_pieces, y_got))
    up_got = across_cores(up_send)
    out_got = across_cores(out_send)
    down_parts = across_plane(down_pieces)
    d_b, *skip_grads = attend_back(at, code_row, proj, skip, o_b, d_o, lse_b, 3, 9, 0, 3, 3, "attend_back_b")
    b_bias, b_send, b_keep = qkv_grad(at, normed, d_b, "qkv_grad_b")
    down_quarters = deal(add_up(down_parts).reshape(4, -1, width), me)
    up_pieces = plane_pieces([(up_got, up_keep)], plane)
    (d_o, b_send), (down_quarters, up_pieces, skip_grads) = gate((d_o, b_send), (down_quarters, up_pieces, skip_grads))
    b_got = across_cores(b_send)
    up_parts = across_plane(up_pieces)
    down_got = trade(down_quarters)
    skip_got = trade(skip_grads)
    (d_a,) = attend_back(at, code_row, proj, [proj], o_a, d_o, lse_a, 0, 6, 12, 0, 3, "attend_back_a")
    down_own = add_up(down_got)
    (d_a, b_got), (down_own, skip_got) = gate((d_a, b_got), (down_own, skip_got))
    down_all = trade([down_own] * 4)
    token_sums, *x_grads = token_grad(at, d_a, d_b, w_qkv, x, row(attn_gain), d_att)
    (d_a, x_grads), down_all = gate((d_a, x_grads), down_all)
    x_got = trade(x_grads)
    a_bias, a_send, a_keep = qkv_grad(at, normed, d_a, "qkv_grad_a")
    a_got = across_cores(a_send)

    two = lambda v: v.reshape(4, strip, 2, fresh).transpose(0, 2, 1, 3)
    rest_pieces = plane_pieces([(two(out_got), two(out_keep)), (b_got, b_keep), (a_got, a_keep)], plane)
    rest_parts = across_plane(rest_pieces)
    up = add_up(up_parts)
    up_quarters = up.reshape(4, -1, strip, fresh)
    rest = add_up(rest_parts)
    by_rows = lambda v: v.reshape(v.shape[0], 4, -1, fresh).transpose(1, 0, 2, 3)
    rest_quarters = by_rows(rest)
    up_own = add_up(trade(deal(up_quarters, me)))
    r_up = arrange(trade([up_own] * 4), me)
    rest_own = add_up(trade(deal(rest_quarters, me)))
    rest = jnp.concatenate(arrange(trade([rest_own] * 4), me), axis=1).astype(F32)

    layer_out = settle(at, y_got, BF16, "settle_out")
    grad_skip = settle(at, skip_got, F32, "settle_skip")
    grad_tokens = settle(at, x_got, F32, "settle_tokens")
    r_down = jnp.concatenate(arrange(down_all, me), axis=0).astype(F32)
    r_up = jnp.concatenate([q[i] for q in r_up for i in range(2)], axis=1).astype(F32)
    r_out = jnp.concatenate([rest[0], rest[1]], axis=1)
    r_qkv = jnp.concatenate([rest[4], rest[2], rest[5], rest[3], rest[6]], axis=1)

    small = (
        token_sums[0],
        token_sums[1],
        jnp.concatenate([a_bias[0, 0], b_bias[0, 0]]),
        a_bias[2, 0],
        mlp_sums[2],
        mlp_sums[0],
        mlp_sums[1],
        g_up_bias[0],
        g_down_bias[0],
    )
    packed = jnp.concatenate(small).reshape(-1, 128)
    for axis, count, bit in (("seq", 8, 1), ("seq", 8, 2), ("seq", 8, 4), ("head", 4, 1), ("head", 4, 3)):
        packed = packed + swap(packed, axis, count, bit)
    packed = packed.reshape(-1)
    sums = []
    for entry in small:
        sums.append(packed[: entry.shape[0]])
        packed = packed[entry.shape[0] :]
    return (
        layer_out,
        grad_tokens,
        grad_skip,
        sums[0],
        sums[1],
        r_qkv,
        sums[2],
        sums[3],
        r_out,
        sums[4],
        sums[5],
        sums[6],
        r_up,
        sums[7],
        r_down,
        sums[8],
    )


def solution(mesh):
    sizes = (mesh.shape["seq"], mesh.shape["head"])
    return jax.shard_map(
        row_body if fits(sizes) else spread_body,
        mesh=mesh,
        in_specs=(
            P("seq", "head", None),
            P("seq", "head", None),
            P("seq", "head"),
            P("seq", "head"),
            P(),
            P(),
            P(),
            P(),
            P(),
            P(),
            P(),
            P(),
            P(),
            P(),
            P(),
            P(),
            P(),
            P("seq", "head", None),
        ),
        out_specs=(
            P("seq", "head", None),
            P("seq", "head", None),
            P("seq", "head", None),
            P(),
            P(),
            P("seq", None),
            P(),
            P(),
            P("seq", None),
            P(),
            P(),
            P(),
            P("seq", None),
            P(),
            P("seq", None),
            P(),
        ),
        check_vma=False,
    )
```

```python
import functools

import jax
import jax.numpy as jnp
from jax import lax
from jax.experimental import pallas as pl
from jax.experimental.pallas import tpu as pltpu
from jax.sharding import PartitionSpec as P

HDIM = 64
PAIR = 2 * HDIM
BLK = 256
LN2 = 0.6931471805599453
LOG2E = 1.4426950408889634
Q_SCALE = LOG2E * HDIM**-0.5
BF16 = jnp.bfloat16
F32 = jnp.float32
VMEM_BYTES = 56 << 20
CODE_ROWS = 16
ATTN_GAIN, ATTN_SHIFT, OUT_BIAS, MLP_GAIN, MLP_SHIFT, DOWN_BIAS = (slice(n, n + 1) for n in range(6))


def dot(left, right, left_dim, right_dim):
    return lax.dot_general(
        left, right, (((left_dim,), (right_dim,)), ((), ())), preferred_element_type=F32
    )


def nn(left, right):
    return dot(left, right, 1, 0)


def nt(left, right):
    return dot(left, right, 1, 1)


def tn(left, right):
    return dot(left, right, 0, 0)


def call(kernel, name, grid, in_specs, out_specs, out_shape, scratch=(), flops=0, moved=0, aliases=None):
    return pl.pallas_call(
        kernel,
        name=name,
        grid_spec=pltpu.PrefetchScalarGridSpec(
            num_scalar_prefetch=1,
            grid=grid,
            in_specs=in_specs,
            out_specs=out_specs,
            scratch_shapes=list(scratch),
        ),
        out_shape=out_shape,
        input_output_aliases=aliases or {},
        cost_estimate=pl.CostEstimate(flops=flops, bytes_accessed=moved, transcendentals=0),
        compiler_params=pltpu.CompilerParams(vmem_limit_bytes=VMEM_BYTES),
    )


def shape(dims, dtype=BF16):
    return jax.ShapeDtypeStruct(dims, dtype)


def whole(dims):
    return pl.BlockSpec(dims, lambda *_: (0,) * len(dims))


def once(dims):
    return pl.BlockSpec(dims, lambda *_: (0,) * len(dims), pipeline_mode=pl.Buffered(1))


def standardize(values):
    center = values - jnp.mean(values, axis=1, keepdims=True)
    rate = lax.rsqrt(jnp.mean(center * center, axis=1, keepdims=True) + EPSILON)
    return center * rate, rate


def standardize_back(grad, unit, rate):
    mean_grad = jnp.mean(grad, axis=1, keepdims=True)
    mean_dot = jnp.mean(grad * unit, axis=1, keepdims=True)
    return rate * (grad - mean_grad - unit * mean_dot)


def column_sums(values):
    return jnp.sum(values, axis=0, keepdims=True)


def ways(core):
    return 0, 1 + 2 * core, 3 - 2 * core, 2


def block_rows(place, d, size):
    return pl.ds(pl.multiple_of((place ^ d) * size, size), size)


def each_way(at_ref, refs):
    return [(block_rows(at_ref[0], d, ref.shape[0]), ref) for d, ref in zip(ways(at_ref[1]), refs)]


def deal_out(at_ref, source_ref, own_ref, away_ref, far_ref):
    place, part = at_ref[0], own_ref.shape[0]
    own, near, far, across = (source_ref[block_rows(place, d, part), :] for d in ways(at_ref[1]))
    own_ref[...] = own.astype(own_ref.dtype)
    away_ref[0] = near.astype(own_ref.dtype)
    away_ref[1] = across.astype(own_ref.dtype)
    far_ref[...] = far.astype(own_ref.dtype)


def piece_specs(pieces, rows, cols, at=lambda *index: (0, 0)):
    specs, arrays = [], []
    for piece in pieces:
        if isinstance(piece, tuple):
            array, number = piece
            specs.append(pl.BlockSpec((None, rows, cols), lambda *index, n=number: (n,) + at(*index)))
        else:
            array = piece
            specs.append(pl.BlockSpec((rows, cols), at))
        arrays.append(array)
    return specs, arrays


def project_kernel(at_ref, x_ref, vec_ref, w_ref, affine_ref, *refs):
    row_ref, normed_ref, proj_ref, code_ref = refs[-4:]
    part = row_ref.shape[0]
    tokens = x_ref[:part, :]
    unit, _ = standardize(tokens.astype(F32))
    normed = (unit * vec_ref[ATTN_GAIN] + vec_ref[ATTN_SHIFT]).astype(BF16)
    row_ref[...] = tokens
    normed_ref[...] = normed
    proj_ref[...] = ((nn(normed, w_ref[...]) + affine_ref[0:1, :]) * affine_ref[1:2, :]).astype(BF16)
    code_ref[...] = x_ref[part : part + CODE_ROWS, :part].astype(F32)[:8].astype(jnp.int32)


def project(at, way, piece, vecs, w, affine, length, so_far):
    part, width = length // 4, piece.shape[1]
    cols = w.shape[1]
    place = lambda at: at[0] ^ ways(at[1])[way]
    block = lambda n: pl.BlockSpec((part, n), lambda i, at: (place(at), 0))
    held = [pl.BlockSpec(memory_space=pl.ANY)] * len(so_far)
    return call(
        project_kernel,
        "project",
        (1,),
        [whole((part + CODE_ROWS, width)), whole(vecs.shape), whole((width, cols)), whole(affine.shape)] + held,
        [block(width), block(width), block(cols), pl.BlockSpec((8, part), lambda i, at: (0, place(at)))],
        [shape((length, width)), shape((length, width)), shape((length, cols)), shape((8, length), jnp.int32)],
        flops=2 * part * width * cols,
        moved=2 * (part * (3 * width + cols) + width * cols),
        aliases={5 + n: n for n in range(len(so_far))},
    )(at, piece, vecs, w, affine, *so_far)


def fill_bias(code_ref, bias_ref):
    length = code_ref.shape[1]
    code = code_ref[0:1, :]
    column = jnp.transpose(jnp.broadcast_to(code, (128, length)))
    for i in range(length // BLK):
        q_doc = column[i * BLK : (i + 1) * BLK, :1] >> 1
        for j in range(i + 1):
            k_code = code[:, j * BLK : (j + 1) * BLK]
            same = q_doc == (k_code >> 1)
            real = (k_code & 1) == 1
            if i == j:
                row_at = lax.broadcasted_iota(jnp.int32, (BLK, BLK), 0)
                col_at = lax.broadcasted_iota(jnp.int32, (BLK, BLK), 1)
                allowed = same & (col_at <= row_at) & (real | (col_at == row_at))
            else:
                allowed = same & real
            bias_ref[i * BLK : (i + 1) * BLK, j * BLK : (j + 1) * BLK] = jnp.where(allowed, 0.0, MASKED)


def halves(pair, other):
    first = lax.broadcasted_iota(jnp.int32, pair.shape, 1) < HDIM
    return jnp.where(first, pair, other), jnp.where(first, other, pair)


def gather_values(me_ref, v_refs, value_ref):
    if len(v_refs) == 1:
        return v_refs[0][...]
    for rows, ref in each_way(me_ref, v_refs):
        value_ref[rows, :] = ref[...]
    return value_ref[...]


def forward_kernel(count, me_ref, code_ref, q_ref, k_ref, *refs):
    v_refs, (o_ref, lse_ref, bias_ref, value_ref) = refs[:count], refs[count:]

    @pl.when(pl.program_id(0) == 0)
    def _():
        fill_bias(code_ref, bias_ref)

    length = q_ref.shape[0]
    v_pair = gather_values(me_ref, v_refs, value_ref)
    k_pair = k_ref[...]
    keys = halves(k_pair, jnp.zeros_like(k_pair))
    vals = halves(v_pair, jnp.ones_like(v_pair))
    first = lax.broadcasted_iota(jnp.int32, (BLK, PAIR), 1) < HDIM
    for i in range(length // BLK):
        end = (i + 1) * BLK
        rows = slice(i * BLK, end)
        q = q_ref[rows, :]
        outs, lses = [], []
        for h in range(2):
            scores = nt(q, keys[h][:end]) + bias_ref[rows, :end]
            top = jnp.max(scores, axis=1, keepdims=True)
            weights = jnp.exp2(scores - top).astype(BF16)
            mixed = nn(weights, vals[h][:end])
            total = pltpu.roll(mixed, HDIM, 1)
            outs.append(mixed / total)
            lses.append(top + jnp.log2(total))
        o_ref[rows, :] = jnp.where(first, outs[0], outs[1]).astype(BF16)
        lse_ref[rows, :] = jnp.where(first, lses[0], lses[1])


def backward_kernel(count, first_call, last_call, split, me_ref, code_ref, q_ref, k_ref, *refs):
    refs = list(refs)
    take = lambda n: [refs.pop(0) for _ in range(n)]
    v_refs = take(count)
    o_ref, do_ref, lse_ref, normed_ref = take(4)
    w_refs = take(2 if split else 3)
    before_ref = None if first_call else take(1)[0]
    x_ref, vec_ref, d_att_ref = take(3) if last_call else (None, None, None)
    send_ref, keep_ref, bias_sums_ref = take(3)
    piece_refs = take(3) if split else []
    if last_call:
        *y_refs, sums_ref = take(4)
    else:
        (after_ref,) = take(1)
    bias_ref, value_ref, dkt_ref, dvt_ref, d_ref, w_ref, acc_ref, stage_ref = refs
    step = pl.program_id(0)
    lane = lambda n: slice(n * PAIR, (n + 1) * PAIR)

    @pl.when(step == 0)
    def _():
        fill_bias(code_ref, bias_ref)
        acc_ref[...] = jnp.zeros_like(acc_ref) if first_call else before_ref[...]

    length = q_ref.shape[0]
    v_pair = gather_values(me_ref, v_refs, value_ref)
    k_pair = k_ref[...]
    zero = jnp.zeros_like(k_pair)
    keys = halves(k_pair, zero)
    vals = halves(v_pair, zero)
    first = lax.broadcasted_iota(jnp.int32, (BLK, PAIR), 1) < HDIM
    blocks = length // BLK
    for i in reversed(range(blocks)):
        end = (i + 1) * BLK
        rows = slice(i * BLK, end)
        q, do = q_ref[rows, :], do_ref[rows, :]
        q_t, do_t = jnp.transpose(q), jnp.transpose(do)
        prod = do.astype(F32) * o_ref[rows, :].astype(F32)
        dq = None
        for h in range(2):
            head = slice(h * HDIM, (h + 1) * HDIM)
            lse = lse_ref[rows, h * HDIM : h * HDIM + 1]
            mine = first if h == 0 else ~first
            delta = jnp.sum(jnp.where(mine, prod, 0.0), axis=1, keepdims=True)
            probs = jnp.exp2(nt(q, keys[h][:end]) + bias_ref[rows, :end] - lse)
            d_scores = (probs * (nt(do, vals[h][:end]) - delta)).astype(BF16)
            part = nn(d_scores, keys[h][:end])
            dq = part if dq is None else dq + part
            dv = nn(do_t[head], probs.astype(BF16))
            dk = nn(q_t[head], d_scores)
            if i == blocks - 1:
                dvt_ref[head, :] = dv
                dkt_ref[head, :] = dk
            else:
                dvt_ref[head, :end] += dv
                dkt_ref[head, :end] += dk
        d_ref[rows, lane(0)] = (dq * HDIM**-0.5).astype(BF16)
    d_ref[:, lane(1)] = jnp.transpose(dkt_ref[...] * LN2).astype(BF16)
    dv = jnp.transpose(dvt_ref[...]).astype(BF16)
    if split:
        value_ref[...] = dv
        deal_out(me_ref, value_ref, *piece_refs)
    else:
        d_ref[:, lane(2)] = dv
    for n, ref in enumerate(w_refs):
        w_ref[:, lane(n)] = ref[...]
    grad = d_ref[...]
    bias_sums_ref[0] = column_sums(grad.astype(F32))
    acc_ref[...] += nt(grad, w_ref[...])
    store_units(tn(normed_ref[...], grad), me_ref[1], stage_ref, send_ref, keep_ref, (0,))

    @pl.when(step == pl.num_programs(0) - 1)
    def _():
        if last_call:
            total = acc_ref[...]
            unit, rate = standardize(x_ref[...].astype(F32))
            sums_ref[0:1, :] = column_sums(total * unit)
            sums_ref[1:2, :] = column_sums(total)
            acc_ref[...] = d_att_ref[...].astype(F32) + standardize_back(total * vec_ref[ATTN_GAIN], unit, rate)
            deal_out(me_ref, acc_ref, *y_refs)
        else:
            after_ref[...] = acc_ref[...]


def pair_specs(length, offset):
    return pl.BlockSpec((length, PAIR), lambda p, me: (0, p + offset))


def value_specs(values, length, offset):
    if len(values) == 1:
        return [pair_specs(length, offset)], values
    return piece_specs(values, length // 4, PAIR, lambda p, me: (0, p))


def attend(me, code, proj, values, q_at, k_at, v_at, pairs, name):
    length = proj.shape[0]
    v_specs, v_arrays = value_specs(values, length, v_at)
    return call(
        functools.partial(forward_kernel, len(values)),
        name,
        (pairs,),
        [whole((8, length)), pair_specs(length, q_at), pair_specs(length, k_at)]
        + v_specs,
        [pair_specs(length, 0)] * 2,
        [shape((length, pairs * PAIR)), shape((length, pairs * PAIR), F32)],
        [pltpu.VMEM((length, length), F32), pltpu.VMEM((length, PAIR), BF16)],
        flops=pairs * 24 * length * length * PAIR,
        moved=pairs * length * PAIR * 12,
    )(me, code, proj, proj, *v_arrays)


def attend_back(at, code, proj, values, o, do, lse, normed, w, pair, pairs, o_at, before, last, name):
    length, width = normed.shape
    count = width // PAIR
    split = len(values) > 1
    units = 2 if split else 3
    cols = units * PAIR
    strip, part = width // 8, length // 4
    full = once((length, width))
    v_specs, v_arrays = value_specs(values, length, 2 * count + pair)
    w_spec = lambda offset: pl.BlockSpec((width, PAIR), lambda p, at: (0, p + offset))
    grads = pl.BlockSpec((4, 1, units, strip, PAIR), lambda p, at: (0, p, 0, 0, 0))
    in_specs = (
        [whole((8, length)), pair_specs(length, pair), pair_specs(length, count + pair)]
        + v_specs
        + [pair_specs(length, o_at), pair_specs(length, pair), pair_specs(length, o_at), full]
        + [w_spec(n * count + pair) for n in range(units)]
    )
    args = [code, proj, proj, *v_arrays, o, do, lse, normed] + [w] * units
    out_specs = [grads, grads, pl.BlockSpec((1, 1, cols), lambda p, at: (p, 0, 0))]
    out_shape = [shape((4, pairs, units, strip, PAIR))] * 2 + [shape((pairs, 1, cols), F32)]
    if before is not None:
        in_specs.append(full)
        args.append(before)
    if last is not None:
        in_specs += [full, once(last[1].shape), full]
        args += last
    if split:
        one = pl.BlockSpec((part, PAIR), lambda p, at: (0, p))
        out_specs += [one, pl.BlockSpec((2, part, PAIR), lambda p, at: (0, 0, p)), one]
        out_shape += [shape((part, pairs * PAIR)), shape((2, part, pairs * PAIR)), shape((part, pairs * PAIR))]
    if last is not None:
        out_specs += [once((part, width)), once((2, part, width)), once((part, width)), once((8, width))]
        out_shape += [shape((part, width)), shape((2, part, width)), shape((part, width)), shape((8, width), F32)]
    else:
        out_specs.append(full)
        out_shape.append(shape((length, width), F32))
    return call(
        functools.partial(backward_kernel, len(values), before is None, last is not None, split),
        name,
        (pairs,),
        in_specs,
        out_specs,
        out_shape,
        [
            pltpu.VMEM((length, length), F32),
            pltpu.VMEM((length, PAIR), BF16),
            pltpu.VMEM((PAIR, length), F32),
            pltpu.VMEM((PAIR, length), F32),
            pltpu.VMEM((length, cols), BF16),
            pltpu.VMEM((width, cols), BF16),
            pltpu.VMEM((length, width), F32),
            pltpu.VMEM((4, 2, strip, cols), BF16),
        ],
        flops=pairs * (30 * length * length * PAIR + 4 * length * width * cols),
        moved=pairs * length * PAIR * 18 + 12 * length * width,
    )(at, *args)


GELU_A = 0.7978845608028654
GELU_B = 0.044715


def split_store(grad, core, stage_ref, send_ref, keep_ref, lead):
    stage_ref[...] = grad.astype(BF16).reshape(stage_ref.shape)
    for j in range(4):
        send_ref[(j,) + lead] = stage_ref[j, 1 - core]
        keep_ref[(j,) + lead] = stage_ref[j, core]


def store_units(grad, core, stage_ref, send_ref, keep_ref, lead):
    stage_ref[...] = grad.astype(BF16).reshape(stage_ref.shape)
    for u in range(stage_ref.shape[3] // PAIR):
        lanes = slice(u * PAIR, (u + 1) * PAIR)
        for j in range(4):
            send_ref[(j,) + lead + (u,)] = stage_ref[j, 1 - core, :, lanes]
            keep_ref[(j,) + lead + (u,)] = stage_ref[j, core, :, lanes]


def feed_kernel(
    at_ref, x_ref, oa_ref, ob_ref, d0_ref, d1_ref, d2_ref, d3_ref, wo_ref, vec_ref,
    wu_ref, ub_ref, wd_ref,
    y_own_ref, y_away_ref, y_far_ref, down_send_ref, down_keep_ref, up_send_ref, up_keep_ref, up_bias_ref,
    d_att_ref, d_o_ref, sums_ref, out_send_ref, out_keep_ref,
    dy_ref, middle_ref, normed_ref, y_ref, acc_ref, down_stage_ref, up_stage_ref, out_stage_ref,
):
    step = pl.program_id(0)
    core = at_ref[1]

    @pl.when(step == 0)
    def _():
        for rows, ref in each_way(at_ref, (d0_ref, d1_ref, d2_ref, d3_ref)):
            dy_ref[rows, :] = ref[...]
        half = oa_ref.shape[1]
        middle = (
            x_ref[...].astype(F32)
            + nn(oa_ref[...], wo_ref[:half, :])
            + nn(ob_ref[...], wo_ref[half:, :])
            + vec_ref[OUT_BIAS]
        )
        middle_ref[...] = middle
        unit, _ = standardize(middle)
        normed_ref[...] = (unit * vec_ref[MLP_GAIN] + vec_ref[MLP_SHIFT]).astype(BF16)
        y_ref[...] = middle + vec_ref[DOWN_BIAS]
        acc_ref[...] = jnp.zeros_like(acc_ref)

    dy = dy_ref[...]
    pre = nn(normed_ref[...], wu_ref[...]) + ub_ref[...]
    d_act = nt(dy, wd_ref[...])
    square = pre * pre
    curve = jnp.tanh(pre * (GELU_A + (GELU_A * GELU_B) * square))
    half_up = 0.5 + 0.5 * curve
    act = (pre * half_up).astype(BF16)
    bend = (0.5 * GELU_A) + (1.5 * GELU_A * GELU_B) * square
    d_pre = (d_act * (half_up + pre * bend * (1.0 - curve * curve))).astype(BF16)
    y_ref[...] += nn(act, wd_ref[...])
    down_stage_ref[...] = tn(act, dy).astype(BF16).reshape(down_stage_ref.shape)
    down_send_ref[0] = down_stage_ref[1 - core]
    down_keep_ref[0] = down_stage_ref[core]
    up_bias_ref[...] = column_sums(d_pre.astype(F32))
    acc_ref[...] += nt(d_pre, wu_ref[...])
    split_store(tn(normed_ref[...], d_pre), core, up_stage_ref, up_send_ref, up_keep_ref, (0,))

    @pl.when(step == pl.num_programs(0) - 1)
    def _():
        deal_out(at_ref, y_ref, y_own_ref, y_away_ref, y_far_ref)
        total = acc_ref[...]
        unit, rate = standardize(middle_ref[...])
        dy_f = dy_ref[...].astype(F32)
        sums_ref[0:1, :] = column_sums(total * unit)
        sums_ref[1:2, :] = column_sums(total)
        d_att = (dy_f + standardize_back(total * vec_ref[MLP_GAIN], unit, rate)).astype(BF16)
        d_att_ref[...] = d_att
        sums_ref[2:3, :] = column_sums(d_att.astype(F32))
        sums_ref[3:4, :] = column_sums(dy_f)
        d_o_ref[...] = nt(d_att, wo_ref[...]).astype(BF16)
        grad = jnp.concatenate([tn(oa_ref[...], d_att), tn(ob_ref[...], d_att)], axis=0)
        store_units(grad, core, out_stage_ref, out_send_ref, out_keep_ref, ())


def feed(at, x, o_a, o_b, dy_pieces, w_out, vecs, w_up, up_bias, w_down):
    length, width = x.shape
    ff = w_up.shape[1]
    part = length // 4
    strip, shard, chunk, units = width // 8, ff // 8, ff // 4, width // PAIR
    down = pl.BlockSpec((1, shard, width), lambda c, at: (c, 0, 0))
    up = pl.BlockSpec((4, 1, strip, chunk), lambda c, at: (0, c, 0, 0))
    cols = pl.BlockSpec((1, chunk), lambda c, at: (0, c))
    full = once((length, width))
    dy_specs, dy_arrays = piece_specs(dy_pieces, part, width)
    return call(
        feed_kernel,
        "feed",
        (4,),
        [full, once(o_a.shape), once(o_b.shape)] + dy_specs + [once((width, width)), once(vecs.shape)]
        + [
            pl.BlockSpec((width, chunk), lambda c, at: (0, c)),
            cols,
            pl.BlockSpec((chunk, width), lambda c, at: (c, 0)),
        ],
        [once((part, width)), once((2, part, width)), once((part, width)), down, down, up, up, cols, full, full, once((8, width)), once((4, units, strip, PAIR)), once((4, units, strip, PAIR))],
        [shape((part, width)), shape((2, part, width)), shape((part, width))]
        + [shape((4, shard, width))] * 2
        + [shape((4, 4, strip, chunk))] * 2
        + [shape((1, ff), F32), shape((length, width)), shape((length, width)), shape((8, width), F32)]
        + [shape((4, units, strip, PAIR))] * 2,
        [
            pltpu.VMEM((length, width), BF16),
            pltpu.VMEM((length, width), F32),
            pltpu.VMEM((length, width), BF16),
            pltpu.VMEM((length, width), F32),
            pltpu.VMEM((length, width), F32),
            pltpu.VMEM((2, shard, width), BF16),
            pltpu.VMEM((4, 2, strip, chunk), BF16),
            pltpu.VMEM((4, 2, strip, width), BF16),
        ],
        flops=2 * length * width * (6 * ff + 3 * width),
        moved=2 * (length * width * 7 + 4 * width * ff + 3 * width * width),
    )(at, x, o_a, o_b, *dy_arrays, w_out, vecs, w_up, up_bias, w_down)


def settle_kernel(at_ref, *refs):
    out_ref = refs[-1]
    for d, ref in zip(ways(at_ref[1]), refs[:-1]):
        out_ref[at_ref[0] ^ d] = ref[...].astype(out_ref.dtype)


def settle(at, pieces, dtype, name):
    part, width = pieces[0].shape
    rows = part // 2
    specs, arrays = piece_specs(pieces, rows, width, lambda i, at: (i, 0))
    return call(
        settle_kernel,
        name,
        (2,),
        specs,
        pl.BlockSpec((4, rows, width), lambda i, at: (0, i, 0)),
        shape((4, part, width), dtype),
        moved=4 * part * width * 6,
    )(at, *arrays)


QBLOCK = 512


EPSILON = 1e-05
MASKED = -1e30


def layer_norm(inputs, norm_gain, norm_shift):
    center = inputs - jnp.mean(inputs, axis=-1, keepdims=True)
    spread = jnp.mean(center * center, axis=-1, keepdims=True)
    return center * lax.rsqrt(spread + EPSILON) * norm_gain + norm_shift


def gelu_tanh(inputs):
    return jax.nn.gelu(inputs, approximate=True)


def split_pairs(array):
    return array.reshape(array.shape[0], array.shape[1], 2, array.shape[2] // 2)


def block_scores(q_block, k_block, seg_items, mask_items, q_start, k_end, factor):
    raw = jnp.einsum("iqhc,ikhc->ihqk", q_block, k_block, preferred_element_type=jnp.float32)
    q_pos = q_start + jnp.arange(q_block.shape[1])
    k_pos = jnp.arange(k_end)
    causal = k_pos[None, :] <= q_pos[:, None]
    diagonal = k_pos[None, :] == q_pos[:, None]
    same_doc = (
        seg_items[:, q_start : q_start + q_block.shape[1], None] == seg_items[:, None, :k_end]
    )
    allowed = same_doc & causal[None] & ((mask_items[:, None, :k_end] == 1) | diagonal[None])
    return jnp.where(allowed[:, None], raw * factor, MASKED)


def spread_body(
    tokens,
    skip_values,
    segments,
    token_mask,
    attn_gain,
    attn_shift,
    w_qkv,
    q_bias,
    v_bias,
    w_out,
    out_bias,
    mlp_gain,
    mlp_shift,
    w_up,
    up_bias,
    w_down,
    down_bias,
    cotangent,
):
    rows_here, seq_here, width = tokens.shape
    pair_width = 2 * HDIM
    pair_count = width // pair_width
    fresh_pairs = pair_count // 2
    factor = float(HDIM) ** (-0.5)
    tokens_f = tokens.astype(jnp.float32)
    normed_f, first_back = jax.vjp(
        layer_norm, tokens_f, attn_gain.astype(jnp.float32), attn_shift.astype(jnp.float32)
    )
    normed = normed_f.astype(jnp.bfloat16)
    w_pairs = w_qkv.reshape(width, 2 * pair_count + fresh_pairs, pair_width)
    project = jnp.einsum("rsd,dpc->rpsc", normed, w_pairs, preferred_element_type=jnp.float32)
    queries = (
        project[:, :pair_count] + q_bias.astype(jnp.float32).reshape(1, pair_count, 1, pair_width)
    ).astype(jnp.bfloat16)
    key_rows = project[:, pair_count : 2 * pair_count].astype(jnp.bfloat16)
    fresh = (
        project[:, 2 * pair_count :]
        + v_bias.astype(jnp.float32).reshape(1, fresh_pairs, 1, pair_width)
    ).astype(jnp.bfloat16)
    reused = skip_values.reshape(rows_here, seq_here, fresh_pairs, pair_width).transpose(0, 2, 1, 3)
    value_rows = jnp.concatenate([fresh, reused], axis=1)
    flat_shape = (rows_here * pair_count, seq_here, pair_width)
    q_items, k_items, v_items = (
        lax.all_to_all(
            queries.reshape(flat_shape), "head", split_axis=0, concat_axis=1, tiled=True
        ),
        lax.all_to_all(
            key_rows.reshape(flat_shape), "head", split_axis=0, concat_axis=1, tiled=True
        ),
        lax.all_to_all(
            value_rows.reshape(flat_shape), "head", split_axis=0, concat_axis=1, tiled=True
        ),
    )
    seg_rows, mask_rows = (
        lax.all_gather(segments, "head", axis=1, tiled=True),
        lax.all_gather(token_mask, "head", axis=1, tiled=True),
    )
    item_count = q_items.shape[0]
    length = q_items.shape[1]
    item_row = (lax.axis_index("head") * item_count + jnp.arange(item_count)) // pair_count
    picker = (item_row[:, None] == jnp.arange(rows_here)[None, :]).astype(jnp.int32)
    seg_items = jnp.sum(picker[:, :, None] * seg_rows[None], axis=1)
    mask_items = jnp.sum(picker[:, :, None] * mask_rows[None], axis=1)
    q_split = split_pairs(q_items)
    k_split = split_pairs(k_items)
    v_split = split_pairs(v_items)
    block_count = length // QBLOCK
    mixed_blocks = []
    log_sums = []
    for block_id in range(block_count):
        q_start = block_id * QBLOCK
        k_end = q_start + QBLOCK
        scores = block_scores(
            q_split[:, q_start:k_end],
            k_split[:, :k_end],
            seg_items,
            mask_items,
            q_start,
            k_end,
            factor,
        )
        row_max = jnp.max(scores, axis=-1, keepdims=True)
        exp_scores = jnp.exp(scores - row_max)
        row_sum = jnp.sum(exp_scores, axis=-1, keepdims=True)
        soft_probs = (exp_scores / row_sum).astype(jnp.bfloat16)
        mixed = jnp.einsum(
            "ihqk,ikhc->iqhc", soft_probs, v_split[:, :k_end], preferred_element_type=jnp.float32
        )
        mixed_blocks.append(mixed.astype(jnp.bfloat16).reshape(item_count, QBLOCK, pair_width))
        log_sums.append(row_max + jnp.log(row_sum))
    mixed_items = jnp.concatenate(mixed_blocks, axis=1)
    mixed_rows = lax.all_to_all(
        mixed_items, "head", split_axis=1, concat_axis=0, tiled=True
    ).reshape(rows_here, pair_count, seq_here, pair_width)
    w_out_pairs = w_out.reshape(pair_count, pair_width, width)
    attended = jnp.einsum(
        "rpsc,pcd->rsd", mixed_rows, w_out_pairs, preferred_element_type=jnp.float32
    ) + out_bias.astype(jnp.float32)
    middle = tokens_f + attended
    normed_mid, second_back = jax.vjp(
        layer_norm, middle, mlp_gain.astype(jnp.float32), mlp_shift.astype(jnp.float32)
    )
    normed_two = normed_mid.astype(jnp.bfloat16)
    hidden = jnp.einsum(
        "rsd,df->rsf", normed_two, w_up, preferred_element_type=jnp.float32
    ) + up_bias.astype(jnp.float32)
    active_f, gelu_back = jax.vjp(gelu_tanh, hidden)
    active = active_f.astype(jnp.bfloat16)
    result = (
        middle
        + jnp.einsum("rsf,fd->rsd", active, w_down, preferred_element_type=jnp.float32)
        + down_bias.astype(jnp.float32)
    )
    layer_out = result.astype(jnp.bfloat16)
    g_down = jnp.einsum("rsf,rsd->fd", active, cotangent, preferred_element_type=jnp.float32)
    g_down_bias = jnp.sum(cotangent, axis=(0, 1), dtype=jnp.float32)
    d_active = jnp.einsum("rsd,fd->rsf", cotangent, w_down, preferred_element_type=jnp.float32)
    d_hidden = gelu_back(d_active)[0].astype(jnp.bfloat16)
    g_up_bias = jnp.sum(d_hidden, axis=(0, 1), dtype=jnp.float32)
    g_up = jnp.einsum("rsd,rsf->df", normed_two, d_hidden, preferred_element_type=jnp.float32)
    d_normed_two = jnp.einsum("rsf,df->rsd", d_hidden, w_up, preferred_element_type=jnp.float32)
    d_mid_norm, g_mlp_gain, g_mlp_shift = second_back(d_normed_two)
    d_middle = cotangent.astype(jnp.float32) + d_mid_norm
    d_att = d_middle.astype(jnp.bfloat16)
    g_out_bias = jnp.sum(d_att, axis=(0, 1), dtype=jnp.float32)
    g_out = jnp.einsum(
        "rpsc,rsd->pcd", mixed_rows, d_att, preferred_element_type=jnp.float32
    ).reshape(width, width)
    d_mixed = (
        jnp.einsum("rsd,pcd->rpsc", d_att, w_out_pairs, preferred_element_type=jnp.float32)
        .astype(jnp.bfloat16)
        .reshape(flat_shape)
    )
    d_items = lax.all_to_all(d_mixed, "head", split_axis=0, concat_axis=1, tiled=True)
    d_split = split_pairs(d_items)
    dk_total = jnp.zeros((item_count, length, 2, HDIM), jnp.float32)
    dv_total = jnp.zeros((item_count, length, 2, HDIM), jnp.float32)
    dq_blocks = []
    for block_id in range(block_count):
        q_start = block_id * QBLOCK
        k_end = q_start + QBLOCK
        scores = block_scores(
            q_split[:, q_start:k_end],
            k_split[:, :k_end],
            seg_items,
            mask_items,
            q_start,
            k_end,
            factor,
        )
        soft = jnp.exp(scores - log_sums[block_id])
        d_block = d_split[:, q_start:k_end]
        d_probs = jnp.einsum(
            "iqhc,ikhc->ihqk", d_block, v_split[:, :k_end], preferred_element_type=jnp.float32
        )
        delta = jnp.sum(d_probs * soft, axis=-1, keepdims=True)
        d_raw = (soft * (d_probs - delta) * factor).astype(jnp.bfloat16)
        dq_blocks.append(
            jnp.einsum(
                "ihqk,ikhc->iqhc", d_raw, k_split[:, :k_end], preferred_element_type=jnp.float32
            )
        )
        dk_total = dk_total.at[:, :k_end].add(
            jnp.einsum(
                "ihqk,iqhc->ikhc",
                d_raw,
                q_split[:, q_start:k_end],
                preferred_element_type=jnp.float32,
            )
        )
        dv_total = dv_total.at[:, :k_end].add(
            jnp.einsum(
                "ihqk,iqhc->ikhc",
                soft.astype(jnp.bfloat16),
                d_block,
                preferred_element_type=jnp.float32,
            )
        )
    item_shape = (item_count, length, pair_width)
    dq_items = jnp.concatenate(dq_blocks, axis=1).astype(jnp.bfloat16).reshape(item_shape)
    dk_items = dk_total.astype(jnp.bfloat16).reshape(item_shape)
    dv_items = dv_total.astype(jnp.bfloat16).reshape(item_shape)
    dq_rows, dk_rows, dv_rows = (
        lax.all_to_all(dq_items, "head", split_axis=1, concat_axis=0, tiled=True),
        lax.all_to_all(dk_items, "head", split_axis=1, concat_axis=0, tiled=True),
        lax.all_to_all(dv_items, "head", split_axis=1, concat_axis=0, tiled=True),
    )
    row_shape = (rows_here, pair_count, seq_here, pair_width)
    dq_rows = dq_rows.reshape(row_shape)
    dk_rows = dk_rows.reshape(row_shape)
    dv_rows = dv_rows.reshape(row_shape)
    grad_skip = (
        dv_rows[:, fresh_pairs:]
        .transpose(0, 2, 1, 3)
        .reshape(rows_here, seq_here, fresh_pairs * pair_width)
        .astype(jnp.float32)
    )
    d_project = jnp.concatenate([dq_rows, dk_rows, dv_rows[:, :fresh_pairs]], axis=1)
    g_qkv = jnp.einsum(
        "rsd,rpsc->dpc", normed, d_project, preferred_element_type=jnp.float32
    ).reshape(width, -1)
    g_q_bias = jnp.sum(dq_rows, axis=(0, 2), dtype=jnp.float32).reshape(-1)
    g_v_bias = jnp.sum(dv_rows[:, :fresh_pairs], axis=(0, 2), dtype=jnp.float32).reshape(-1)
    d_normed = jnp.einsum("rpsc,dpc->rsd", d_project, w_pairs, preferred_element_type=jnp.float32)
    d_tok_norm, g_attn_gain, g_attn_shift = first_back(d_normed)
    grad_tokens = d_middle + d_tok_norm
    small_sums = lax.psum(
        (
            g_attn_gain,
            g_attn_shift,
            g_q_bias,
            g_v_bias,
            g_out_bias,
            g_mlp_gain,
            g_mlp_shift,
            g_up_bias,
            g_down_bias,
        ),
        ("seq", "head"),
    )
    shards = (
        lax.psum_scatter(g_qkv.astype(jnp.bfloat16), "seq", scatter_dimension=0, tiled=True).astype(
            jnp.float32
        ),
        lax.psum_scatter(g_out.astype(jnp.bfloat16), "seq", scatter_dimension=0, tiled=True).astype(
            jnp.float32
        ),
        lax.psum_scatter(g_up.astype(jnp.bfloat16), "seq", scatter_dimension=0, tiled=True).astype(
            jnp.float32
        ),
        lax.psum_scatter(
            g_down.astype(jnp.bfloat16), "seq", scatter_dimension=0, tiled=True
        ).astype(jnp.float32),
    )
    reduced = (
        lax.psum(shards[0].astype(jnp.bfloat16), "head").astype(jnp.float32),
        lax.psum(shards[1].astype(jnp.bfloat16), "head").astype(jnp.float32),
        lax.psum(shards[2].astype(jnp.bfloat16), "head").astype(jnp.float32),
        lax.psum(shards[3].astype(jnp.bfloat16), "head").astype(jnp.float32),
    )
    return (
        layer_out,
        grad_tokens,
        grad_skip,
        small_sums[0],
        small_sums[1],
        reduced[0],
        small_sums[2],
        small_sums[3],
        reduced[1],
        small_sums[4],
        small_sums[5],
        small_sums[6],
        reduced[2],
        small_sums[7],
        reduced[3],
        small_sums[8],
    )


def pick(array, index):
    return lax.dynamic_index_in_dim(array, index, 0, keepdims=False)


def gate(first, second):
    return lax.optimization_barrier((first, second))


def add_up(parts):
    total = parts[0].astype(F32)
    for part in parts[1:]:
        total = total + part.astype(F32)
    return total.astype(BF16)


def across_cores(array):
    return lax.ppermute(array, "seq", [(i, i ^ 1) for i in range(8)])


def group_swap(array, core_zero, core_one):
    pairs = [(4 * s + z, 4 * s + (z ^ (core_one if s & 1 else core_zero))) for s in range(8) for z in range(4)]
    return lax.ppermute(array, ("seq", "head"), pairs)


def near_swap(array):
    return group_swap(array, 1, 3)


def far_swap(array):
    return group_swap(array, 3, 1)


def across_swap(array):
    return group_swap(array, 2, 2)


def plane_swap(array, core_zero, core_one):
    return lax.ppermute(array, "seq", [(s, s ^ (core_one if s & 1 else core_zero)) for s in range(8)])


def first_hop(array):
    return plane_swap(array, 2, 4)


def second_hop(array):
    return plane_swap(array, 4, 2)


def plane_first(pairs, plane, core):
    bit = 1 + core
    away, stay = [], []
    for other in range(2):
        at = (plane & bit) | (other * (3 - bit))
        stay.append(jnp.concatenate([add_up([pick(a, at), pick(b, at)]) for a, b in pairs]))
        away.append(jnp.concatenate([add_up([pick(a, at ^ bit), pick(b, at ^ bit)]) for a, b in pairs]))
    return jnp.stack(away), jnp.stack(stay)


def plane_second(got, keep, plane, core):
    mine = jnp.where(plane & (2 - core) > 0, 1, 0)
    both = lambda at: add_up([pick(got, at), pick(keep, at)])
    return both(1 - mine), both(mine)


def group_first(blocks, me, core):
    near, far = 1 + 2 * core, 3 - 2 * core
    take = lambda d: pick(blocks, me ^ d)
    return jnp.stack([take(near), take(2)]), jnp.stack([take(0), take(far)])


def by_owner(own, far, near, me, core):
    one, three = jnp.where(core == 0, near[0], far), jnp.where(core == 0, far, near[0])
    by_distance = [own, one, near[1], three]
    return [lax.select_n(me, *(by_distance[q ^ m] for m in range(4))) for q in range(4)]


def fits(sizes):
    return sizes == (8, 4)


def row_body(
    tokens,
    skip_values,
    segments,
    token_mask,
    attn_gain,
    attn_shift,
    w_qkv,
    q_bias,
    v_bias,
    w_out,
    out_bias,
    mlp_gain,
    mlp_shift,
    w_up,
    up_bias,
    w_down,
    down_bias,
    cotangent,
):
    me = lax.axis_index("head")
    seq = lax.axis_index("seq")
    core, plane = seq & 1, seq >> 1
    near, far = 1 + 2 * core, 3 - 2 * core
    at = jnp.stack([me, core]).astype(jnp.int32)
    rows, part, width = tokens.shape
    length = rows * part
    fresh = width // 2
    ff = w_up.shape[1]
    strip = width // 8
    up_row = up_bias.astype(F32).reshape(1, ff)
    vecs = jnp.stack([attn_gain, attn_shift, out_bias, mlp_gain, mlp_shift, down_bias, down_bias, down_bias]).astype(F32)
    qkv_bias = jnp.concatenate([q_bias, jnp.zeros_like(q_bias), v_bias]).astype(F32)
    scale = jnp.where(jnp.arange(w_qkv.shape[1]) < width, Q_SCALE, 1.0).astype(F32)
    affine = jnp.stack([qkv_bias, scale])

    def forward(array, got):
        return jnp.stack([array, got[1]])

    code = (segments * 2 + token_mask).astype(BF16)
    code = jnp.broadcast_to(jnp.pad(code, ((0, 0), (0, width - part)))[:, None], (rows, CODE_ROWS, width))
    tokens_at = lambda d: jnp.concatenate([pick(tokens, me ^ d), pick(code, me ^ d)])
    pro = lambda way, piece, so_far: project(at, way, piece, vecs, w_qkv, affine, length, so_far)
    near_x = near_swap(tokens_at(near))
    far_x = far_swap(tokens_at(far))
    across_x = across_swap(tokens_at(2))
    so_far = pro(0, tokens_at(0), ())
    so_far = pro(1, near_x, so_far)
    so_far = pro(2, far_x, so_far)
    (across_x, so_far), (skip_values, cotangent) = gate((across_x, so_far), (skip_values, cotangent))
    skip_across = across_swap(pick(skip_values, me ^ 2))
    skip_near = near_swap(pick(skip_values, me ^ near))
    skip_far = far_swap(pick(skip_values, me ^ far))
    dy_across = across_swap(pick(cotangent, me ^ 2))
    dy_near = near_swap(pick(cotangent, me ^ near))
    x, normed, proj, code_row = pro(3, across_x, so_far)
    skip = [pick(skip_values, me), skip_near, skip_far, skip_across]

    from_a = attend(at, code_row, proj, [proj], 0, 6, 12, 3, "attend_a")
    (o_a, lse_a, skip), cotangent = gate((*from_a, skip), cotangent)
    dy_far = far_swap(pick(cotangent, me ^ far))
    o_b, lse_b = attend(at, code_row, proj, skip, 3, 9, 0, 3, "attend_b")
    dy = [pick(cotangent, me), dy_near, dy_far, dy_across]
    fed = feed(at, x, o_a, o_b, dy, w_out, vecs, w_up, up_row, w_down)
    y_own, y_away, y_far, down_send, down_keep, up_send, up_keep, g_up_bias, d_att, d_o, mlp_sums, out_send, out_keep = fed
    down_got = across_cores(down_send)
    up_got = across_cores(up_send)
    y_got = near_swap(y_away)
    out_got = across_cores(out_send)
    from_b = attend_back(
        at, code_row, proj, skip, o_b, d_o, lse_b, normed, w_qkv, 3, 3, 0, None, None, "attend_back_b"
    )
    from_b, (down_got, up_got, y_got, out_got) = gate(from_b, (down_got, up_got, y_got, out_got))
    b_send, b_keep, b_bias, s_own, s_away, s_far, d_normed = from_b
    lines = lambda v: v.reshape(4, -1, strip, width)
    big_away, big_stay = plane_first([(up_got, up_keep), (lines(down_got), lines(down_keep))], plane, core)
    y_last = forward(y_far, y_got)
    (d_normed, s_away, b_send), (big_away, big_stay, y_last) = gate((d_normed, s_away, b_send), (big_away, big_stay, y_last))
    big_got = first_hop(big_away)
    y_last = far_swap(y_last)
    s_got = near_swap(s_away)
    b_got = across_cores(b_send)
    from_a = attend_back(
        at, code_row, proj, [proj], o_a, d_o, lse_a, normed, w_qkv, 0, 3, 0, d_normed, [x, vecs, d_att], "attend_back_a"
    )
    from_a, (big_got, y_last, s_got, b_got) = gate(from_a, (big_got, y_last, s_got, b_got))
    a_send, a_keep, a_bias, x_own, x_away, x_far, token_sums = from_a

    q_sums = jnp.concatenate([v[:, 0, :PAIR].reshape(-1) for v in (a_bias, b_bias)])
    v_sums = a_bias[:, 0, 2 * PAIR :].reshape(-1)
    small = (
        token_sums[0],
        token_sums[1],
        q_sums,
        v_sums,
        mlp_sums[2],
        mlp_sums[0],
        mlp_sums[1],
        g_up_bias[0],
        mlp_sums[3],
    )
    packed = jnp.concatenate(small).reshape(-1, 128)
    units = lambda v: v.reshape(4, -1, strip, PAIR)

    x_across = across_swap(x_away[1])
    a_got = across_cores(a_send)
    big_send, big_stay = plane_second(big_got, big_stay, plane, core)
    big_got = second_hop(big_send)
    small_got = across_cores(packed)
    s_last = far_swap(forward(s_far, s_got))

    (big_got, a_got, x_away, x_far), (x_across, small_got, s_last) = gate(
        (big_got, a_got, x_away, x_far), (x_across, small_got, s_last)
    )
    x_near = near_swap(x_away[0])
    x_far = far_swap(x_far)
    big = add_up([big_got, big_stay]).reshape(2, 4, strip, width).transpose(1, 0, 2, 3)
    big_send, big_keep = group_first(big, me, core)
    big_got = near_swap(big_send)
    rest_away, rest_stay = plane_first(
        [(out_got, out_keep), (units(b_got), units(b_keep)), (units(a_got), units(a_keep))], plane, core
    )
    rest_got = first_hop(rest_away)
    packed = packed + small_got
    small_got = plane_swap(packed, 2, 2)

    rest_got, (small_got, x_near, x_far) = gate(rest_got, (small_got, x_near, x_far))
    rest_send, rest_stay = plane_second(rest_got, rest_stay, plane, core)
    rest_got = second_hop(rest_send)
    packed = packed + small_got
    small_got = plane_swap(packed, 4, 4)

    big_got, (rest_got, small_got) = gate(big_got, (rest_got, small_got))
    rest = add_up([rest_got, rest_stay]).reshape(-1, 4, strip // 4, PAIR).transpose(1, 0, 2, 3)
    rest_send, rest_keep = group_first(rest, me, core)
    rest_got = near_swap(rest_send)
    big_sum = add_up([big_got, big_keep])
    big_got = far_swap(big_sum[1])
    packed = packed + small_got
    small_got = group_swap(packed, 1, 1)

    big_got, rest_got = gate(big_got, rest_got)
    rest_sum = add_up([rest_got, rest_keep])
    rest_got = far_swap(rest_sum[1])
    big_own = add_up([big_got, big_sum[0]])
    big_far = far_swap(big_own)

    (big_far, rest_got), small_got = gate((big_far, rest_got), small_got)
    rest_own = add_up([rest_got, rest_sum[0]])
    rest_far = far_swap(rest_own)
    packed = packed + small_got
    small_got = group_swap(packed, 3, 3)
    big_near = near_swap(jnp.stack([big_own, big_far]))
    rest_near = near_swap(jnp.stack([rest_own, rest_far]))
    packed = (packed + small_got).reshape(-1)

    layer_out = settle(at, [y_own, (y_got, 0), (y_last, 0), (y_last, 1)], BF16, "settle_out")
    grad_skip = settle(at, [s_own, (s_got, 0), (s_last, 0), (s_last, 1)], F32, "settle_skip")
    grad_tokens = settle(at, [x_own, x_near, x_far, x_across], F32, "settle_tokens")
    big = by_owner(big_own, big_far, big_near, me, core)
    rest = jnp.concatenate(by_owner(rest_own, rest_far, rest_near, me, core), axis=1).astype(F32)
    r_up = jnp.concatenate([q[0] for q in big], axis=1).astype(F32)
    r_down = jnp.concatenate([q[1] for q in big], axis=0).astype(F32)
    count = width // PAIR
    r_out = jnp.concatenate([rest[u] for u in range(count)], axis=1)
    unit_of = lambda p, n: rest[count + (p - count // 2) * 2 + n] if p >= count // 2 else rest[2 * count + 3 * p + n]
    order = [unit_of(p, n) for n in range(2) for p in range(count)] + [unit_of(p, 2) for p in range(count // 2)]
    r_qkv = jnp.concatenate(order, axis=1)
    sums = []
    for entry in small:
        sums.append(packed[: entry.shape[0]])
        packed = packed[entry.shape[0] :]
    return (
        layer_out,
        grad_tokens,
        grad_skip,
        sums[0],
        sums[1],
        r_qkv,
        sums[2],
        sums[3],
        r_out,
        sums[4],
        sums[5],
        sums[6],
        r_up,
        sums[7],
        r_down,
        sums[8],
    )


def solution(mesh):
    sizes = (mesh.shape["seq"], mesh.shape["head"])
    return jax.shard_map(
        row_body if fits(sizes) else spread_body,
        mesh=mesh,
        in_specs=(
            P("seq", "head", None),
            P("seq", "head", None),
            P("seq", "head"),
            P("seq", "head"),
            P(),
            P(),
            P(),
            P(),
            P(),
            P(),
            P(),
            P(),
            P(),
            P(),
            P(),
            P(),
            P(),
            P("seq", "head", None),
        ),
        out_specs=(
            P("seq", "head", None),
            P("seq", "head", None),
            P("seq", "head", None),
            P(),
            P(),
            P("seq", None),
            P(),
            P(),
            P("seq", None),
            P(),
            P(),
            P(),
            P("seq", None),
            P(),
            P("seq", None),
            P(),
        ),
        check_vma=False,
    )
```

```python
import functools

import jax
import jax.numpy as jnp
from jax import lax
from jax.experimental import pallas as pl
from jax.experimental.pallas import tpu as pltpu
from jax.sharding import PartitionSpec as P

HDIM = 64
PAIR = 2 * HDIM
BLK = 256
LN2 = 0.6931471805599453
LOG2E = 1.4426950408889634
Q_SCALE = LOG2E * HDIM**-0.5
BF16 = jnp.bfloat16
F32 = jnp.float32
VMEM_BYTES = 56 << 20
CODE_ROWS = 16
GAIN_ROWS, Q_ROWS, V_ROWS, SUM_ROWS = 6, 12, 18, 72
ATTN_GAIN, ATTN_SHIFT, OUT_BIAS, MLP_GAIN, MLP_SHIFT, DOWN_BIAS = (slice(n, n + 1) for n in range(6))


def dot(left, right, left_dim, right_dim):
    return lax.dot_general(
        left, right, (((left_dim,), (right_dim,)), ((), ())), preferred_element_type=F32
    )


def nn(left, right):
    return dot(left, right, 1, 0)


def nt(left, right):
    return dot(left, right, 1, 1)


def tn(left, right):
    return dot(left, right, 0, 0)


def call(kernel, name, grid, in_specs, out_specs, out_shape, scratch=(), flops=0, moved=0, aliases=None):
    return pl.pallas_call(
        kernel,
        name=name,
        grid_spec=pltpu.PrefetchScalarGridSpec(
            num_scalar_prefetch=1,
            grid=grid,
            in_specs=in_specs,
            out_specs=out_specs,
            scratch_shapes=list(scratch),
        ),
        out_shape=out_shape,
        input_output_aliases=aliases or {},
        cost_estimate=pl.CostEstimate(flops=flops, bytes_accessed=moved, transcendentals=0),
        compiler_params=pltpu.CompilerParams(vmem_limit_bytes=VMEM_BYTES),
    )


def shape(dims, dtype=BF16):
    return jax.ShapeDtypeStruct(dims, dtype)


def whole(dims):
    return pl.BlockSpec(dims, lambda *_: (0,) * len(dims))


def once(dims):
    return pl.BlockSpec(dims, lambda *_: (0,) * len(dims), pipeline_mode=pl.Buffered(1))


def standardize(values):
    center = values - jnp.mean(values, axis=1, keepdims=True)
    rate = lax.rsqrt(jnp.mean(center * center, axis=1, keepdims=True) + EPSILON)
    return center * rate, rate


def standardize_back(grad, unit, rate):
    mean_grad = jnp.mean(grad, axis=1, keepdims=True)
    mean_dot = jnp.mean(grad * unit, axis=1, keepdims=True)
    return rate * (grad - mean_grad - unit * mean_dot)


def column_sums(values):
    return jnp.sum(values, axis=0, keepdims=True)


def ways(core):
    return 0, 1 + 2 * core, 3 - 2 * core, 2


def block_rows(place, d, size):
    return pl.ds(pl.multiple_of((place ^ d) * size, size), size)


def each_way(at_ref, refs):
    return [(block_rows(at_ref[0], d, ref.shape[0]), ref) for d, ref in zip(ways(at_ref[1]), refs)]


def deal_out(at_ref, source_ref, own_ref, away_ref, far_ref):
    place, part = at_ref[0], own_ref.shape[0]
    own, near, far, across = (source_ref[block_rows(place, d, part), :] for d in ways(at_ref[1]))
    own_ref[...] = own.astype(own_ref.dtype)
    away_ref[0] = near.astype(own_ref.dtype)
    away_ref[1] = across.astype(own_ref.dtype)
    far_ref[...] = far.astype(own_ref.dtype)


def piece_specs(pieces, rows, cols, at=lambda *index: (0, 0)):
    specs, arrays = [], []
    for piece in pieces:
        if isinstance(piece, tuple):
            array, number = piece
            specs.append(pl.BlockSpec((None, rows, cols), lambda *index, n=number: (n,) + at(*index)))
        else:
            array = piece
            specs.append(pl.BlockSpec((rows, cols), at))
        arrays.append(array)
    return specs, arrays


def project_kernel(at_ref, x_ref, vec_ref, w_ref, affine_ref, *refs):
    row_ref, normed_ref, proj_ref, code_ref = refs[-4:]
    part = row_ref.shape[0]
    tokens = x_ref[:part, :]
    unit, _ = standardize(tokens.astype(F32))
    normed = (unit * vec_ref[ATTN_GAIN] + vec_ref[ATTN_SHIFT]).astype(BF16)
    row_ref[...] = tokens
    normed_ref[...] = normed
    proj_ref[...] = ((nn(normed, w_ref[...]) + affine_ref[0:1, :]) * affine_ref[1:2, :]).astype(BF16)
    code_ref[...] = x_ref[part : part + CODE_ROWS, :part].astype(F32)[:8].astype(jnp.int32)


def project(at, way, piece, vecs, w, affine, length, so_far):
    part, width = length // 4, piece.shape[1]
    cols = w.shape[1]
    place = lambda at: at[0] ^ ways(at[1])[way]
    block = lambda n: pl.BlockSpec((part, n), lambda i, at: (place(at), 0))
    held = [pl.BlockSpec(memory_space=pl.ANY)] * len(so_far)
    return call(
        project_kernel,
        "project",
        (1,),
        [whole((part + CODE_ROWS, width)), whole(vecs.shape), whole((width, cols)), whole(affine.shape)] + held,
        [block(width), block(width), block(cols), pl.BlockSpec((8, part), lambda i, at: (0, place(at)))],
        [shape((length, width)), shape((length, width)), shape((length, cols)), shape((8, length), jnp.int32)],
        flops=2 * part * width * cols,
        moved=2 * (part * (3 * width + cols) + width * cols),
        aliases={5 + n: n for n in range(len(so_far))},
    )(at, piece, vecs, w, affine, *so_far)


def fill_bias(code_ref, bias_ref):
    length = code_ref.shape[1]
    code = code_ref[0:1, :]
    column = jnp.transpose(jnp.broadcast_to(code, (128, length)))
    for i in range(length // BLK):
        q_doc = column[i * BLK : (i + 1) * BLK, :1] >> 1
        for j in range(i + 1):
            k_code = code[:, j * BLK : (j + 1) * BLK]
            same = q_doc == (k_code >> 1)
            real = (k_code & 1) == 1
            if i == j:
                row_at = lax.broadcasted_iota(jnp.int32, (BLK, BLK), 0)
                col_at = lax.broadcasted_iota(jnp.int32, (BLK, BLK), 1)
                allowed = same & (col_at <= row_at) & (real | (col_at == row_at))
            else:
                allowed = same & real
            bias_ref[i * BLK : (i + 1) * BLK, j * BLK : (j + 1) * BLK] = jnp.where(allowed, 0.0, MASKED)


def halves(pair, other):
    first = lax.broadcasted_iota(jnp.int32, pair.shape, 1) < HDIM
    return jnp.where(first, pair, other), jnp.where(first, other, pair)


def gather_values(me_ref, v_refs, value_ref):
    if len(v_refs) == 1:
        return v_refs[0][...]
    for rows, ref in each_way(me_ref, v_refs):
        value_ref[rows, :] = ref[...]
    return value_ref[...]


def forward_kernel(count, me_ref, code_ref, q_ref, k_ref, *refs):
    v_refs, (o_ref, lse_ref, bias_ref, value_ref) = refs[:count], refs[count:]

    @pl.when(pl.program_id(0) == 0)
    def _():
        fill_bias(code_ref, bias_ref)

    length = q_ref.shape[0]
    v_pair = gather_values(me_ref, v_refs, value_ref)
    k_pair = k_ref[...]
    keys = halves(k_pair, jnp.zeros_like(k_pair))
    vals = halves(v_pair, jnp.ones_like(v_pair))
    first = lax.broadcasted_iota(jnp.int32, (BLK, PAIR), 1) < HDIM
    for i in range(length // BLK):
        end = (i + 1) * BLK
        rows = slice(i * BLK, end)
        q = q_ref[rows, :]
        outs, lses = [], []
        for h in range(2):
            scores = nt(q, keys[h][:end]) + bias_ref[rows, :end]
            top = jnp.max(scores, axis=1, keepdims=True)
            weights = jnp.exp2(scores - top).astype(BF16)
            mixed = nn(weights, vals[h][:end])
            total = pltpu.roll(mixed, HDIM, 1)
            outs.append(mixed / total)
            lses.append(top + jnp.log2(total))
        o_ref[rows, :] = jnp.where(first, outs[0], outs[1]).astype(BF16)
        lse_ref[rows, :] = jnp.where(first, lses[0], lses[1])


def backward_kernel(count, first_call, last_call, split, me_ref, code_ref, q_ref, k_ref, *refs):
    refs = list(refs)
    take = lambda n: [refs.pop(0) for _ in range(n)]
    v_refs = take(count)
    o_ref, do_ref, lse_ref, normed_ref = take(4)
    w_refs = take(2 if split else 3)
    before_ref = None if first_call else take(1)[0]
    if last_call:
        x_ref, vec_ref, d_att_ref, mlp_sums_ref, up_sums_ref, other_sums_ref = take(6)
    send_ref, keep_ref = take(2)
    bias_sums_ref = None if last_call else take(1)[0]
    piece_refs = take(3) if split else []
    if last_call:
        *y_refs, packed_ref = take(4)
    else:
        (after_ref,) = take(1)
    bias_ref, value_ref, dkt_ref, dvt_ref, d_ref, w_ref, acc_ref, stage_ref = refs
    step = pl.program_id(0)
    lane = lambda n: slice(n * PAIR, (n + 1) * PAIR)

    @pl.when(step == 0)
    def _():
        fill_bias(code_ref, bias_ref)
        acc_ref[...] = jnp.zeros_like(acc_ref) if first_call else before_ref[...]

    length = q_ref.shape[0]
    v_pair = gather_values(me_ref, v_refs, value_ref)
    k_pair = k_ref[...]
    zero = jnp.zeros_like(k_pair)
    keys = halves(k_pair, zero)
    vals = halves(v_pair, zero)
    first = lax.broadcasted_iota(jnp.int32, (BLK, PAIR), 1) < HDIM
    blocks = length // BLK
    for i in reversed(range(blocks)):
        end = (i + 1) * BLK
        rows = slice(i * BLK, end)
        q, do = q_ref[rows, :], do_ref[rows, :]
        q_t, do_t = jnp.transpose(q), jnp.transpose(do)
        prod = do.astype(F32) * o_ref[rows, :].astype(F32)
        dq = None
        for h in range(2):
            head = slice(h * HDIM, (h + 1) * HDIM)
            lse = lse_ref[rows, h * HDIM : h * HDIM + 1]
            mine = first if h == 0 else ~first
            delta = jnp.sum(jnp.where(mine, prod, 0.0), axis=1, keepdims=True)
            probs = jnp.exp2(nt(q, keys[h][:end]) + bias_ref[rows, :end] - lse)
            d_scores = (probs * (nt(do, vals[h][:end]) - delta)).astype(BF16)
            part = nn(d_scores, keys[h][:end])
            dq = part if dq is None else dq + part
            dv = nn(do_t[head], probs.astype(BF16))
            dk = nn(q_t[head], d_scores)
            if i == blocks - 1:
                dvt_ref[head, :] = dv
                dkt_ref[head, :] = dk
            else:
                dvt_ref[head, :end] += dv
                dkt_ref[head, :end] += dk
        d_ref[rows, lane(0)] = (dq * HDIM**-0.5).astype(BF16)
    d_ref[:, lane(1)] = jnp.transpose(dkt_ref[...] * LN2).astype(BF16)
    dv = jnp.transpose(dvt_ref[...]).astype(BF16)
    if split:
        value_ref[...] = dv
        deal_out(me_ref, value_ref, *piece_refs)
    else:
        d_ref[:, lane(2)] = dv
    for n, ref in enumerate(w_refs):
        w_ref[:, lane(n)] = ref[...]
    grad = d_ref[...]
    sums = column_sums(grad.astype(F32))
    if last_call:
        packed_ref[pl.ds(Q_ROWS + step, 1), :] = sums[:, lane(0)]
        packed_ref[pl.ds(V_ROWS + step, 1), :] = sums[:, lane(2)]
    else:
        bias_sums_ref[0] = sums
    acc_ref[...] += nt(grad, w_ref[...])
    store_units(tn(normed_ref[...], grad), me_ref, stage_ref, send_ref, keep_ref, (0,))

    @pl.when(step == pl.num_programs(0) - 1)
    def _():
        if last_call:
            total = acc_ref[...]
            unit, rate = standardize(x_ref[...].astype(F32))
            rows_of = lambda ref, row: [ref[row : row + 1, lane(n)] for n in range(ref.shape[1] // PAIR)]
            for first_row, vector in ((0, column_sums(total * unit)), (GAIN_ROWS, column_sums(total))):
                for n in range(GAIN_ROWS):
                    packed_ref[first_row + n : first_row + n + 1, :] = vector[:, lane(n)]
            others = [other_sums_ref[p, :, lane(0)] for p in range(other_sums_ref.shape[0])]
            tail_rows = rows_of(mlp_sums_ref, 2) + rows_of(mlp_sums_ref, 0) + rows_of(mlp_sums_ref, 1)
            tail_rows += rows_of(up_sums_ref, 0) + rows_of(mlp_sums_ref, 3)
            for first_row, values in ((Q_ROWS + len(others), others), (V_ROWS + len(others), tail_rows)):
                for n, value in enumerate(values):
                    packed_ref[first_row + n : first_row + n + 1, :] = value
            acc_ref[...] = d_att_ref[...].astype(F32) + standardize_back(total * vec_ref[ATTN_GAIN], unit, rate)
            deal_out(me_ref, acc_ref, *y_refs)
        else:
            after_ref[...] = acc_ref[...]


def pair_specs(length, offset):
    return pl.BlockSpec((length, PAIR), lambda p, me: (0, p + offset))


def value_specs(values, length, offset):
    if len(values) == 1:
        return [pair_specs(length, offset)], values
    return piece_specs(values, length // 4, PAIR, lambda p, me: (0, p))


def attend(me, code, proj, values, q_at, k_at, v_at, pairs, name):
    length = proj.shape[0]
    v_specs, v_arrays = value_specs(values, length, v_at)
    return call(
        functools.partial(forward_kernel, len(values)),
        name,
        (pairs,),
        [whole((8, length)), pair_specs(length, q_at), pair_specs(length, k_at)]
        + v_specs,
        [pair_specs(length, 0)] * 2,
        [shape((length, pairs * PAIR)), shape((length, pairs * PAIR), F32)],
        [pltpu.VMEM((length, length), F32), pltpu.VMEM((length, PAIR), BF16)],
        flops=pairs * 24 * length * length * PAIR,
        moved=pairs * length * PAIR * 12,
    )(me, code, proj, proj, *v_arrays)


def attend_back(at, code, proj, values, o, do, lse, normed, w, pair, pairs, o_at, before, last, name):
    length, width = normed.shape
    count = width // PAIR
    split = len(values) > 1
    units = 2 if split else 3
    cols = units * PAIR
    strip, part = width // 8, length // 4
    full = once((length, width))
    v_specs, v_arrays = value_specs(values, length, 2 * count + pair)
    w_spec = lambda offset: pl.BlockSpec((width, PAIR), lambda p, at: (0, p + offset))
    grads = pl.BlockSpec((4, 1, units, strip, PAIR), lambda p, at: (0, p, 0, 0, 0))
    in_specs = (
        [whole((8, length)), pair_specs(length, pair), pair_specs(length, count + pair)]
        + v_specs
        + [pair_specs(length, o_at), pair_specs(length, pair), pair_specs(length, o_at), full]
        + [w_spec(n * count + pair) for n in range(units)]
    )
    args = [code, proj, proj, *v_arrays, o, do, lse, normed] + [w] * units
    out_specs = [grads, grads]
    out_shape = [shape((4, pairs, units, strip, PAIR))] * 2
    if last is None:
        out_specs.append(pl.BlockSpec((1, 1, cols), lambda p, at: (p, 0, 0)))
        out_shape.append(shape((pairs, 1, cols), F32))
    if before is not None:
        in_specs.append(full)
        args.append(before)
    if last is not None:
        in_specs += [full, once(last[1].shape), full] + [once(v.shape) for v in last[3:]]
        args += last
    if split:
        one = pl.BlockSpec((part, PAIR), lambda p, at: (0, p))
        out_specs += [one, pl.BlockSpec((2, part, PAIR), lambda p, at: (0, 0, p)), one]
        out_shape += [shape((part, pairs * PAIR)), shape((2, part, pairs * PAIR)), shape((part, pairs * PAIR))]
    if last is not None:
        out_specs += [once((part, width)), once((2, part, width)), once((part, width)), once((SUM_ROWS, PAIR))]
        out_shape += [shape((part, width)), shape((2, part, width)), shape((part, width)), shape((SUM_ROWS, PAIR), F32)]
    else:
        out_specs.append(full)
        out_shape.append(shape((length, width), F32))
    return call(
        functools.partial(backward_kernel, len(values), before is None, last is not None, split),
        name,
        (pairs,),
        in_specs,
        out_specs,
        out_shape,
        [
            pltpu.VMEM((length, length), F32),
            pltpu.VMEM((length, PAIR), BF16),
            pltpu.VMEM((PAIR, length), F32),
            pltpu.VMEM((PAIR, length), F32),
            pltpu.VMEM((length, cols), BF16),
            pltpu.VMEM((width, cols), BF16),
            pltpu.VMEM((length, width), F32),
            pltpu.VMEM((4, 2, strip, cols), BF16),
        ],
        flops=pairs * (30 * length * length * PAIR + 4 * length * width * cols),
        moved=pairs * length * PAIR * 18 + 12 * length * width,
    )(at, *args)


GELU_A = 0.7978845608028654
GELU_B = 0.044715


def plane_order(core):
    return 3, 1 + core, 2 - core, 0


def plane_place(chip, core):
    return jnp.where(chip == 3, 0, jnp.where(chip == 0, 3, jnp.where(chip == 1 + core, 1, 2)))


def split_store(grad, at_ref, stage_ref, send_ref, keep_ref, lead):
    core, chip = at_ref[1], at_ref[2]
    stage_ref[...] = grad.astype(BF16).reshape(stage_ref.shape)
    for j, (theirs, mine) in enumerate(zip(plane_order(1 - core), plane_order(core))):
        send_ref[(j,) + lead] = stage_ref[chip ^ theirs, 1 - core]
        keep_ref[(j,) + lead] = stage_ref[chip ^ mine, core]


def store_units(grad, at_ref, stage_ref, send_ref, keep_ref, lead):
    core, chip = at_ref[1], at_ref[2]
    stage_ref[...] = grad.astype(BF16).reshape(stage_ref.shape)
    for u in range(stage_ref.shape[3] // PAIR):
        lanes = slice(u * PAIR, (u + 1) * PAIR)
        for j, (theirs, mine) in enumerate(zip(plane_order(1 - core), plane_order(core))):
            send_ref[(j,) + lead + (u,)] = stage_ref[chip ^ theirs, 1 - core, :, lanes]
            keep_ref[(j,) + lead + (u,)] = stage_ref[chip ^ mine, core, :, lanes]


def feed_kernel(
    at_ref, x_ref, oa_ref, ob_ref, d0_ref, d1_ref, d2_ref, d3_ref, wo_ref, vec_ref,
    wu_ref, ub_ref, wd_ref,
    y_own_ref, y_away_ref, y_far_ref, down_send_ref, down_keep_ref, up_send_ref, up_keep_ref, up_bias_ref,
    d_att_ref, d_o_ref, sums_ref, out_send_ref, out_keep_ref,
    dy_ref, middle_ref, normed_ref, y_ref, acc_ref, down_stage_ref, up_stage_ref, out_stage_ref,
):
    step = pl.program_id(0)
    core = at_ref[1]

    @pl.when(step == 0)
    def _():
        for rows, ref in each_way(at_ref, (d0_ref, d1_ref, d2_ref, d3_ref)):
            dy_ref[rows, :] = ref[...]
        half = oa_ref.shape[1]
        middle = (
            x_ref[...].astype(F32)
            + nn(oa_ref[...], wo_ref[:half, :])
            + nn(ob_ref[...], wo_ref[half:, :])
            + vec_ref[OUT_BIAS]
        )
        middle_ref[...] = middle
        unit, _ = standardize(middle)
        normed_ref[...] = (unit * vec_ref[MLP_GAIN] + vec_ref[MLP_SHIFT]).astype(BF16)
        y_ref[...] = middle + vec_ref[DOWN_BIAS]
        acc_ref[...] = jnp.zeros_like(acc_ref)

    dy = dy_ref[...]
    pre = nn(normed_ref[...], wu_ref[...]) + ub_ref[...]
    d_act = nt(dy, wd_ref[...])
    square = pre * pre
    curve = jnp.tanh(pre * (GELU_A + (GELU_A * GELU_B) * square))
    half_up = 0.5 + 0.5 * curve
    act = (pre * half_up).astype(BF16)
    bend = (0.5 * GELU_A) + (1.5 * GELU_A * GELU_B) * square
    d_pre = (d_act * (half_up + pre * bend * (1.0 - curve * curve))).astype(BF16)
    y_ref[...] += nn(act, wd_ref[...])
    down_stage_ref[...] = tn(act, dy).astype(BF16).reshape(down_stage_ref.shape)
    down_send_ref[0] = down_stage_ref[1 - core]
    down_keep_ref[0] = down_stage_ref[core]
    up_bias_ref[...] = column_sums(d_pre.astype(F32))
    acc_ref[...] += nt(d_pre, wu_ref[...])
    split_store(tn(normed_ref[...], d_pre), at_ref, up_stage_ref, up_send_ref, up_keep_ref, (0,))

    @pl.when(step == pl.num_programs(0) - 1)
    def _():
        deal_out(at_ref, y_ref, y_own_ref, y_away_ref, y_far_ref)
        total = acc_ref[...]
        unit, rate = standardize(middle_ref[...])
        dy_f = dy_ref[...].astype(F32)
        sums_ref[0:1, :] = column_sums(total * unit)
        sums_ref[1:2, :] = column_sums(total)
        d_att = (dy_f + standardize_back(total * vec_ref[MLP_GAIN], unit, rate)).astype(BF16)
        d_att_ref[...] = d_att
        sums_ref[2:3, :] = column_sums(d_att.astype(F32))
        sums_ref[3:4, :] = column_sums(dy_f)
        d_o_ref[...] = nt(d_att, wo_ref[...]).astype(BF16)
        grad = jnp.concatenate([tn(oa_ref[...], d_att), tn(ob_ref[...], d_att)], axis=0)
        store_units(grad, at_ref, out_stage_ref, out_send_ref, out_keep_ref, ())


def feed(at, x, o_a, o_b, dy_pieces, w_out, vecs, w_up, up_bias, w_down):
    length, width = x.shape
    ff = w_up.shape[1]
    part = length // 4
    strip, shard, chunk, units = width // 8, ff // 8, ff // 4, width // PAIR
    down_send = pl.BlockSpec((1, shard, width), lambda c, at: (plane_place(c ^ at[2], 1 - at[1]), 0, 0))
    down_keep = pl.BlockSpec((1, shard, width), lambda c, at: (plane_place(c ^ at[2], at[1]), 0, 0))
    up = pl.BlockSpec((4, 1, strip, chunk), lambda c, at: (0, c, 0, 0))
    cols = pl.BlockSpec((1, chunk), lambda c, at: (0, c))
    full = once((length, width))
    dy_specs, dy_arrays = piece_specs(dy_pieces, part, width)
    return call(
        feed_kernel,
        "feed",
        (4,),
        [full, once(o_a.shape), once(o_b.shape)] + dy_specs + [once((width, width)), once(vecs.shape)]
        + [
            pl.BlockSpec((width, chunk), lambda c, at: (0, c)),
            cols,
            pl.BlockSpec((chunk, width), lambda c, at: (c, 0)),
        ],
        [once((part, width)), once((2, part, width)), once((part, width)), down_send, down_keep, up, up, cols, full, full, once((8, width)), once((4, units, strip, PAIR)), once((4, units, strip, PAIR))],
        [shape((part, width)), shape((2, part, width)), shape((part, width))]
        + [shape((4, shard, width))] * 2
        + [shape((4, 4, strip, chunk))] * 2
        + [shape((1, ff), F32), shape((length, width)), shape((length, width)), shape((8, width), F32)]
        + [shape((4, units, strip, PAIR))] * 2,
        [
            pltpu.VMEM((length, width), BF16),
            pltpu.VMEM((length, width), F32),
            pltpu.VMEM((length, width), BF16),
            pltpu.VMEM((length, width), F32),
            pltpu.VMEM((length, width), F32),
            pltpu.VMEM((2, shard, width), BF16),
            pltpu.VMEM((4, 2, strip, chunk), BF16),
            pltpu.VMEM((4, 2, strip, width), BF16),
        ],
        flops=2 * length * width * (6 * ff + 3 * width),
        moved=2 * (length * width * 7 + 4 * width * ff + 3 * width * width),
    )(at, x, o_a, o_b, *dy_arrays, w_out, vecs, w_up, up_bias, w_down)


def settle_kernel(at_ref, *refs):
    out_ref = refs[-1]
    for d, ref in zip(ways(at_ref[1]), refs[:-1]):
        out_ref[at_ref[0] ^ d] = ref[...].astype(out_ref.dtype)


def settle(at, pieces, dtype, name):
    part, width = pieces[0].shape
    rows = part // 2
    specs, arrays = piece_specs(pieces, rows, width, lambda i, at: (i, 0))
    return call(
        settle_kernel,
        name,
        (2,),
        specs,
        pl.BlockSpec((4, rows, width), lambda i, at: (0, i, 0)),
        shape((4, part, width), dtype),
        moved=4 * part * width * 6,
    )(at, *arrays)


QBLOCK = 512


EPSILON = 1e-05
MASKED = -1e30


def layer_norm(inputs, norm_gain, norm_shift):
    center = inputs - jnp.mean(inputs, axis=-1, keepdims=True)
    spread = jnp.mean(center * center, axis=-1, keepdims=True)
    return center * lax.rsqrt(spread + EPSILON) * norm_gain + norm_shift


def gelu_tanh(inputs):
    return jax.nn.gelu(inputs, approximate=True)


def split_pairs(array):
    return array.reshape(array.shape[0], array.shape[1], 2, array.shape[2] // 2)


def block_scores(q_block, k_block, seg_items, mask_items, q_start, k_end, factor):
    raw = jnp.einsum("iqhc,ikhc->ihqk", q_block, k_block, preferred_element_type=jnp.float32)
    q_pos = q_start + jnp.arange(q_block.shape[1])
    k_pos = jnp.arange(k_end)
    causal = k_pos[None, :] <= q_pos[:, None]
    diagonal = k_pos[None, :] == q_pos[:, None]
    same_doc = (
        seg_items[:, q_start : q_start + q_block.shape[1], None] == seg_items[:, None, :k_end]
    )
    allowed = same_doc & causal[None] & ((mask_items[:, None, :k_end] == 1) | diagonal[None])
    return jnp.where(allowed[:, None], raw * factor, MASKED)


def spread_body(
    tokens,
    skip_values,
    segments,
    token_mask,
    attn_gain,
    attn_shift,
    w_qkv,
    q_bias,
    v_bias,
    w_out,
    out_bias,
    mlp_gain,
    mlp_shift,
    w_up,
    up_bias,
    w_down,
    down_bias,
    cotangent,
):
    rows_here, seq_here, width = tokens.shape
    pair_width = 2 * HDIM
    pair_count = width // pair_width
    fresh_pairs = pair_count // 2
    factor = float(HDIM) ** (-0.5)
    tokens_f = tokens.astype(jnp.float32)
    normed_f, first_back = jax.vjp(
        layer_norm, tokens_f, attn_gain.astype(jnp.float32), attn_shift.astype(jnp.float32)
    )
    normed = normed_f.astype(jnp.bfloat16)
    w_pairs = w_qkv.reshape(width, 2 * pair_count + fresh_pairs, pair_width)
    project = jnp.einsum("rsd,dpc->rpsc", normed, w_pairs, preferred_element_type=jnp.float32)
    queries = (
        project[:, :pair_count] + q_bias.astype(jnp.float32).reshape(1, pair_count, 1, pair_width)
    ).astype(jnp.bfloat16)
    key_rows = project[:, pair_count : 2 * pair_count].astype(jnp.bfloat16)
    fresh = (
        project[:, 2 * pair_count :]
        + v_bias.astype(jnp.float32).reshape(1, fresh_pairs, 1, pair_width)
    ).astype(jnp.bfloat16)
    reused = skip_values.reshape(rows_here, seq_here, fresh_pairs, pair_width).transpose(0, 2, 1, 3)
    value_rows = jnp.concatenate([fresh, reused], axis=1)
    flat_shape = (rows_here * pair_count, seq_here, pair_width)
    q_items, k_items, v_items = (
        lax.all_to_all(
            queries.reshape(flat_shape), "head", split_axis=0, concat_axis=1, tiled=True
        ),
        lax.all_to_all(
            key_rows.reshape(flat_shape), "head", split_axis=0, concat_axis=1, tiled=True
        ),
        lax.all_to_all(
            value_rows.reshape(flat_shape), "head", split_axis=0, concat_axis=1, tiled=True
        ),
    )
    seg_rows, mask_rows = (
        lax.all_gather(segments, "head", axis=1, tiled=True),
        lax.all_gather(token_mask, "head", axis=1, tiled=True),
    )
    item_count = q_items.shape[0]
    length = q_items.shape[1]
    item_row = (lax.axis_index("head") * item_count + jnp.arange(item_count)) // pair_count
    picker = (item_row[:, None] == jnp.arange(rows_here)[None, :]).astype(jnp.int32)
    seg_items = jnp.sum(picker[:, :, None] * seg_rows[None], axis=1)
    mask_items = jnp.sum(picker[:, :, None] * mask_rows[None], axis=1)
    q_split = split_pairs(q_items)
    k_split = split_pairs(k_items)
    v_split = split_pairs(v_items)
    block_count = length // QBLOCK
    mixed_blocks = []
    log_sums = []
    for block_id in range(block_count):
        q_start = block_id * QBLOCK
        k_end = q_start + QBLOCK
        scores = block_scores(
            q_split[:, q_start:k_end],
            k_split[:, :k_end],
            seg_items,
            mask_items,
            q_start,
            k_end,
            factor,
        )
        row_max = jnp.max(scores, axis=-1, keepdims=True)
        exp_scores = jnp.exp(scores - row_max)
        row_sum = jnp.sum(exp_scores, axis=-1, keepdims=True)
        soft_probs = (exp_scores / row_sum).astype(jnp.bfloat16)
        mixed = jnp.einsum(
            "ihqk,ikhc->iqhc", soft_probs, v_split[:, :k_end], preferred_element_type=jnp.float32
        )
        mixed_blocks.append(mixed.astype(jnp.bfloat16).reshape(item_count, QBLOCK, pair_width))
        log_sums.append(row_max + jnp.log(row_sum))
    mixed_items = jnp.concatenate(mixed_blocks, axis=1)
    mixed_rows = lax.all_to_all(
        mixed_items, "head", split_axis=1, concat_axis=0, tiled=True
    ).reshape(rows_here, pair_count, seq_here, pair_width)
    w_out_pairs = w_out.reshape(pair_count, pair_width, width)
    attended = jnp.einsum(
        "rpsc,pcd->rsd", mixed_rows, w_out_pairs, preferred_element_type=jnp.float32
    ) + out_bias.astype(jnp.float32)
    middle = tokens_f + attended
    normed_mid, second_back = jax.vjp(
        layer_norm, middle, mlp_gain.astype(jnp.float32), mlp_shift.astype(jnp.float32)
    )
    normed_two = normed_mid.astype(jnp.bfloat16)
    hidden = jnp.einsum(
        "rsd,df->rsf", normed_two, w_up, preferred_element_type=jnp.float32
    ) + up_bias.astype(jnp.float32)
    active_f, gelu_back = jax.vjp(gelu_tanh, hidden)
    active = active_f.astype(jnp.bfloat16)
    result = (
        middle
        + jnp.einsum("rsf,fd->rsd", active, w_down, preferred_element_type=jnp.float32)
        + down_bias.astype(jnp.float32)
    )
    layer_out = result.astype(jnp.bfloat16)
    g_down = jnp.einsum("rsf,rsd->fd", active, cotangent, preferred_element_type=jnp.float32)
    g_down_bias = jnp.sum(cotangent, axis=(0, 1), dtype=jnp.float32)
    d_active = jnp.einsum("rsd,fd->rsf", cotangent, w_down, preferred_element_type=jnp.float32)
    d_hidden = gelu_back(d_active)[0].astype(jnp.bfloat16)
    g_up_bias = jnp.sum(d_hidden, axis=(0, 1), dtype=jnp.float32)
    g_up = jnp.einsum("rsd,rsf->df", normed_two, d_hidden, preferred_element_type=jnp.float32)
    d_normed_two = jnp.einsum("rsf,df->rsd", d_hidden, w_up, preferred_element_type=jnp.float32)
    d_mid_norm, g_mlp_gain, g_mlp_shift = second_back(d_normed_two)
    d_middle = cotangent.astype(jnp.float32) + d_mid_norm
    d_att = d_middle.astype(jnp.bfloat16)
    g_out_bias = jnp.sum(d_att, axis=(0, 1), dtype=jnp.float32)
    g_out = jnp.einsum(
        "rpsc,rsd->pcd", mixed_rows, d_att, preferred_element_type=jnp.float32
    ).reshape(width, width)
    d_mixed = (
        jnp.einsum("rsd,pcd->rpsc", d_att, w_out_pairs, preferred_element_type=jnp.float32)
        .astype(jnp.bfloat16)
        .reshape(flat_shape)
    )
    d_items = lax.all_to_all(d_mixed, "head", split_axis=0, concat_axis=1, tiled=True)
    d_split = split_pairs(d_items)
    dk_total = jnp.zeros((item_count, length, 2, HDIM), jnp.float32)
    dv_total = jnp.zeros((item_count, length, 2, HDIM), jnp.float32)
    dq_blocks = []
    for block_id in range(block_count):
        q_start = block_id * QBLOCK
        k_end = q_start + QBLOCK
        scores = block_scores(
            q_split[:, q_start:k_end],
            k_split[:, :k_end],
            seg_items,
            mask_items,
            q_start,
            k_end,
            factor,
        )
        soft = jnp.exp(scores - log_sums[block_id])
        d_block = d_split[:, q_start:k_end]
        d_probs = jnp.einsum(
            "iqhc,ikhc->ihqk", d_block, v_split[:, :k_end], preferred_element_type=jnp.float32
        )
        delta = jnp.sum(d_probs * soft, axis=-1, keepdims=True)
        d_raw = (soft * (d_probs - delta) * factor).astype(jnp.bfloat16)
        dq_blocks.append(
            jnp.einsum(
                "ihqk,ikhc->iqhc", d_raw, k_split[:, :k_end], preferred_element_type=jnp.float32
            )
        )
        dk_total = dk_total.at[:, :k_end].add(
            jnp.einsum(
                "ihqk,iqhc->ikhc",
                d_raw,
                q_split[:, q_start:k_end],
                preferred_element_type=jnp.float32,
            )
        )
        dv_total = dv_total.at[:, :k_end].add(
            jnp.einsum(
                "ihqk,iqhc->ikhc",
                soft.astype(jnp.bfloat16),
                d_block,
                preferred_element_type=jnp.float32,
            )
        )
    item_shape = (item_count, length, pair_width)
    dq_items = jnp.concatenate(dq_blocks, axis=1).astype(jnp.bfloat16).reshape(item_shape)
    dk_items = dk_total.astype(jnp.bfloat16).reshape(item_shape)
    dv_items = dv_total.astype(jnp.bfloat16).reshape(item_shape)
    dq_rows, dk_rows, dv_rows = (
        lax.all_to_all(dq_items, "head", split_axis=1, concat_axis=0, tiled=True),
        lax.all_to_all(dk_items, "head", split_axis=1, concat_axis=0, tiled=True),
        lax.all_to_all(dv_items, "head", split_axis=1, concat_axis=0, tiled=True),
    )
    row_shape = (rows_here, pair_count, seq_here, pair_width)
    dq_rows = dq_rows.reshape(row_shape)
    dk_rows = dk_rows.reshape(row_shape)
    dv_rows = dv_rows.reshape(row_shape)
    grad_skip = (
        dv_rows[:, fresh_pairs:]
        .transpose(0, 2, 1, 3)
        .reshape(rows_here, seq_here, fresh_pairs * pair_width)
        .astype(jnp.float32)
    )
    d_project = jnp.concatenate([dq_rows, dk_rows, dv_rows[:, :fresh_pairs]], axis=1)
    g_qkv = jnp.einsum(
        "rsd,rpsc->dpc", normed, d_project, preferred_element_type=jnp.float32
    ).reshape(width, -1)
    g_q_bias = jnp.sum(dq_rows, axis=(0, 2), dtype=jnp.float32).reshape(-1)
    g_v_bias = jnp.sum(dv_rows[:, :fresh_pairs], axis=(0, 2), dtype=jnp.float32).reshape(-1)
    d_normed = jnp.einsum("rpsc,dpc->rsd", d_project, w_pairs, preferred_element_type=jnp.float32)
    d_tok_norm, g_attn_gain, g_attn_shift = first_back(d_normed)
    grad_tokens = d_middle + d_tok_norm
    small_sums = lax.psum(
        (
            g_attn_gain,
            g_attn_shift,
            g_q_bias,
            g_v_bias,
            g_out_bias,
            g_mlp_gain,
            g_mlp_shift,
            g_up_bias,
            g_down_bias,
        ),
        ("seq", "head"),
    )
    shards = (
        lax.psum_scatter(g_qkv.astype(jnp.bfloat16), "seq", scatter_dimension=0, tiled=True).astype(
            jnp.float32
        ),
        lax.psum_scatter(g_out.astype(jnp.bfloat16), "seq", scatter_dimension=0, tiled=True).astype(
            jnp.float32
        ),
        lax.psum_scatter(g_up.astype(jnp.bfloat16), "seq", scatter_dimension=0, tiled=True).astype(
            jnp.float32
        ),
        lax.psum_scatter(
            g_down.astype(jnp.bfloat16), "seq", scatter_dimension=0, tiled=True
        ).astype(jnp.float32),
    )
    reduced = (
        lax.psum(shards[0].astype(jnp.bfloat16), "head").astype(jnp.float32),
        lax.psum(shards[1].astype(jnp.bfloat16), "head").astype(jnp.float32),
        lax.psum(shards[2].astype(jnp.bfloat16), "head").astype(jnp.float32),
        lax.psum(shards[3].astype(jnp.bfloat16), "head").astype(jnp.float32),
    )
    return (
        layer_out,
        grad_tokens,
        grad_skip,
        small_sums[0],
        small_sums[1],
        reduced[0],
        small_sums[2],
        small_sums[3],
        reduced[1],
        small_sums[4],
        small_sums[5],
        small_sums[6],
        reduced[2],
        small_sums[7],
        reduced[3],
        small_sums[8],
    )


def pick(array, index):
    return lax.dynamic_index_in_dim(array, index, 0, keepdims=False)


def gate(first, second):
    return lax.optimization_barrier((first, second))


def after(value, *others):
    return lax.optimization_barrier((value, *others))[0]


def add_up(parts):
    total = parts[0].astype(F32)
    for part in parts[1:]:
        total = total + part.astype(F32)
    return total.astype(BF16)


def across_cores(array):
    return lax.ppermute(array, "seq", [(i, i ^ 1) for i in range(8)])


def group_swap(array, core_zero, core_one):
    pairs = [(4 * s + z, 4 * s + (z ^ (core_one if s & 1 else core_zero))) for s in range(8) for z in range(4)]
    return lax.ppermute(array, ("seq", "head"), pairs)


def near_swap(array):
    return group_swap(array, 1, 3)


def far_swap(array):
    return group_swap(array, 3, 1)


def across_swap(array):
    return group_swap(array, 2, 2)


def plane_swap(array, core_zero, core_one):
    return lax.ppermute(array, "seq", [(s, s ^ (core_one if s & 1 else core_zero)) for s in range(8)])


def first_hop(array):
    return plane_swap(array, 2, 4)


def second_hop(array):
    return plane_swap(array, 4, 2)


def plane_away(pairs):
    return jnp.concatenate([add_up([a[:2], b[:2]]) for a, b in pairs], axis=1)


def plane_stay(pairs):
    return jnp.concatenate([add_up([a[2:], b[2:]]) for a, b in pairs], axis=1)


def group_first(blocks, me, core):
    near, far = 1 + 2 * core, 3 - 2 * core
    take = lambda d: pick(blocks, me ^ d)
    return jnp.stack([take(near), take(2)]), jnp.stack([take(0), take(far)])


def by_owner(own, far, near, me, core):
    one, three = jnp.where(core == 0, near[0], far), jnp.where(core == 0, far, near[0])
    by_distance = [own, one, near[1], three]
    return [lax.select_n(me, *(by_distance[q ^ m] for m in range(4))) for q in range(4)]


def fits(sizes):
    return sizes == (8, 4)


def row_body(
    tokens,
    skip_values,
    segments,
    token_mask,
    attn_gain,
    attn_shift,
    w_qkv,
    q_bias,
    v_bias,
    w_out,
    out_bias,
    mlp_gain,
    mlp_shift,
    w_up,
    up_bias,
    w_down,
    down_bias,
    cotangent,
):
    me = lax.axis_index("head")
    seq = lax.axis_index("seq")
    core, plane = seq & 1, seq >> 1
    near, far = 1 + 2 * core, 3 - 2 * core
    at = jnp.stack([me, core, plane]).astype(jnp.int32)
    rows, part, width = tokens.shape
    length = rows * part
    fresh = width // 2
    ff = w_up.shape[1]
    strip = width // 8
    up_row = up_bias.astype(F32).reshape(1, ff)
    vecs = jnp.stack([attn_gain, attn_shift, out_bias, mlp_gain, mlp_shift, down_bias, down_bias, down_bias]).astype(F32)
    qkv_bias = jnp.concatenate([q_bias, jnp.zeros_like(q_bias), v_bias]).astype(F32)
    scale = jnp.where(jnp.arange(w_qkv.shape[1]) < width, Q_SCALE, 1.0).astype(F32)
    affine = jnp.stack([qkv_bias, scale])

    def forward(array, got):
        return jnp.stack([array, got[1]])

    code = (segments * 2 + token_mask).astype(BF16)
    code = jnp.broadcast_to(jnp.pad(code, ((0, 0), (0, width - part)))[:, None], (rows, CODE_ROWS, width))
    tokens_at = lambda d: jnp.concatenate([pick(tokens, me ^ d), pick(code, me ^ d)])
    pro = lambda way, piece, so_far: project(at, way, piece, vecs, w_qkv, affine, length, so_far)
    near_x = tokens_at(near)
    far_x = after(tokens_at(far), near_x)
    across_x = after(tokens_at(2), far_x)
    near_x, far_x, across_x = near_swap(near_x), far_swap(far_x), across_swap(across_x)
    so_far = pro(0, tokens_at(0), ())
    so_far = pro(1, near_x, so_far)
    so_far = pro(2, far_x, so_far)
    (across_x, so_far), (skip_values, cotangent) = gate((across_x, so_far), (skip_values, cotangent))
    skip_across = across_swap(pick(skip_values, me ^ 2))
    skip_near = near_swap(pick(skip_values, me ^ near))
    skip_far = far_swap(pick(skip_values, me ^ far))
    dy_across = across_swap(pick(cotangent, me ^ 2))
    dy_near = near_swap(pick(cotangent, me ^ near))
    x, normed, proj, code_row = pro(3, across_x, so_far)
    skip = [pick(skip_values, me), skip_near, skip_far, skip_across]

    from_a = attend(at, code_row, proj, [proj], 0, 6, 12, 3, "attend_a")
    (o_a, lse_a, skip), cotangent = gate((*from_a, skip), cotangent)
    dy_far = far_swap(pick(cotangent, me ^ far))
    o_b, lse_b = attend(at, code_row, proj, skip, 3, 9, 0, 3, "attend_b")
    dy = [pick(cotangent, me), dy_near, dy_far, dy_across]
    fed = feed(at, x, o_a, o_b, dy, w_out, vecs, w_up, up_row, w_down)
    y_own, y_away, y_far, down_send, down_keep, up_send, up_keep, g_up_bias, d_att, d_o, mlp_sums, out_send, out_keep = fed
    down_got = across_cores(down_send)
    up_got = across_cores(up_send)
    y_got = near_swap(y_away)
    out_got = across_cores(out_send)
    from_b = attend_back(
        at, code_row, proj, skip, o_b, d_o, lse_b, normed, w_qkv, 3, 3, 0, None, None, "attend_back_b"
    )
    from_b, (down_got, up_got, y_got, out_got) = gate(from_b, (down_got, up_got, y_got, out_got))
    b_send, b_keep, b_bias, s_own, s_away, s_far, d_normed = from_b
    lines = lambda v: v.reshape(4, -1, strip, width)
    big_pairs = [(up_got, up_keep), (lines(down_got), lines(down_keep))]
    big_away = plane_away(big_pairs)
    y_last = forward(y_far, y_got)
    (d_normed, s_away, b_send), (big_away, y_last) = gate((d_normed, s_away, b_send), (big_away, y_last))
    big_got = first_hop(big_away)
    y_last = far_swap(y_last)
    s_got = near_swap(s_away)
    b_got = across_cores(b_send)
    from_a = attend_back(
        at, code_row, proj, [proj], o_a, d_o, lse_a, normed, w_qkv, 0, 3, 0, d_normed,
        [x, vecs, d_att, mlp_sums, g_up_bias, b_bias], "attend_back_a"
    )
    from_a, (big_got, y_last, s_got, b_got) = gate(from_a, (big_got, y_last, s_got, b_got))
    a_send, a_keep, x_own, x_away, x_far, packed = from_a

    units = lambda v: v.reshape(4, -1, strip, PAIR)

    s_last = far_swap(forward(s_far, s_got))
    x_near = near_swap(x_away[0])
    x_far = far_swap(x_far)
    a_got = across_cores(a_send)
    big_half = add_up([big_got, plane_stay(big_pairs)])
    big_got = second_hop(big_half[0])
    layer_out = settle(at, [y_own, (y_got, 0), (y_last, 0), (y_last, 1)], BF16, "settle_out")
    (big_got, a_got, packed, x_away), (layer_out, s_last, x_near, x_far) = gate(
        (big_got, a_got, packed, x_away), (layer_out, s_last, x_near, x_far)
    )

    x_across = across_swap(x_away[1])
    grad_skip = settle(at, [s_own, (s_got, 0), (s_last, 0), (s_last, 1)], F32, "settle_skip")
    rest_pairs = [(out_got, out_keep), (units(b_got), units(b_keep)), (units(a_got), units(a_keep))]
    rest_got = first_hop(plane_away(rest_pairs))
    small_got = group_swap(packed, 1, 1)
    big = add_up([big_got, big_half[1]]).reshape(2, 4, strip, width).transpose(1, 0, 2, 3)
    big_send, big_keep = group_first(big, me, core)
    (big_send, rest_got), (x_across, small_got, grad_skip) = gate((big_send, rest_got), (x_across, small_got, grad_skip))

    big_got = near_swap(big_send)
    packed = packed + small_got
    small_got = group_swap(packed, 3, 3)
    rest_half = add_up([rest_got, plane_stay(rest_pairs)])
    rest_got = second_hop(rest_half[0])
    rest = add_up([rest_got, rest_half[1]]).reshape(-1, 4, strip // 4, PAIR).transpose(1, 0, 2, 3)
    rest_send, rest_keep = group_first(rest, me, core)
    rest_got = near_swap(rest_send)
    grad_tokens = settle(at, [x_own, x_near, x_far, x_across], F32, "settle_tokens")

    big_sum = add_up([after(big_got, rest_send, grad_tokens), big_keep])
    big_got = far_swap(big_sum[1])
    packed = packed + after(small_got, big_sum)
    small_got = across_cores(packed)
    rest_sum = add_up([after(rest_got, big_sum), rest_keep])
    rest_got = far_swap(rest_sum[1])
    big_own = add_up([after(big_got, rest_sum), big_sum[0]])
    big_far = far_swap(big_own)
    packed = packed + after(small_got, big_own)
    small_got = plane_swap(packed, 2, 2)
    rest_own = add_up([after(rest_got, big_own), rest_sum[0]])
    rest_far = far_swap(rest_own)
    big_near = near_swap(jnp.stack([big_own, after(big_far, rest_own)]))
    packed = packed + after(small_got, rest_own)
    small_got = plane_swap(packed, 4, 4)
    rest_near = near_swap(jnp.stack([rest_own, rest_far]))
    packed = (packed + small_got).reshape(-1)

    rest = jnp.concatenate(by_owner(rest_own, rest_far, rest_near, me, core), axis=1).astype(F32)
    big = by_owner(big_own, big_far, big_near, me, core)
    r_up = jnp.concatenate([q[0] for q in big], axis=1).astype(F32)
    r_down = jnp.concatenate([q[1] for q in big], axis=0).astype(F32)
    count = width // PAIR
    r_out = jnp.concatenate([rest[u] for u in range(count)], axis=1)
    unit_of = lambda p, n: rest[count + (p - count // 2) * 2 + n] if p >= count // 2 else rest[2 * count + 3 * p + n]
    order = [unit_of(p, n) for n in range(2) for p in range(count)] + [unit_of(p, 2) for p in range(count // 2)]
    r_qkv = jnp.concatenate(order, axis=1)
    sums = []
    for size in (width, width, width, fresh, width, width, width, ff, width):
        sums.append(packed[:size])
        packed = packed[size:]
    return (
        layer_out,
        grad_tokens,
        grad_skip,
        sums[0],
        sums[1],
        r_qkv,
        sums[2],
        sums[3],
        r_out,
        sums[4],
        sums[5],
        sums[6],
        r_up,
        sums[7],
        r_down,
        sums[8],
    )


def solution(mesh):
    sizes = (mesh.shape["seq"], mesh.shape["head"])
    return jax.shard_map(
        row_body if fits(sizes) else spread_body,
        mesh=mesh,
        in_specs=(
            P("seq", "head", None),
            P("seq", "head", None),
            P("seq", "head"),
            P("seq", "head"),
            P(),
            P(),
            P(),
            P(),
            P(),
            P(),
            P(),
            P(),
            P(),
            P(),
            P(),
            P(),
            P(),
            P("seq", "head", None),
        ),
        out_specs=(
            P("seq", "head", None),
            P("seq", "head", None),
            P("seq", "head", None),
            P(),
            P(),
            P("seq", None),
            P(),
            P(),
            P("seq", None),
            P(),
            P(),
            P(),
            P("seq", None),
            P(),
            P("seq", None),
            P(),
        ),
        check_vma=False,
    )
```

```python
import functools

import jax
import jax.numpy as jnp
from jax import lax
from jax.experimental import pallas as pl
from jax.experimental.pallas import tpu as pltpu
from jax.sharding import PartitionSpec as P

HDIM = 64
PAIR = 2 * HDIM
BLK = 256
LN2 = 0.6931471805599453
LOG2E = 1.4426950408889634
Q_SCALE = LOG2E * HDIM**-0.5
BF16 = jnp.bfloat16
F32 = jnp.float32
VMEM_BYTES = 56 << 20
CODE_ROWS = 16
GAIN_ROWS, Q_ROWS, V_ROWS, SUM_ROWS = 6, 12, 18, 72
ATTN_GAIN, ATTN_SHIFT, OUT_BIAS, MLP_GAIN, MLP_SHIFT, DOWN_BIAS = (slice(n, n + 1) for n in range(6))


def dot(left, right, left_dim, right_dim):
    return lax.dot_general(
        left, right, (((left_dim,), (right_dim,)), ((), ())), preferred_element_type=F32
    )


def nn(left, right):
    return dot(left, right, 1, 0)


def nt(left, right):
    return dot(left, right, 1, 1)


def tn(left, right):
    return dot(left, right, 0, 0)


def call(kernel, name, grid, in_specs, out_specs, out_shape, scratch=(), flops=0, moved=0, aliases=None):
    return pl.pallas_call(
        kernel,
        name=name,
        grid_spec=pltpu.PrefetchScalarGridSpec(
            num_scalar_prefetch=1,
            grid=grid,
            in_specs=in_specs,
            out_specs=out_specs,
            scratch_shapes=list(scratch),
        ),
        out_shape=out_shape,
        input_output_aliases=aliases or {},
        cost_estimate=pl.CostEstimate(flops=flops, bytes_accessed=moved, transcendentals=0),
        compiler_params=pltpu.CompilerParams(vmem_limit_bytes=VMEM_BYTES),
    )


def shape(dims, dtype=BF16):
    return jax.ShapeDtypeStruct(dims, dtype)


def whole(dims):
    return pl.BlockSpec(dims, lambda *_: (0,) * len(dims))


def once(dims):
    return pl.BlockSpec(dims, lambda *_: (0,) * len(dims), pipeline_mode=pl.Buffered(1))


def standardize(values):
    center = values - jnp.mean(values, axis=1, keepdims=True)
    rate = lax.rsqrt(jnp.mean(center * center, axis=1, keepdims=True) + EPSILON)
    return center * rate, rate


def standardize_back(grad, unit, rate):
    mean_grad = jnp.mean(grad, axis=1, keepdims=True)
    mean_dot = jnp.mean(grad * unit, axis=1, keepdims=True)
    return rate * (grad - mean_grad - unit * mean_dot)


def column_sums(values):
    return jnp.sum(values, axis=0, keepdims=True)


def ways(core):
    return 0, 1 + 2 * core, 3 - 2 * core, 2


def block_rows(place, d, size):
    return pl.ds(pl.multiple_of((place ^ d) * size, size), size)


def each_way(at_ref, refs):
    return [(block_rows(at_ref[0], d, ref.shape[0]), ref) for d, ref in zip(ways(at_ref[1]), refs)]


def deal_out(at_ref, source_ref, own_ref, away_ref, far_ref):
    place, part = at_ref[0], own_ref.shape[0]
    own, near, far, across = (source_ref[block_rows(place, d, part), :] for d in ways(at_ref[1]))
    own_ref[...] = own.astype(own_ref.dtype)
    away_ref[0] = near.astype(own_ref.dtype)
    away_ref[1] = across.astype(own_ref.dtype)
    far_ref[...] = far.astype(own_ref.dtype)


def piece_specs(pieces, rows, cols, at=lambda *index: (0, 0)):
    specs, arrays = [], []
    for piece in pieces:
        if isinstance(piece, tuple):
            array, number = piece
            specs.append(pl.BlockSpec((None, rows, cols), lambda *index, n=number: (n,) + at(*index)))
        else:
            array = piece
            specs.append(pl.BlockSpec((rows, cols), at))
        arrays.append(array)
    return specs, arrays


def project_kernel(at_ref, x_ref, vec_ref, w_ref, affine_ref, *refs):
    row_ref, normed_ref, proj_ref, code_ref = refs[-4:]
    part = row_ref.shape[0]
    tokens = x_ref[:part, :]
    unit, _ = standardize(tokens.astype(F32))
    normed = (unit * vec_ref[ATTN_GAIN] + vec_ref[ATTN_SHIFT]).astype(BF16)
    row_ref[...] = tokens
    normed_ref[...] = normed
    proj_ref[...] = ((nn(normed, w_ref[...]) + affine_ref[0:1, :]) * affine_ref[1:2, :]).astype(BF16)
    code_ref[...] = x_ref[part : part + CODE_ROWS, :part].astype(F32)[:8].astype(jnp.int32)


def project(at, way, piece, vecs, w, affine, length, so_far):
    part, width = length // 4, piece.shape[1]
    cols = w.shape[1]
    place = lambda at: at[0] ^ ways(at[1])[way]
    block = lambda n: pl.BlockSpec((part, n), lambda i, at: (place(at), 0))
    held = [pl.BlockSpec(memory_space=pl.ANY)] * len(so_far)
    return call(
        project_kernel,
        "project",
        (1,),
        [whole((part + CODE_ROWS, width)), whole(vecs.shape), whole((width, cols)), whole(affine.shape)] + held,
        [block(width), block(width), block(cols), pl.BlockSpec((8, part), lambda i, at: (0, place(at)))],
        [shape((length, width)), shape((length, width)), shape((length, cols)), shape((8, length), jnp.int32)],
        flops=2 * part * width * cols,
        moved=2 * (part * (3 * width + cols) + width * cols),
        aliases={5 + n: n for n in range(len(so_far))},
    )(at, piece, vecs, w, affine, *so_far)


def fill_bias(code_ref, bias_ref):
    length = code_ref.shape[1]
    code = code_ref[0:1, :]
    column = jnp.transpose(jnp.broadcast_to(code, (128, length)))
    for i in range(length // BLK):
        q_doc = column[i * BLK : (i + 1) * BLK, :1] >> 1
        for j in range(i + 1):
            k_code = code[:, j * BLK : (j + 1) * BLK]
            same = q_doc == (k_code >> 1)
            real = (k_code & 1) == 1
            if i == j:
                row_at = lax.broadcasted_iota(jnp.int32, (BLK, BLK), 0)
                col_at = lax.broadcasted_iota(jnp.int32, (BLK, BLK), 1)
                allowed = same & (col_at <= row_at) & (real | (col_at == row_at))
            else:
                allowed = same & real
            bias_ref[i * BLK : (i + 1) * BLK, j * BLK : (j + 1) * BLK] = jnp.where(allowed, 0.0, MASKED)


def halves(pair, other):
    first = lax.broadcasted_iota(jnp.int32, pair.shape, 1) < HDIM
    return jnp.where(first, pair, other), jnp.where(first, other, pair)


def gather_values(me_ref, v_refs, value_ref):
    if len(v_refs) == 1:
        return v_refs[0][...]
    for rows, ref in each_way(me_ref, v_refs):
        value_ref[rows, :] = ref[...]
    return value_ref[...]


def forward_kernel(count, me_ref, code_ref, q_ref, k_ref, *refs):
    v_refs, (o_ref, lse_ref, bias_ref, value_ref) = refs[:count], refs[count:]

    @pl.when(pl.program_id(0) == 0)
    def _():
        fill_bias(code_ref, bias_ref)

    length = q_ref.shape[0]
    v_pair = gather_values(me_ref, v_refs, value_ref)
    k_pair = k_ref[...]
    keys = halves(k_pair, jnp.zeros_like(k_pair))
    vals = halves(v_pair, jnp.ones_like(v_pair))
    first = lax.broadcasted_iota(jnp.int32, (BLK, PAIR), 1) < HDIM
    for i in range(length // BLK):
        end = (i + 1) * BLK
        rows = slice(i * BLK, end)
        q = q_ref[rows, :]
        outs, lses = [], []
        for h in range(2):
            scores = nt(q, keys[h][:end]) + bias_ref[rows, :end]
            top = jnp.max(scores, axis=1, keepdims=True)
            weights = jnp.exp2(scores - top).astype(BF16)
            mixed = nn(weights, vals[h][:end])
            total = pltpu.roll(mixed, HDIM, 1)
            outs.append(mixed / total)
            lses.append(top + jnp.log2(total))
        o_ref[rows, :] = jnp.where(first, outs[0], outs[1]).astype(BF16)
        lse_ref[rows, :] = jnp.where(first, lses[0], lses[1])


def backward_kernel(count, first_call, last_call, split, me_ref, code_ref, q_ref, k_ref, *refs):
    refs = list(refs)
    take = lambda n: [refs.pop(0) for _ in range(n)]
    v_refs = take(count)
    o_ref, do_ref, lse_ref, normed_ref = take(4)
    w_refs = take(2 if split else 3)
    before_ref = None if first_call else take(1)[0]
    if last_call:
        x_ref, vec_ref, d_att_ref, mlp_sums_ref, up_sums_ref, other_sums_ref = take(6)
    send_ref, keep_ref = take(2)
    bias_sums_ref = None if last_call else take(1)[0]
    piece_refs = take(3) if split else []
    if last_call:
        *y_refs, packed_ref = take(4)
    else:
        (after_ref,) = take(1)
    bias_ref, value_ref, dkt_ref, dvt_ref, d_ref, w_ref, acc_ref, stage_ref = refs
    step = pl.program_id(0)
    lane = lambda n: slice(n * PAIR, (n + 1) * PAIR)

    @pl.when(step == 0)
    def _():
        fill_bias(code_ref, bias_ref)
        acc_ref[...] = jnp.zeros_like(acc_ref) if first_call else before_ref[...]

    length = q_ref.shape[0]
    v_pair = gather_values(me_ref, v_refs, value_ref)
    k_pair = k_ref[...]
    zero = jnp.zeros_like(k_pair)
    keys = halves(k_pair, zero)
    vals = halves(v_pair, zero)
    first = lax.broadcasted_iota(jnp.int32, (BLK, PAIR), 1) < HDIM
    blocks = length // BLK
    for i in reversed(range(blocks)):
        end = (i + 1) * BLK
        rows = slice(i * BLK, end)
        q, do = q_ref[rows, :], do_ref[rows, :]
        q_t, do_t = jnp.transpose(q), jnp.transpose(do)
        prod = do.astype(F32) * o_ref[rows, :].astype(F32)
        dq = None
        for h in range(2):
            head = slice(h * HDIM, (h + 1) * HDIM)
            lse = lse_ref[rows, h * HDIM : h * HDIM + 1]
            mine = first if h == 0 else ~first
            delta = jnp.sum(jnp.where(mine, prod, 0.0), axis=1, keepdims=True)
            probs = jnp.exp2(nt(q, keys[h][:end]) + bias_ref[rows, :end] - lse)
            d_scores = (probs * (nt(do, vals[h][:end]) - delta)).astype(BF16)
            part = nn(d_scores, keys[h][:end])
            dq = part if dq is None else dq + part
            dv = nn(do_t[head], probs.astype(BF16))
            dk = nn(q_t[head], d_scores)
            if i == blocks - 1:
                dvt_ref[head, :] = dv
                dkt_ref[head, :] = dk
            else:
                dvt_ref[head, :end] += dv
                dkt_ref[head, :end] += dk
        d_ref[rows, lane(0)] = (dq * HDIM**-0.5).astype(BF16)
    d_ref[:, lane(1)] = jnp.transpose(dkt_ref[...] * LN2).astype(BF16)
    dv = jnp.transpose(dvt_ref[...]).astype(BF16)
    if split:
        value_ref[...] = dv
        deal_out(me_ref, value_ref, *piece_refs)
    else:
        d_ref[:, lane(2)] = dv
    for n, ref in enumerate(w_refs):
        w_ref[:, lane(n)] = ref[...]
    grad = d_ref[...]
    sums = column_sums(grad.astype(F32))
    if last_call:
        packed_ref[pl.ds(Q_ROWS + step, 1), :] = sums[:, lane(0)]
        packed_ref[pl.ds(V_ROWS + step, 1), :] = sums[:, lane(2)]
    else:
        bias_sums_ref[0] = sums
    acc_ref[...] += nt(grad, w_ref[...])
    store_units(tn(normed_ref[...], grad), me_ref, stage_ref, send_ref, keep_ref, (0,))

    @pl.when(step == pl.num_programs(0) - 1)
    def _():
        if last_call:
            total = acc_ref[...]
            unit, rate = standardize(x_ref[...].astype(F32))
            rows_of = lambda ref, row: [ref[row : row + 1, lane(n)] for n in range(ref.shape[1] // PAIR)]
            for first_row, vector in ((0, column_sums(total * unit)), (GAIN_ROWS, column_sums(total))):
                for n in range(GAIN_ROWS):
                    packed_ref[first_row + n : first_row + n + 1, :] = vector[:, lane(n)]
            others = [other_sums_ref[p, :, lane(0)] for p in range(other_sums_ref.shape[0])]
            tail_rows = rows_of(mlp_sums_ref, 2) + rows_of(mlp_sums_ref, 0) + rows_of(mlp_sums_ref, 1)
            tail_rows += rows_of(up_sums_ref, 0) + rows_of(mlp_sums_ref, 3)
            for first_row, values in ((Q_ROWS + len(others), others), (V_ROWS + len(others), tail_rows)):
                for n, value in enumerate(values):
                    packed_ref[first_row + n : first_row + n + 1, :] = value
            acc_ref[...] = d_att_ref[...].astype(F32) + standardize_back(total * vec_ref[ATTN_GAIN], unit, rate)
            deal_out(me_ref, acc_ref, *y_refs)
        else:
            after_ref[...] = acc_ref[...]


def pair_specs(length, offset):
    return pl.BlockSpec((length, PAIR), lambda p, me: (0, p + offset))


def value_specs(values, length, offset):
    if len(values) == 1:
        return [pair_specs(length, offset)], values
    return piece_specs(values, length // 4, PAIR, lambda p, me: (0, p))


def attend(me, code, proj, values, q_at, k_at, v_at, pairs, name):
    length = proj.shape[0]
    v_specs, v_arrays = value_specs(values, length, v_at)
    return call(
        functools.partial(forward_kernel, len(values)),
        name,
        (pairs,),
        [whole((8, length)), pair_specs(length, q_at), pair_specs(length, k_at)]
        + v_specs,
        [pair_specs(length, 0)] * 2,
        [shape((length, pairs * PAIR)), shape((length, pairs * PAIR), F32)],
        [pltpu.VMEM((length, length), F32), pltpu.VMEM((length, PAIR), BF16)],
        flops=pairs * 24 * length * length * PAIR,
        moved=pairs * length * PAIR * 12,
    )(me, code, proj, proj, *v_arrays)


def attend_back(at, code, proj, values, o, do, lse, normed, w, pair, pairs, o_at, before, last, name):
    length, width = normed.shape
    count = width // PAIR
    split = len(values) > 1
    units = 2 if split else 3
    cols = units * PAIR
    strip, part = width // 8, length // 4
    full = once((length, width))
    v_specs, v_arrays = value_specs(values, length, 2 * count + pair)
    w_spec = lambda offset: pl.BlockSpec((width, PAIR), lambda p, at: (0, p + offset))
    grads = pl.BlockSpec((4, 1, units, strip, PAIR), lambda p, at: (0, p, 0, 0, 0))
    in_specs = (
        [whole((8, length)), pair_specs(length, pair), pair_specs(length, count + pair)]
        + v_specs
        + [pair_specs(length, o_at), pair_specs(length, pair), pair_specs(length, o_at), full]
        + [w_spec(n * count + pair) for n in range(units)]
    )
    args = [code, proj, proj, *v_arrays, o, do, lse, normed] + [w] * units
    out_specs = [grads, grads]
    out_shape = [shape((4, pairs, units, strip, PAIR))] * 2
    if last is None:
        out_specs.append(pl.BlockSpec((1, 1, cols), lambda p, at: (p, 0, 0)))
        out_shape.append(shape((pairs, 1, cols), F32))
    if before is not None:
        in_specs.append(full)
        args.append(before)
    if last is not None:
        in_specs += [full, once(last[1].shape), full] + [once(v.shape) for v in last[3:]]
        args += last
    if split:
        one = pl.BlockSpec((part, PAIR), lambda p, at: (0, p))
        out_specs += [one, pl.BlockSpec((2, part, PAIR), lambda p, at: (0, 0, p)), one]
        out_shape += [shape((part, pairs * PAIR)), shape((2, part, pairs * PAIR)), shape((part, pairs * PAIR))]
    if last is not None:
        out_specs += [once((part, width)), once((2, part, width)), once((part, width)), once((SUM_ROWS, PAIR))]
        out_shape += [shape((part, width)), shape((2, part, width)), shape((part, width)), shape((SUM_ROWS, PAIR), F32)]
    else:
        out_specs.append(full)
        out_shape.append(shape((length, width), F32))
    return call(
        functools.partial(backward_kernel, len(values), before is None, last is not None, split),
        name,
        (pairs,),
        in_specs,
        out_specs,
        out_shape,
        [
            pltpu.VMEM((length, length), F32),
            pltpu.VMEM((length, PAIR), BF16),
            pltpu.VMEM((PAIR, length), F32),
            pltpu.VMEM((PAIR, length), F32),
            pltpu.VMEM((length, cols), BF16),
            pltpu.VMEM((width, cols), BF16),
            pltpu.VMEM((length, width), F32),
            pltpu.VMEM((4, 2, strip, cols), BF16),
        ],
        flops=pairs * (30 * length * length * PAIR + 4 * length * width * cols),
        moved=pairs * length * PAIR * 18 + 12 * length * width,
    )(at, *args)


GELU_A = 0.7978845608028654
GELU_B = 0.044715


def plane_order(core):
    return 3, 1 + core, 2 - core, 0


def plane_place(chip, core):
    return jnp.where(chip == 3, 0, jnp.where(chip == 0, 3, jnp.where(chip == 1 + core, 1, 2)))


def split_store(grad, at_ref, stage_ref, send_ref, keep_ref, lead):
    core, chip = at_ref[1], at_ref[2]
    stage_ref[...] = grad.astype(BF16).reshape(stage_ref.shape)
    for j, (theirs, mine) in enumerate(zip(plane_order(1 - core), plane_order(core))):
        send_ref[(j,) + lead] = stage_ref[chip ^ theirs, 1 - core]
        keep_ref[(j,) + lead] = stage_ref[chip ^ mine, core]


def store_units(grad, at_ref, stage_ref, send_ref, keep_ref, lead):
    core, chip = at_ref[1], at_ref[2]
    stage_ref[...] = grad.astype(BF16).reshape(stage_ref.shape)
    for u in range(stage_ref.shape[3] // PAIR):
        lanes = slice(u * PAIR, (u + 1) * PAIR)
        for j, (theirs, mine) in enumerate(zip(plane_order(1 - core), plane_order(core))):
            send_ref[(j,) + lead + (u,)] = stage_ref[chip ^ theirs, 1 - core, :, lanes]
            keep_ref[(j,) + lead + (u,)] = stage_ref[chip ^ mine, core, :, lanes]


def feed_kernel(
    at_ref, x_ref, oa_ref, ob_ref, d0_ref, d1_ref, d2_ref, d3_ref, wo_ref, vec_ref,
    wu_ref, ub_ref, wd_ref,
    y_own_ref, y_away_ref, y_far_ref, down_send_ref, down_keep_ref, up_send_ref, up_keep_ref, up_bias_ref,
    d_att_ref, d_o_ref, sums_ref, out_send_ref, out_keep_ref,
    dy_ref, middle_ref, normed_ref, y_ref, acc_ref, down_stage_ref, up_stage_ref, out_stage_ref,
):
    step = pl.program_id(0)
    core = at_ref[1]

    @pl.when(step == 0)
    def _():
        for d, ref in enumerate((d0_ref, d1_ref, d2_ref, d3_ref)):
            dy_ref[block_rows(at_ref[0], d, ref.shape[0]), :] = ref[...]
        half = oa_ref.shape[1]
        middle = (
            x_ref[...].astype(F32)
            + nn(oa_ref[...], wo_ref[:half, :])
            + nn(ob_ref[...], wo_ref[half:, :])
            + vec_ref[OUT_BIAS]
        )
        middle_ref[...] = middle
        unit, _ = standardize(middle)
        normed_ref[...] = (unit * vec_ref[MLP_GAIN] + vec_ref[MLP_SHIFT]).astype(BF16)
        y_ref[...] = middle + vec_ref[DOWN_BIAS]
        acc_ref[...] = jnp.zeros_like(acc_ref)

    dy = dy_ref[...]
    pre = nn(normed_ref[...], wu_ref[...]) + ub_ref[...]
    d_act = nt(dy, wd_ref[...])
    square = pre * pre
    curve = jnp.tanh(pre * (GELU_A + (GELU_A * GELU_B) * square))
    half_up = 0.5 + 0.5 * curve
    act = (pre * half_up).astype(BF16)
    bend = (0.5 * GELU_A) + (1.5 * GELU_A * GELU_B) * square
    d_pre = (d_act * (half_up + pre * bend * (1.0 - curve * curve))).astype(BF16)
    y_ref[...] += nn(act, wd_ref[...])
    down_stage_ref[...] = tn(act, dy).astype(BF16).reshape(down_stage_ref.shape)
    down_send_ref[0] = down_stage_ref[1 - core]
    down_keep_ref[0] = down_stage_ref[core]
    up_bias_ref[...] = column_sums(d_pre.astype(F32))
    acc_ref[...] += nt(d_pre, wu_ref[...])
    split_store(tn(normed_ref[...], d_pre), at_ref, up_stage_ref, up_send_ref, up_keep_ref, (0,))

    @pl.when(step == pl.num_programs(0) - 1)
    def _():
        deal_out(at_ref, y_ref, y_own_ref, y_away_ref, y_far_ref)
        total = acc_ref[...]
        unit, rate = standardize(middle_ref[...])
        dy_f = dy_ref[...].astype(F32)
        sums_ref[0:1, :] = column_sums(total * unit)
        sums_ref[1:2, :] = column_sums(total)
        d_att = (dy_f + standardize_back(total * vec_ref[MLP_GAIN], unit, rate)).astype(BF16)
        d_att_ref[...] = d_att
        sums_ref[2:3, :] = column_sums(d_att.astype(F32))
        sums_ref[3:4, :] = column_sums(dy_f)
        d_o_ref[...] = nt(d_att, wo_ref[...]).astype(BF16)
        grad = jnp.concatenate([tn(oa_ref[...], d_att), tn(ob_ref[...], d_att)], axis=0)
        store_units(grad, at_ref, out_stage_ref, out_send_ref, out_keep_ref, ())


def feed(at, x, o_a, o_b, dy_pieces, w_out, vecs, w_up, up_bias, w_down):
    length, width = x.shape
    ff = w_up.shape[1]
    part = length // 4
    strip, shard, chunk, units = width // 8, ff // 8, ff // 4, width // PAIR
    down_send = pl.BlockSpec((1, shard, width), lambda c, at: (plane_place(c ^ at[2], 1 - at[1]), 0, 0))
    down_keep = pl.BlockSpec((1, shard, width), lambda c, at: (plane_place(c ^ at[2], at[1]), 0, 0))
    up = pl.BlockSpec((4, 1, strip, chunk), lambda c, at: (0, c, 0, 0))
    cols = pl.BlockSpec((1, chunk), lambda c, at: (0, c))
    full = once((length, width))
    dy_specs, dy_arrays = piece_specs(dy_pieces, part, width)
    return call(
        feed_kernel,
        "feed",
        (4,),
        [full, once(o_a.shape), once(o_b.shape)] + dy_specs + [once((width, width)), once(vecs.shape)]
        + [
            pl.BlockSpec((width, chunk), lambda c, at: (0, c)),
            cols,
            pl.BlockSpec((chunk, width), lambda c, at: (c, 0)),
        ],
        [once((part, width)), once((2, part, width)), once((part, width)), down_send, down_keep, up, up, cols, full, full, once((8, width)), once((4, units, strip, PAIR)), once((4, units, strip, PAIR))],
        [shape((part, width)), shape((2, part, width)), shape((part, width))]
        + [shape((4, shard, width))] * 2
        + [shape((4, 4, strip, chunk))] * 2
        + [shape((1, ff), F32), shape((length, width)), shape((length, width)), shape((8, width), F32)]
        + [shape((4, units, strip, PAIR))] * 2,
        [
            pltpu.VMEM((length, width), BF16),
            pltpu.VMEM((length, width), F32),
            pltpu.VMEM((length, width), BF16),
            pltpu.VMEM((length, width), F32),
            pltpu.VMEM((length, width), F32),
            pltpu.VMEM((2, shard, width), BF16),
            pltpu.VMEM((4, 2, strip, chunk), BF16),
            pltpu.VMEM((4, 2, strip, width), BF16),
        ],
        flops=2 * length * width * (6 * ff + 3 * width),
        moved=2 * (length * width * 7 + 4 * width * ff + 3 * width * width),
    )(at, x, o_a, o_b, *dy_arrays, w_out, vecs, w_up, up_bias, w_down)


def settle_kernel(at_ref, *refs):
    out_ref = refs[-1]
    for d, ref in zip(ways(at_ref[1]), refs[:-1]):
        out_ref[at_ref[0] ^ d] = ref[...].astype(out_ref.dtype)


def settle(at, pieces, dtype, name):
    part, width = pieces[0].shape
    rows = part // 2
    specs, arrays = piece_specs(pieces, rows, width, lambda i, at: (i, 0))
    return call(
        settle_kernel,
        name,
        (2,),
        specs,
        pl.BlockSpec((4, rows, width), lambda i, at: (0, i, 0)),
        shape((4, part, width), dtype),
        moved=4 * part * width * 6,
    )(at, *arrays)


QBLOCK = 512


EPSILON = 1e-05
MASKED = -1e30


def layer_norm(inputs, norm_gain, norm_shift):
    center = inputs - jnp.mean(inputs, axis=-1, keepdims=True)
    spread = jnp.mean(center * center, axis=-1, keepdims=True)
    return center * lax.rsqrt(spread + EPSILON) * norm_gain + norm_shift


def gelu_tanh(inputs):
    return jax.nn.gelu(inputs, approximate=True)


def split_pairs(array):
    return array.reshape(array.shape[0], array.shape[1], 2, array.shape[2] // 2)


def block_scores(q_block, k_block, seg_items, mask_items, q_start, k_end, factor):
    raw = jnp.einsum("iqhc,ikhc->ihqk", q_block, k_block, preferred_element_type=jnp.float32)
    q_pos = q_start + jnp.arange(q_block.shape[1])
    k_pos = jnp.arange(k_end)
    causal = k_pos[None, :] <= q_pos[:, None]
    diagonal = k_pos[None, :] == q_pos[:, None]
    same_doc = (
        seg_items[:, q_start : q_start + q_block.shape[1], None] == seg_items[:, None, :k_end]
    )
    allowed = same_doc & causal[None] & ((mask_items[:, None, :k_end] == 1) | diagonal[None])
    return jnp.where(allowed[:, None], raw * factor, MASKED)


def spread_body(
    tokens,
    skip_values,
    segments,
    token_mask,
    attn_gain,
    attn_shift,
    w_qkv,
    q_bias,
    v_bias,
    w_out,
    out_bias,
    mlp_gain,
    mlp_shift,
    w_up,
    up_bias,
    w_down,
    down_bias,
    cotangent,
):
    rows_here, seq_here, width = tokens.shape
    pair_width = 2 * HDIM
    pair_count = width // pair_width
    fresh_pairs = pair_count // 2
    factor = float(HDIM) ** (-0.5)
    tokens_f = tokens.astype(jnp.float32)
    normed_f, first_back = jax.vjp(
        layer_norm, tokens_f, attn_gain.astype(jnp.float32), attn_shift.astype(jnp.float32)
    )
    normed = normed_f.astype(jnp.bfloat16)
    w_pairs = w_qkv.reshape(width, 2 * pair_count + fresh_pairs, pair_width)
    project = jnp.einsum("rsd,dpc->rpsc", normed, w_pairs, preferred_element_type=jnp.float32)
    queries = (
        project[:, :pair_count] + q_bias.astype(jnp.float32).reshape(1, pair_count, 1, pair_width)
    ).astype(jnp.bfloat16)
    key_rows = project[:, pair_count : 2 * pair_count].astype(jnp.bfloat16)
    fresh = (
        project[:, 2 * pair_count :]
        + v_bias.astype(jnp.float32).reshape(1, fresh_pairs, 1, pair_width)
    ).astype(jnp.bfloat16)
    reused = skip_values.reshape(rows_here, seq_here, fresh_pairs, pair_width).transpose(0, 2, 1, 3)
    value_rows = jnp.concatenate([fresh, reused], axis=1)
    flat_shape = (rows_here * pair_count, seq_here, pair_width)
    q_items, k_items, v_items = (
        lax.all_to_all(
            queries.reshape(flat_shape), "head", split_axis=0, concat_axis=1, tiled=True
        ),
        lax.all_to_all(
            key_rows.reshape(flat_shape), "head", split_axis=0, concat_axis=1, tiled=True
        ),
        lax.all_to_all(
            value_rows.reshape(flat_shape), "head", split_axis=0, concat_axis=1, tiled=True
        ),
    )
    seg_rows, mask_rows = (
        lax.all_gather(segments, "head", axis=1, tiled=True),
        lax.all_gather(token_mask, "head", axis=1, tiled=True),
    )
    item_count = q_items.shape[0]
    length = q_items.shape[1]
    item_row = (lax.axis_index("head") * item_count + jnp.arange(item_count)) // pair_count
    picker = (item_row[:, None] == jnp.arange(rows_here)[None, :]).astype(jnp.int32)
    seg_items = jnp.sum(picker[:, :, None] * seg_rows[None], axis=1)
    mask_items = jnp.sum(picker[:, :, None] * mask_rows[None], axis=1)
    q_split = split_pairs(q_items)
    k_split = split_pairs(k_items)
    v_split = split_pairs(v_items)
    block_count = length // QBLOCK
    mixed_blocks = []
    log_sums = []
    for block_id in range(block_count):
        q_start = block_id * QBLOCK
        k_end = q_start + QBLOCK
        scores = block_scores(
            q_split[:, q_start:k_end],
            k_split[:, :k_end],
            seg_items,
            mask_items,
            q_start,
            k_end,
            factor,
        )
        row_max = jnp.max(scores, axis=-1, keepdims=True)
        exp_scores = jnp.exp(scores - row_max)
        row_sum = jnp.sum(exp_scores, axis=-1, keepdims=True)
        soft_probs = (exp_scores / row_sum).astype(jnp.bfloat16)
        mixed = jnp.einsum(
            "ihqk,ikhc->iqhc", soft_probs, v_split[:, :k_end], preferred_element_type=jnp.float32
        )
        mixed_blocks.append(mixed.astype(jnp.bfloat16).reshape(item_count, QBLOCK, pair_width))
        log_sums.append(row_max + jnp.log(row_sum))
    mixed_items = jnp.concatenate(mixed_blocks, axis=1)
    mixed_rows = lax.all_to_all(
        mixed_items, "head", split_axis=1, concat_axis=0, tiled=True
    ).reshape(rows_here, pair_count, seq_here, pair_width)
    w_out_pairs = w_out.reshape(pair_count, pair_width, width)
    attended = jnp.einsum(
        "rpsc,pcd->rsd", mixed_rows, w_out_pairs, preferred_element_type=jnp.float32
    ) + out_bias.astype(jnp.float32)
    middle = tokens_f + attended
    normed_mid, second_back = jax.vjp(
        layer_norm, middle, mlp_gain.astype(jnp.float32), mlp_shift.astype(jnp.float32)
    )
    normed_two = normed_mid.astype(jnp.bfloat16)
    hidden = jnp.einsum(
        "rsd,df->rsf", normed_two, w_up, preferred_element_type=jnp.float32
    ) + up_bias.astype(jnp.float32)
    active_f, gelu_back = jax.vjp(gelu_tanh, hidden)
    active = active_f.astype(jnp.bfloat16)
    result = (
        middle
        + jnp.einsum("rsf,fd->rsd", active, w_down, preferred_element_type=jnp.float32)
        + down_bias.astype(jnp.float32)
    )
    layer_out = result.astype(jnp.bfloat16)
    g_down = jnp.einsum("rsf,rsd->fd", active, cotangent, preferred_element_type=jnp.float32)
    g_down_bias = jnp.sum(cotangent, axis=(0, 1), dtype=jnp.float32)
    d_active = jnp.einsum("rsd,fd->rsf", cotangent, w_down, preferred_element_type=jnp.float32)
    d_hidden = gelu_back(d_active)[0].astype(jnp.bfloat16)
    g_up_bias = jnp.sum(d_hidden, axis=(0, 1), dtype=jnp.float32)
    g_up = jnp.einsum("rsd,rsf->df", normed_two, d_hidden, preferred_element_type=jnp.float32)
    d_normed_two = jnp.einsum("rsf,df->rsd", d_hidden, w_up, preferred_element_type=jnp.float32)
    d_mid_norm, g_mlp_gain, g_mlp_shift = second_back(d_normed_two)
    d_middle = cotangent.astype(jnp.float32) + d_mid_norm
    d_att = d_middle.astype(jnp.bfloat16)
    g_out_bias = jnp.sum(d_att, axis=(0, 1), dtype=jnp.float32)
    g_out = jnp.einsum(
        "rpsc,rsd->pcd", mixed_rows, d_att, preferred_element_type=jnp.float32
    ).reshape(width, width)
    d_mixed = (
        jnp.einsum("rsd,pcd->rpsc", d_att, w_out_pairs, preferred_element_type=jnp.float32)
        .astype(jnp.bfloat16)
        .reshape(flat_shape)
    )
    d_items = lax.all_to_all(d_mixed, "head", split_axis=0, concat_axis=1, tiled=True)
    d_split = split_pairs(d_items)
    dk_total = jnp.zeros((item_count, length, 2, HDIM), jnp.float32)
    dv_total = jnp.zeros((item_count, length, 2, HDIM), jnp.float32)
    dq_blocks = []
    for block_id in range(block_count):
        q_start = block_id * QBLOCK
        k_end = q_start + QBLOCK
        scores = block_scores(
            q_split[:, q_start:k_end],
            k_split[:, :k_end],
            seg_items,
            mask_items,
            q_start,
            k_end,
            factor,
        )
        soft = jnp.exp(scores - log_sums[block_id])
        d_block = d_split[:, q_start:k_end]
        d_probs = jnp.einsum(
            "iqhc,ikhc->ihqk", d_block, v_split[:, :k_end], preferred_element_type=jnp.float32
        )
        delta = jnp.sum(d_probs * soft, axis=-1, keepdims=True)
        d_raw = (soft * (d_probs - delta) * factor).astype(jnp.bfloat16)
        dq_blocks.append(
            jnp.einsum(
                "ihqk,ikhc->iqhc", d_raw, k_split[:, :k_end], preferred_element_type=jnp.float32
            )
        )
        dk_total = dk_total.at[:, :k_end].add(
            jnp.einsum(
                "ihqk,iqhc->ikhc",
                d_raw,
                q_split[:, q_start:k_end],
                preferred_element_type=jnp.float32,
            )
        )
        dv_total = dv_total.at[:, :k_end].add(
            jnp.einsum(
                "ihqk,iqhc->ikhc",
                soft.astype(jnp.bfloat16),
                d_block,
                preferred_element_type=jnp.float32,
            )
        )
    item_shape = (item_count, length, pair_width)
    dq_items = jnp.concatenate(dq_blocks, axis=1).astype(jnp.bfloat16).reshape(item_shape)
    dk_items = dk_total.astype(jnp.bfloat16).reshape(item_shape)
    dv_items = dv_total.astype(jnp.bfloat16).reshape(item_shape)
    dq_rows, dk_rows, dv_rows = (
        lax.all_to_all(dq_items, "head", split_axis=1, concat_axis=0, tiled=True),
        lax.all_to_all(dk_items, "head", split_axis=1, concat_axis=0, tiled=True),
        lax.all_to_all(dv_items, "head", split_axis=1, concat_axis=0, tiled=True),
    )
    row_shape = (rows_here, pair_count, seq_here, pair_width)
    dq_rows = dq_rows.reshape(row_shape)
    dk_rows = dk_rows.reshape(row_shape)
    dv_rows = dv_rows.reshape(row_shape)
    grad_skip = (
        dv_rows[:, fresh_pairs:]
        .transpose(0, 2, 1, 3)
        .reshape(rows_here, seq_here, fresh_pairs * pair_width)
        .astype(jnp.float32)
    )
    d_project = jnp.concatenate([dq_rows, dk_rows, dv_rows[:, :fresh_pairs]], axis=1)
    g_qkv = jnp.einsum(
        "rsd,rpsc->dpc", normed, d_project, preferred_element_type=jnp.float32
    ).reshape(width, -1)
    g_q_bias = jnp.sum(dq_rows, axis=(0, 2), dtype=jnp.float32).reshape(-1)
    g_v_bias = jnp.sum(dv_rows[:, :fresh_pairs], axis=(0, 2), dtype=jnp.float32).reshape(-1)
    d_normed = jnp.einsum("rpsc,dpc->rsd", d_project, w_pairs, preferred_element_type=jnp.float32)
    d_tok_norm, g_attn_gain, g_attn_shift = first_back(d_normed)
    grad_tokens = d_middle + d_tok_norm
    small_sums = lax.psum(
        (
            g_attn_gain,
            g_attn_shift,
            g_q_bias,
            g_v_bias,
            g_out_bias,
            g_mlp_gain,
            g_mlp_shift,
            g_up_bias,
            g_down_bias,
        ),
        ("seq", "head"),
    )
    shards = (
        lax.psum_scatter(g_qkv.astype(jnp.bfloat16), "seq", scatter_dimension=0, tiled=True).astype(
            jnp.float32
        ),
        lax.psum_scatter(g_out.astype(jnp.bfloat16), "seq", scatter_dimension=0, tiled=True).astype(
            jnp.float32
        ),
        lax.psum_scatter(g_up.astype(jnp.bfloat16), "seq", scatter_dimension=0, tiled=True).astype(
            jnp.float32
        ),
        lax.psum_scatter(
            g_down.astype(jnp.bfloat16), "seq", scatter_dimension=0, tiled=True
        ).astype(jnp.float32),
    )
    reduced = (
        lax.psum(shards[0].astype(jnp.bfloat16), "head").astype(jnp.float32),
        lax.psum(shards[1].astype(jnp.bfloat16), "head").astype(jnp.float32),
        lax.psum(shards[2].astype(jnp.bfloat16), "head").astype(jnp.float32),
        lax.psum(shards[3].astype(jnp.bfloat16), "head").astype(jnp.float32),
    )
    return (
        layer_out,
        grad_tokens,
        grad_skip,
        small_sums[0],
        small_sums[1],
        reduced[0],
        small_sums[2],
        small_sums[3],
        reduced[1],
        small_sums[4],
        small_sums[5],
        small_sums[6],
        reduced[2],
        small_sums[7],
        reduced[3],
        small_sums[8],
    )


def pick(array, index):
    return lax.dynamic_index_in_dim(array, index, 0, keepdims=False)


def gate(first, second):
    return lax.optimization_barrier((first, second))


def after(value, *others):
    return lax.optimization_barrier((value, *others))[0]


def add_up(parts):
    total = parts[0].astype(F32)
    for part in parts[1:]:
        total = total + part.astype(F32)
    return total.astype(BF16)


def across_cores(array):
    return lax.ppermute(array, "seq", [(i, i ^ 1) for i in range(8)])


def group_swap(array, core_zero, core_one):
    pairs = [(4 * s + z, 4 * s + (z ^ (core_one if s & 1 else core_zero))) for s in range(8) for z in range(4)]
    return lax.ppermute(array, ("seq", "head"), pairs)


def near_swap(array):
    return group_swap(array, 1, 3)


def far_swap(array):
    return group_swap(array, 3, 1)


def across_swap(array):
    return group_swap(array, 2, 2)


def plane_swap(array, core_zero, core_one):
    return lax.ppermute(array, "seq", [(s, s ^ (core_one if s & 1 else core_zero)) for s in range(8)])


def first_hop(array):
    return plane_swap(array, 2, 4)


def second_hop(array):
    return plane_swap(array, 4, 2)


def plane_away(pairs):
    return jnp.concatenate([add_up([a[:2], b[:2]]) for a, b in pairs], axis=1)


def plane_stay(pairs):
    return jnp.concatenate([add_up([a[2:], b[2:]]) for a, b in pairs], axis=1)


def group_first(blocks, me, core):
    near, far = 1 + 2 * core, 3 - 2 * core
    take = lambda d: pick(blocks, me ^ d)
    return jnp.stack([take(near), take(2)]), jnp.stack([take(0), take(far)])


def by_owner(own, far, near, me, core):
    one, three = jnp.where(core == 0, near[0], far), jnp.where(core == 0, far, near[0])
    by_distance = [own, one, near[1], three]
    return [lax.select_n(me, *(by_distance[q ^ m] for m in range(4))) for q in range(4)]


def fits(sizes):
    return sizes == (8, 4)


def row_body(
    tokens,
    skip_values,
    segments,
    token_mask,
    attn_gain,
    attn_shift,
    w_qkv,
    q_bias,
    v_bias,
    w_out,
    out_bias,
    mlp_gain,
    mlp_shift,
    w_up,
    up_bias,
    w_down,
    down_bias,
    cotangent,
):
    me = lax.axis_index("head")
    seq = lax.axis_index("seq")
    core, plane = seq & 1, seq >> 1
    near, far = 1 + 2 * core, 3 - 2 * core
    at = jnp.stack([me, core, plane]).astype(jnp.int32)
    rows, part, width = tokens.shape
    length = rows * part
    fresh = width // 2
    ff = w_up.shape[1]
    strip = width // 8
    up_row = up_bias.astype(F32).reshape(1, ff)
    vecs = jnp.stack([attn_gain, attn_shift, out_bias, mlp_gain, mlp_shift, down_bias, down_bias, down_bias]).astype(F32)
    qkv_bias = jnp.concatenate([q_bias, jnp.zeros_like(q_bias), v_bias]).astype(F32)
    scale = jnp.where(jnp.arange(w_qkv.shape[1]) < width, Q_SCALE, 1.0).astype(F32)
    affine = jnp.stack([qkv_bias, scale])

    def forward(array, got):
        return jnp.stack([array, got[1]])

    code = (segments * 2 + token_mask).astype(BF16)
    code = jnp.broadcast_to(jnp.pad(code, ((0, 0), (0, width - part)))[:, None], (rows, CODE_ROWS, width))
    tokens_at = lambda d: jnp.concatenate([pick(tokens, me ^ d), pick(code, me ^ d)])
    pro = lambda way, piece, so_far: project(at, way, piece, vecs, w_qkv, affine, length, so_far)
    near_x = tokens_at(near)
    far_x = after(tokens_at(far), near_x)
    across_x = after(tokens_at(2), far_x)
    near_x, far_x, across_x = near_swap(near_x), far_swap(far_x), across_swap(across_x)
    so_far = pro(0, tokens_at(0), ())
    so_far = pro(1, near_x, so_far)
    so_far = pro(2, far_x, so_far)
    (across_x, so_far), (skip_values, cotangent) = gate((across_x, so_far), (skip_values, cotangent))
    skip_across = across_swap(pick(skip_values, me ^ 2))
    skip_near = near_swap(pick(skip_values, me ^ near))
    skip_far = far_swap(pick(skip_values, me ^ far))
    dy_across = across_swap(pick(cotangent, me ^ 2))
    dy_three = group_swap(pick(cotangent, me ^ 3), 3, 3)
    x, normed, proj, code_row = pro(3, across_x, so_far)
    skip = [pick(skip_values, me), skip_near, skip_far, skip_across]

    from_a = attend(at, code_row, proj, [proj], 0, 6, 12, 3, "attend_a")
    (o_a, lse_a, skip), cotangent = gate((*from_a, skip), cotangent)
    dy_one = group_swap(pick(cotangent, me ^ 1), 1, 1)
    o_b, lse_b = attend(at, code_row, proj, skip, 3, 9, 0, 3, "attend_b")
    dy = [pick(cotangent, me), dy_one, dy_across, dy_three]
    fed = feed(at, x, o_a, o_b, dy, w_out, vecs, w_up, up_row, w_down)
    y_own, y_away, y_far, down_send, down_keep, up_send, up_keep, g_up_bias, d_att, d_o, mlp_sums, out_send, out_keep = fed
    down_got = across_cores(down_send)
    up_got = across_cores(up_send)
    y_got = near_swap(y_away)
    out_got = across_cores(out_send)
    from_b = attend_back(
        at, code_row, proj, skip, o_b, d_o, lse_b, normed, w_qkv, 3, 3, 0, None, None, "attend_back_b"
    )
    from_b, (down_got, up_got, y_got, out_got) = gate(from_b, (down_got, up_got, y_got, out_got))
    b_send, b_keep, b_bias, s_own, s_away, s_far, d_normed = from_b
    lines = lambda v: v.reshape(4, -1, strip, width)
    big_pairs = [(up_got, up_keep), (lines(down_got), lines(down_keep))]
    big_away = plane_away(big_pairs)
    y_last = forward(y_far, y_got)
    (d_normed, s_away, b_send), (big_away, y_last) = gate((d_normed, s_away, b_send), (big_away, y_last))
    big_got = first_hop(big_away)
    y_last = far_swap(y_last)
    s_got = near_swap(s_away)
    b_got = across_cores(b_send)
    from_a = attend_back(
        at, code_row, proj, [proj], o_a, d_o, lse_a, normed, w_qkv, 0, 3, 0, d_normed,
        [x, vecs, d_att, mlp_sums, g_up_bias, b_bias], "attend_back_a"
    )
    from_a, (big_got, y_last, s_got, b_got) = gate(from_a, (big_got, y_last, s_got, b_got))
    a_send, a_keep, x_own, x_away, x_far, packed = from_a

    units = lambda v: v.reshape(4, -1, strip, PAIR)

    s_last = far_swap(forward(s_far, s_got))
    x_near = near_swap(x_away[0])
    x_far = far_swap(x_far)
    a_got = across_cores(a_send)
    big_half = add_up([big_got, plane_stay(big_pairs)])
    big_got = second_hop(big_half[0])
    layer_out = settle(at, [y_own, (y_got, 0), (y_last, 0), (y_last, 1)], BF16, "settle_out")
    (big_got, a_got, packed, x_away), (layer_out, s_last, x_near, x_far) = gate(
        (big_got, a_got, packed, x_away), (layer_out, s_last, x_near, x_far)
    )

    x_across = across_swap(x_away[1])
    grad_skip = settle(at, [s_own, (s_got, 0), (s_last, 0), (s_last, 1)], F32, "settle_skip")
    rest_pairs = [(out_got, out_keep), (units(b_got), units(b_keep)), (units(a_got), units(a_keep))]
    rest_got = first_hop(plane_away(rest_pairs))
    small_got = group_swap(packed, 1, 1)
    big = add_up([big_got, big_half[1]]).reshape(2, 4, strip, width).transpose(1, 0, 2, 3)
    big_send, big_keep = group_first(big, me, core)
    big_got = near_swap(big_send)
    (rest_got, packed), (small_got, grad_skip) = gate((rest_got, packed), (small_got, grad_skip))

    packed = packed + small_got
    small_got = group_swap(packed, 3, 3)
    rest_half = add_up([rest_got, plane_stay(rest_pairs)])
    rest_got = second_hop(rest_half[0])
    (rest_got, big_got), (x_across, small_got) = gate((rest_got, big_got), (x_across, small_got))
    rest = add_up([rest_got, rest_half[1]]).reshape(-1, 4, strip // 4, PAIR).transpose(1, 0, 2, 3)
    rest_send, rest_keep = group_first(rest, me, core)
    rest_got = near_swap(rest_send)
    grad_tokens = settle(at, [x_own, x_near, x_far, x_across], F32, "settle_tokens")

    big_sum = add_up([big_got, big_keep])
    big_got = far_swap(big_sum[1])
    packed = packed + after(small_got, big_sum)
    small_got = across_cores(packed)
    rest_sum = add_up([after(rest_got, big_sum, grad_tokens), rest_keep])
    rest_got = far_swap(rest_sum[1])
    big_own = add_up([after(big_got, rest_sum), big_sum[0]])
    big_far = far_swap(big_own)
    packed = packed + after(small_got, big_own)
    small_got = plane_swap(packed, 2, 2)
    rest_own = add_up([after(rest_got, big_own), rest_sum[0]])
    rest_far = far_swap(rest_own)
    big_far = jnp.stack([big_own, big_far])
    big_near = near_swap(big_far)
    packed = packed + after(small_got, rest_own)
    small_got = plane_swap(packed, 4, 4)
    rest_near = near_swap(jnp.stack([rest_own, after(rest_far, big_far)]))
    packed = (packed + small_got).reshape(-1)

    rest = jnp.concatenate(by_owner(rest_own, rest_far, rest_near, me, core), axis=1).astype(F32)
    big = by_owner(big_own, big_far[1], big_near, me, core)
    r_up = jnp.concatenate([q[0] for q in big], axis=1).astype(F32)
    r_down = jnp.concatenate([q[1] for q in big], axis=0).astype(F32)
    count = width // PAIR
    r_out = jnp.concatenate([rest[u] for u in range(count)], axis=1)
    unit_of = lambda p, n: rest[count + (p - count // 2) * 2 + n] if p >= count // 2 else rest[2 * count + 3 * p + n]
    order = [unit_of(p, n) for n in range(2) for p in range(count)] + [unit_of(p, 2) for p in range(count // 2)]
    r_qkv = jnp.concatenate(order, axis=1)
    sums = []
    for size in (width, width, width, fresh, width, width, width, ff, width):
        sums.append(packed[:size])
        packed = packed[size:]
    return (
        layer_out,
        grad_tokens,
        grad_skip,
        sums[0],
        sums[1],
        r_qkv,
        sums[2],
        sums[3],
        r_out,
        sums[4],
        sums[5],
        sums[6],
        r_up,
        sums[7],
        r_down,
        sums[8],
    )


def solution(mesh):
    sizes = (mesh.shape["seq"], mesh.shape["head"])
    return jax.shard_map(
        row_body if fits(sizes) else spread_body,
        mesh=mesh,
        in_specs=(
            P("seq", "head", None),
            P("seq", "head", None),
            P("seq", "head"),
            P("seq", "head"),
            P(),
            P(),
            P(),
            P(),
            P(),
            P(),
            P(),
            P(),
            P(),
            P(),
            P(),
            P(),
            P(),
            P("seq", "head", None),
        ),
        out_specs=(
            P("seq", "head", None),
            P("seq", "head", None),
            P("seq", "head", None),
            P(),
            P(),
            P("seq", None),
            P(),
            P(),
            P("seq", None),
            P(),
            P(),
            P(),
            P("seq", None),
            P(),
            P("seq", None),
            P(),
        ),
        check_vma=False,
    )
```

```python
import functools

import jax
import jax.numpy as jnp
from jax import lax
from jax.experimental import pallas as pl
from jax.experimental.pallas import tpu as pltpu
from jax.sharding import PartitionSpec as P

HDIM = 64
PAIR = 2 * HDIM
BLK = 256
LN2 = 0.6931471805599453
LOG2E = 1.4426950408889634
Q_SCALE = LOG2E * HDIM**-0.5
BF16 = jnp.bfloat16
F32 = jnp.float32
VMEM_BYTES = 56 << 20
CODE_ROWS = 16
GAIN_ROWS, Q_ROWS, V_ROWS, SUM_ROWS = 6, 12, 18, 72
ATTN_GAIN, ATTN_SHIFT, OUT_BIAS, MLP_GAIN, MLP_SHIFT, DOWN_BIAS = (slice(n, n + 1) for n in range(6))


def dot(left, right, left_dim, right_dim):
    return lax.dot_general(
        left, right, (((left_dim,), (right_dim,)), ((), ())), preferred_element_type=F32
    )


def nn(left, right):
    return dot(left, right, 1, 0)


def nt(left, right):
    return dot(left, right, 1, 1)


def tn(left, right):
    return dot(left, right, 0, 0)


def call(kernel, name, grid, in_specs, out_specs, out_shape, scratch=(), flops=0, moved=0, aliases=None):
    return pl.pallas_call(
        kernel,
        name=name,
        grid_spec=pltpu.PrefetchScalarGridSpec(
            num_scalar_prefetch=1,
            grid=grid,
            in_specs=in_specs,
            out_specs=out_specs,
            scratch_shapes=list(scratch),
        ),
        out_shape=out_shape,
        input_output_aliases=aliases or {},
        cost_estimate=pl.CostEstimate(flops=flops, bytes_accessed=moved, transcendentals=0),
        compiler_params=pltpu.CompilerParams(vmem_limit_bytes=VMEM_BYTES),
    )


def shape(dims, dtype=BF16):
    return jax.ShapeDtypeStruct(dims, dtype)


def whole(dims):
    return pl.BlockSpec(dims, lambda *_: (0,) * len(dims))


def once(dims):
    return pl.BlockSpec(dims, lambda *_: (0,) * len(dims), pipeline_mode=pl.Buffered(1))


def standardize(values):
    center = values - jnp.mean(values, axis=1, keepdims=True)
    rate = lax.rsqrt(jnp.mean(center * center, axis=1, keepdims=True) + EPSILON)
    return center * rate, rate


def standardize_back(grad, unit, rate):
    mean_grad = jnp.mean(grad, axis=1, keepdims=True)
    mean_dot = jnp.mean(grad * unit, axis=1, keepdims=True)
    return rate * (grad - mean_grad - unit * mean_dot)


def column_sums(values):
    return jnp.sum(values, axis=0, keepdims=True)


def ways(core):
    return 0, 1 + 2 * core, 3 - 2 * core, 2


def block_rows(place, d, size):
    return pl.ds(pl.multiple_of((place ^ d) * size, size), size)


def each_way(at_ref, refs):
    return [(block_rows(at_ref[0], d, ref.shape[0]), ref) for d, ref in zip(ways(at_ref[1]), refs)]


def deal_out(at_ref, source_ref, own_ref, away_ref, far_ref):
    place, part = at_ref[0], own_ref.shape[0]
    own, near, far, across = (source_ref[block_rows(place, d, part), :] for d in ways(at_ref[1]))
    own_ref[...] = own.astype(own_ref.dtype)
    away_ref[0] = near.astype(own_ref.dtype)
    away_ref[1] = across.astype(own_ref.dtype)
    far_ref[...] = far.astype(own_ref.dtype)


def piece_specs(pieces, rows, cols, at=lambda *index: (0, 0)):
    specs, arrays = [], []
    for piece in pieces:
        if isinstance(piece, tuple):
            array, number = piece
            specs.append(pl.BlockSpec((None, rows, cols), lambda *index, n=number: (n,) + at(*index)))
        else:
            array = piece
            specs.append(pl.BlockSpec((rows, cols), at))
        arrays.append(array)
    return specs, arrays


def project_kernel(at_ref, x_ref, vec_ref, w_ref, affine_ref, *refs):
    row_ref, normed_ref, proj_ref, code_ref = refs[-4:]
    part = row_ref.shape[0]
    tokens = x_ref[:part, :]
    unit, _ = standardize(tokens.astype(F32))
    normed = (unit * vec_ref[ATTN_GAIN] + vec_ref[ATTN_SHIFT]).astype(BF16)
    row_ref[...] = tokens
    normed_ref[...] = normed
    proj_ref[...] = ((nn(normed, w_ref[...]) + affine_ref[0:1, :]) * affine_ref[1:2, :]).astype(BF16)
    code_ref[...] = x_ref[part : part + CODE_ROWS, :part].astype(F32)[:8].astype(jnp.int32)


def project(at, way, piece, vecs, w, affine, length, so_far):
    part, width = length // 4, piece.shape[1]
    cols = w.shape[1]
    place = lambda at: at[0] ^ ways(at[1])[way]
    block = lambda n: pl.BlockSpec((part, n), lambda i, at: (place(at), 0))
    held = [pl.BlockSpec(memory_space=pl.ANY)] * len(so_far)
    return call(
        project_kernel,
        "project",
        (1,),
        [whole((part + CODE_ROWS, width)), whole(vecs.shape), whole((width, cols)), whole(affine.shape)] + held,
        [block(width), block(width), block(cols), pl.BlockSpec((8, part), lambda i, at: (0, place(at)))],
        [shape((length, width)), shape((length, width)), shape((length, cols)), shape((8, length), jnp.int32)],
        flops=2 * part * width * cols,
        moved=2 * (part * (3 * width + cols) + width * cols),
        aliases={5 + n: n for n in range(len(so_far))},
    )(at, piece, vecs, w, affine, *so_far)


def fill_bias(code_ref, bias_ref):
    length = code_ref.shape[1]
    code = code_ref[0:1, :]
    column = jnp.transpose(jnp.broadcast_to(code, (128, length)))
    for i in range(length // BLK):
        q_doc = column[i * BLK : (i + 1) * BLK, :1] >> 1
        for j in range(i + 1):
            k_code = code[:, j * BLK : (j + 1) * BLK]
            same = q_doc == (k_code >> 1)
            real = (k_code & 1) == 1
            if i == j:
                row_at = lax.broadcasted_iota(jnp.int32, (BLK, BLK), 0)
                col_at = lax.broadcasted_iota(jnp.int32, (BLK, BLK), 1)
                allowed = same & (col_at <= row_at) & (real | (col_at == row_at))
            else:
                allowed = same & real
            bias_ref[i * BLK : (i + 1) * BLK, j * BLK : (j + 1) * BLK] = jnp.where(allowed, 0.0, MASKED)


def halves(pair, other):
    first = lax.broadcasted_iota(jnp.int32, pair.shape, 1) < HDIM
    return jnp.where(first, pair, other), jnp.where(first, other, pair)


def gather_values(me_ref, v_refs, value_ref):
    if len(v_refs) == 1:
        return v_refs[0][...]
    for rows, ref in each_way(me_ref, v_refs):
        value_ref[rows, :] = ref[...]
    return value_ref[...]


def forward_kernel(count, me_ref, code_ref, q_ref, k_ref, *refs):
    v_refs, (o_ref, lse_ref, bias_ref, value_ref) = refs[:count], refs[count:]

    @pl.when(pl.program_id(0) == 0)
    def _():
        fill_bias(code_ref, bias_ref)

    length = q_ref.shape[0]
    v_pair = gather_values(me_ref, v_refs, value_ref)
    k_pair = k_ref[...]
    keys = halves(k_pair, jnp.zeros_like(k_pair))
    vals = halves(v_pair, jnp.ones_like(v_pair))
    first = lax.broadcasted_iota(jnp.int32, (BLK, PAIR), 1) < HDIM
    for i in range(length // BLK):
        end = (i + 1) * BLK
        rows = slice(i * BLK, end)
        q = q_ref[rows, :]
        outs, lses = [], []
        for h in range(2):
            scores = nt(q, keys[h][:end]) + bias_ref[rows, :end]
            top = jnp.max(scores, axis=1, keepdims=True)
            weights = jnp.exp2(scores - top).astype(BF16)
            mixed = nn(weights, vals[h][:end])
            total = pltpu.roll(mixed, HDIM, 1)
            outs.append(mixed / total)
            lses.append(top + jnp.log2(total))
        o_ref[rows, :] = jnp.where(first, outs[0], outs[1]).astype(BF16)
        lse_ref[rows, :] = jnp.where(first, lses[0], lses[1])


def backward_kernel(count, first_call, last_call, split, me_ref, code_ref, q_ref, k_ref, *refs):
    refs = list(refs)
    take = lambda n: [refs.pop(0) for _ in range(n)]
    v_refs = take(count)
    o_ref, do_ref, lse_ref, normed_ref = take(4)
    w_refs = take(2 if split else 3)
    before_ref = None if first_call else take(1)[0]
    if last_call:
        x_ref, vec_ref, d_att_ref, mlp_sums_ref, up_sums_ref, other_sums_ref = take(6)
    send_ref, keep_ref = take(2)
    bias_sums_ref = None if last_call else take(1)[0]
    piece_refs = take(3) if split else []
    if last_call:
        *y_refs, packed_ref = take(4)
    else:
        (after_ref,) = take(1)
    bias_ref, value_ref, dkt_ref, dvt_ref, d_ref, w_ref, stage_ref = refs[:7]
    acc_ref = refs[7] if last_call else after_ref
    step = pl.program_id(0)
    lane = lambda n: slice(n * PAIR, (n + 1) * PAIR)

    @pl.when(step == 0)
    def _():
        fill_bias(code_ref, bias_ref)
        if not first_call:
            acc_ref[...] = before_ref[...]

    length = q_ref.shape[0]
    v_pair = gather_values(me_ref, v_refs, value_ref)
    k_pair = k_ref[...]
    zero = jnp.zeros_like(k_pair)
    keys = halves(k_pair, zero)
    vals = halves(v_pair, zero)
    first = lax.broadcasted_iota(jnp.int32, (BLK, PAIR), 1) < HDIM
    blocks = length // BLK
    for i in reversed(range(blocks)):
        end = (i + 1) * BLK
        rows = slice(i * BLK, end)
        q, do = q_ref[rows, :], do_ref[rows, :]
        q_t, do_t = jnp.transpose(q), jnp.transpose(do)
        prod = do.astype(F32) * o_ref[rows, :].astype(F32)
        dq = None
        for h in range(2):
            head = slice(h * HDIM, (h + 1) * HDIM)
            lse = lse_ref[rows, h * HDIM : h * HDIM + 1]
            mine = first if h == 0 else ~first
            delta = jnp.sum(jnp.where(mine, prod, 0.0), axis=1, keepdims=True)
            probs = jnp.exp2(nt(q, keys[h][:end]) + bias_ref[rows, :end] - lse)
            d_scores = (probs * (nt(do, vals[h][:end]) - delta)).astype(BF16)
            part = nn(d_scores, keys[h][:end])
            dq = part if dq is None else dq + part
            dv = nn(do_t[head], probs.astype(BF16))
            dk = nn(q_t[head], d_scores)
            if i == blocks - 1:
                dvt_ref[head, :] = dv
                dkt_ref[head, :] = dk
            else:
                dvt_ref[head, :end] += dv
                dkt_ref[head, :end] += dk
        d_ref[rows, lane(0)] = (dq * HDIM**-0.5).astype(BF16)
    d_ref[:, lane(1)] = jnp.transpose(dkt_ref[...] * LN2).astype(BF16)
    dv = jnp.transpose(dvt_ref[...]).astype(BF16)
    if split:
        value_ref[...] = dv
        deal_out(me_ref, value_ref, *piece_refs)
    else:
        d_ref[:, lane(2)] = dv
    for n, ref in enumerate(w_refs):
        w_ref[:, lane(n)] = ref[...]
    grad = d_ref[...]
    sums = column_sums(grad.astype(F32))
    if last_call:
        packed_ref[pl.ds(Q_ROWS + step, 1), :] = sums[:, lane(0)]
        packed_ref[pl.ds(V_ROWS + step, 1), :] = sums[:, lane(2)]
    else:
        bias_sums_ref[0] = sums
    share = nt(grad, w_ref[...])
    if first_call:

        @pl.when(step == 0)
        def _():
            acc_ref[...] = share

        @pl.when(step > 0)
        def _():
            acc_ref[...] += share

    else:
        acc_ref[...] += share
    store_units(tn(normed_ref[...], grad), me_ref, stage_ref, send_ref, keep_ref, (0,))

    @pl.when(step == pl.num_programs(0) - 1)
    def _():
        if last_call:
            total = acc_ref[...]
            unit, rate = standardize(x_ref[...].astype(F32))
            rows_of = lambda ref, row: [ref[row : row + 1, lane(n)] for n in range(ref.shape[1] // PAIR)]
            for first_row, vector in ((0, column_sums(total * unit)), (GAIN_ROWS, column_sums(total))):
                for n in range(GAIN_ROWS):
                    packed_ref[first_row + n : first_row + n + 1, :] = vector[:, lane(n)]
            others = [other_sums_ref[p, :, lane(0)] for p in range(other_sums_ref.shape[0])]
            tail_rows = rows_of(mlp_sums_ref, 2) + rows_of(mlp_sums_ref, 0) + rows_of(mlp_sums_ref, 1)
            tail_rows += rows_of(up_sums_ref, 0) + rows_of(mlp_sums_ref, 3)
            for first_row, values in ((Q_ROWS + len(others), others), (V_ROWS + len(others), tail_rows)):
                for n, value in enumerate(values):
                    packed_ref[first_row + n : first_row + n + 1, :] = value
            acc_ref[...] = d_att_ref[...].astype(F32) + standardize_back(total * vec_ref[ATTN_GAIN], unit, rate)
            deal_out(me_ref, acc_ref, *y_refs)


def pair_specs(length, offset):
    return pl.BlockSpec((length, PAIR), lambda p, me: (0, p + offset))


def value_specs(values, length, offset):
    if len(values) == 1:
        return [pair_specs(length, offset)], values
    return piece_specs(values, length // 4, PAIR, lambda p, me: (0, p))


def attend(me, code, proj, values, q_at, k_at, v_at, pairs, name):
    length = proj.shape[0]
    v_specs, v_arrays = value_specs(values, length, v_at)
    return call(
        functools.partial(forward_kernel, len(values)),
        name,
        (pairs,),
        [whole((8, length)), pair_specs(length, q_at), pair_specs(length, k_at)]
        + v_specs,
        [pair_specs(length, 0)] * 2,
        [shape((length, pairs * PAIR)), shape((length, pairs * PAIR), F32)],
        [pltpu.VMEM((length, length), F32), pltpu.VMEM((length, PAIR), BF16)],
        flops=pairs * 24 * length * length * PAIR,
        moved=pairs * length * PAIR * 12,
    )(me, code, proj, proj, *v_arrays)


def attend_back(at, code, proj, values, o, do, lse, normed, w, pair, pairs, o_at, before, last, name):
    length, width = normed.shape
    count = width // PAIR
    split = len(values) > 1
    units = 2 if split else 3
    cols = units * PAIR
    strip, part = width // 8, length // 4
    full = once((length, width))
    v_specs, v_arrays = value_specs(values, length, 2 * count + pair)
    w_spec = lambda offset: pl.BlockSpec((width, PAIR), lambda p, at: (0, p + offset))
    grads = pl.BlockSpec((4, 1, units, strip, PAIR), lambda p, at: (0, p, 0, 0, 0))
    in_specs = (
        [whole((8, length)), pair_specs(length, pair), pair_specs(length, count + pair)]
        + v_specs
        + [pair_specs(length, o_at), pair_specs(length, pair), pair_specs(length, o_at), full]
        + [w_spec(n * count + pair) for n in range(units)]
    )
    args = [code, proj, proj, *v_arrays, o, do, lse, normed] + [w] * units
    out_specs = [grads, grads]
    out_shape = [shape((4, pairs, units, strip, PAIR))] * 2
    if last is None:
        out_specs.append(pl.BlockSpec((1, 1, cols), lambda p, at: (p, 0, 0)))
        out_shape.append(shape((pairs, 1, cols), F32))
    if before is not None:
        in_specs.append(full)
        args.append(before)
    if last is not None:
        in_specs += [full, once(last[1].shape), full] + [once(v.shape) for v in last[3:]]
        args += last
    if split:
        one = pl.BlockSpec((part, PAIR), lambda p, at: (0, p))
        out_specs += [one, pl.BlockSpec((2, part, PAIR), lambda p, at: (0, 0, p)), one]
        out_shape += [shape((part, pairs * PAIR)), shape((2, part, pairs * PAIR)), shape((part, pairs * PAIR))]
    if last is not None:
        out_specs += [once((part, width)), once((2, part, width)), once((part, width)), once((SUM_ROWS, PAIR))]
        out_shape += [shape((part, width)), shape((2, part, width)), shape((part, width)), shape((SUM_ROWS, PAIR), F32)]
    else:
        out_specs.append(full)
        out_shape.append(shape((length, width), F32))
    return call(
        functools.partial(backward_kernel, len(values), before is None, last is not None, split),
        name,
        (pairs,),
        in_specs,
        out_specs,
        out_shape,
        [
            pltpu.VMEM((length, length), F32),
            pltpu.VMEM((length, PAIR), BF16),
            pltpu.VMEM((PAIR, length), F32),
            pltpu.VMEM((PAIR, length), F32),
            pltpu.VMEM((length, cols), BF16),
            pltpu.VMEM((width, cols), BF16),
            pltpu.VMEM((4, 2, strip, cols), BF16),
        ]
        + ([] if last is None else [pltpu.VMEM((length, width), F32)]),
        flops=pairs * (30 * length * length * PAIR + 4 * length * width * cols),
        moved=pairs * length * PAIR * 18 + 12 * length * width,
    )(at, *args)


GELU_A = 0.7978845608028654
GELU_B = 0.044715


def plane_order(core):
    return 3, 1 + core, 2 - core, 0


def plane_place(chip, core):
    return jnp.where(chip == 3, 0, jnp.where(chip == 0, 3, jnp.where(chip == 1 + core, 1, 2)))


def split_store(grad, at_ref, stage_ref, send_ref, keep_ref, lead):
    core, chip = at_ref[1], at_ref[2]
    stage_ref[...] = grad.astype(BF16).reshape(stage_ref.shape)
    for j, (theirs, mine) in enumerate(zip(plane_order(1 - core), plane_order(core))):
        send_ref[(j,) + lead] = stage_ref[chip ^ theirs, 1 - core]
        keep_ref[(j,) + lead] = stage_ref[chip ^ mine, core]


def store_units(grad, at_ref, stage_ref, send_ref, keep_ref, lead):
    core, chip = at_ref[1], at_ref[2]
    stage_ref[...] = grad.astype(BF16).reshape(stage_ref.shape)
    for u in range(stage_ref.shape[3] // PAIR):
        lanes = slice(u * PAIR, (u + 1) * PAIR)
        for j, (theirs, mine) in enumerate(zip(plane_order(1 - core), plane_order(core))):
            send_ref[(j,) + lead + (u,)] = stage_ref[chip ^ theirs, 1 - core, :, lanes]
            keep_ref[(j,) + lead + (u,)] = stage_ref[chip ^ mine, core, :, lanes]


def feed_kernel(
    at_ref, x_ref, oa_ref, ob_ref, d0_ref, d1_ref, d2_ref, d3_ref, wo_ref, vec_ref,
    wu_ref, ub_ref, wd_ref,
    y_own_ref, y_away_ref, y_far_ref, down_send_ref, down_keep_ref, up_send_ref, up_keep_ref, up_bias_ref,
    d_att_ref, d_o_ref, sums_ref, out_send_ref, out_keep_ref,
    dy_ref, middle_ref, normed_ref, y_ref, acc_ref, down_stage_ref, up_stage_ref, out_stage_ref,
):
    step = pl.program_id(0)
    core = at_ref[1]

    @pl.when(step == 0)
    def _():
        for d, ref in enumerate((d0_ref, d1_ref, d2_ref, d3_ref)):
            dy_ref[block_rows(at_ref[0], d, ref.shape[0]), :] = ref[...]
        half = oa_ref.shape[1]
        middle = (
            x_ref[...].astype(F32)
            + nn(oa_ref[...], wo_ref[:half, :])
            + nn(ob_ref[...], wo_ref[half:, :])
            + vec_ref[OUT_BIAS]
        )
        middle_ref[...] = middle
        unit, _ = standardize(middle)
        normed_ref[...] = (unit * vec_ref[MLP_GAIN] + vec_ref[MLP_SHIFT]).astype(BF16)
        y_ref[...] = middle + vec_ref[DOWN_BIAS]
        acc_ref[...] = jnp.zeros_like(acc_ref)

    dy = dy_ref[...]
    pre = nn(normed_ref[...], wu_ref[...]) + ub_ref[...]
    d_act = nt(dy, wd_ref[...])
    square = pre * pre
    curve = jnp.tanh(pre * (GELU_A + (GELU_A * GELU_B) * square))
    half_up = 0.5 + 0.5 * curve
    act = (pre * half_up).astype(BF16)
    bend = (0.5 * GELU_A) + (1.5 * GELU_A * GELU_B) * square
    d_pre = (d_act * (half_up + pre * bend * (1.0 - curve * curve))).astype(BF16)
    y_ref[...] += nn(act, wd_ref[...])
    down_stage_ref[...] = tn(act, dy).astype(BF16).reshape(down_stage_ref.shape)
    down_send_ref[0] = down_stage_ref[1 - core]
    down_keep_ref[0] = down_stage_ref[core]
    up_bias_ref[...] = column_sums(d_pre.astype(F32))
    acc_ref[...] += nt(d_pre, wu_ref[...])
    split_store(tn(normed_ref[...], d_pre), at_ref, up_stage_ref, up_send_ref, up_keep_ref, (0,))

    @pl.when(step == pl.num_programs(0) - 1)
    def _():
        deal_out(at_ref, y_ref, y_own_ref, y_away_ref, y_far_ref)
        total = acc_ref[...]
        unit, rate = standardize(middle_ref[...])
        dy_f = dy_ref[...].astype(F32)
        sums_ref[0:1, :] = column_sums(total * unit)
        sums_ref[1:2, :] = column_sums(total)
        d_att = (dy_f + standardize_back(total * vec_ref[MLP_GAIN], unit, rate)).astype(BF16)
        d_att_ref[...] = d_att
        sums_ref[2:3, :] = column_sums(d_att.astype(F32))
        sums_ref[3:4, :] = column_sums(dy_f)
        d_o_ref[...] = nt(d_att, wo_ref[...]).astype(BF16)
        grad = jnp.concatenate([tn(oa_ref[...], d_att), tn(ob_ref[...], d_att)], axis=0)
        store_units(grad, at_ref, out_stage_ref, out_send_ref, out_keep_ref, ())


def feed(at, x, o_a, o_b, dy_pieces, w_out, vecs, w_up, up_bias, w_down):
    length, width = x.shape
    ff = w_up.shape[1]
    part = length // 4
    strip, shard, chunk, units = width // 8, ff // 8, ff // 4, width // PAIR
    down_send = pl.BlockSpec((1, shard, width), lambda c, at: (plane_place(c ^ at[2], 1 - at[1]), 0, 0))
    down_keep = pl.BlockSpec((1, shard, width), lambda c, at: (plane_place(c ^ at[2], at[1]), 0, 0))
    up = pl.BlockSpec((4, 1, strip, chunk), lambda c, at: (0, c, 0, 0))
    cols = pl.BlockSpec((1, chunk), lambda c, at: (0, c))
    full = once((length, width))
    dy_specs, dy_arrays = piece_specs(dy_pieces, part, width)
    return call(
        feed_kernel,
        "feed",
        (4,),
        [full, once(o_a.shape), once(o_b.shape)] + dy_specs + [once((width, width)), once(vecs.shape)]
        + [
            pl.BlockSpec((width, chunk), lambda c, at: (0, c)),
            cols,
            pl.BlockSpec((chunk, width), lambda c, at: (c, 0)),
        ],
        [once((part, width)), once((2, part, width)), once((part, width)), down_send, down_keep, up, up, cols, full, full, once((8, width)), once((4, units, strip, PAIR)), once((4, units, strip, PAIR))],
        [shape((part, width)), shape((2, part, width)), shape((part, width))]
        + [shape((4, shard, width))] * 2
        + [shape((4, 4, strip, chunk))] * 2
        + [shape((1, ff), F32), shape((length, width)), shape((length, width)), shape((8, width), F32)]
        + [shape((4, units, strip, PAIR))] * 2,
        [
            pltpu.VMEM((length, width), BF16),
            pltpu.VMEM((length, width), F32),
            pltpu.VMEM((length, width), BF16),
            pltpu.VMEM((length, width), F32),
            pltpu.VMEM((length, width), F32),
            pltpu.VMEM((2, shard, width), BF16),
            pltpu.VMEM((4, 2, strip, chunk), BF16),
            pltpu.VMEM((4, 2, strip, width), BF16),
        ],
        flops=2 * length * width * (6 * ff + 3 * width),
        moved=2 * (length * width * 7 + 4 * width * ff + 3 * width * width),
    )(at, x, o_a, o_b, *dy_arrays, w_out, vecs, w_up, up_bias, w_down)


def settle_kernel(at_ref, *refs):
    out_ref = refs[-1]
    for d, ref in zip(ways(at_ref[1]), refs[:-1]):
        out_ref[at_ref[0] ^ d] = ref[...].astype(out_ref.dtype)


def settle(at, pieces, dtype, name):
    part, width = pieces[0].shape
    rows = part // 2
    specs, arrays = piece_specs(pieces, rows, width, lambda i, at: (i, 0))
    return call(
        settle_kernel,
        name,
        (2,),
        specs,
        pl.BlockSpec((4, rows, width), lambda i, at: (0, i, 0)),
        shape((4, part, width), dtype),
        moved=4 * part * width * 6,
    )(at, *arrays)


QBLOCK = 512


EPSILON = 1e-05
MASKED = -1e30


def layer_norm(inputs, norm_gain, norm_shift):
    center = inputs - jnp.mean(inputs, axis=-1, keepdims=True)
    spread = jnp.mean(center * center, axis=-1, keepdims=True)
    return center * lax.rsqrt(spread + EPSILON) * norm_gain + norm_shift


def gelu_tanh(inputs):
    return jax.nn.gelu(inputs, approximate=True)


def split_pairs(array):
    return array.reshape(array.shape[0], array.shape[1], 2, array.shape[2] // 2)


def block_scores(q_block, k_block, seg_items, mask_items, q_start, k_end, factor):
    raw = jnp.einsum("iqhc,ikhc->ihqk", q_block, k_block, preferred_element_type=jnp.float32)
    q_pos = q_start + jnp.arange(q_block.shape[1])
    k_pos = jnp.arange(k_end)
    causal = k_pos[None, :] <= q_pos[:, None]
    diagonal = k_pos[None, :] == q_pos[:, None]
    same_doc = (
        seg_items[:, q_start : q_start + q_block.shape[1], None] == seg_items[:, None, :k_end]
    )
    allowed = same_doc & causal[None] & ((mask_items[:, None, :k_end] == 1) | diagonal[None])
    return jnp.where(allowed[:, None], raw * factor, MASKED)


def spread_body(
    tokens,
    skip_values,
    segments,
    token_mask,
    attn_gain,
    attn_shift,
    w_qkv,
    q_bias,
    v_bias,
    w_out,
    out_bias,
    mlp_gain,
    mlp_shift,
    w_up,
    up_bias,
    w_down,
    down_bias,
    cotangent,
):
    rows_here, seq_here, width = tokens.shape
    pair_width = 2 * HDIM
    pair_count = width // pair_width
    fresh_pairs = pair_count // 2
    factor = float(HDIM) ** (-0.5)
    tokens_f = tokens.astype(jnp.float32)
    normed_f, first_back = jax.vjp(
        layer_norm, tokens_f, attn_gain.astype(jnp.float32), attn_shift.astype(jnp.float32)
    )
    normed = normed_f.astype(jnp.bfloat16)
    w_pairs = w_qkv.reshape(width, 2 * pair_count + fresh_pairs, pair_width)
    project = jnp.einsum("rsd,dpc->rpsc", normed, w_pairs, preferred_element_type=jnp.float32)
    queries = (
        project[:, :pair_count] + q_bias.astype(jnp.float32).reshape(1, pair_count, 1, pair_width)
    ).astype(jnp.bfloat16)
    key_rows = project[:, pair_count : 2 * pair_count].astype(jnp.bfloat16)
    fresh = (
        project[:, 2 * pair_count :]
        + v_bias.astype(jnp.float32).reshape(1, fresh_pairs, 1, pair_width)
    ).astype(jnp.bfloat16)
    reused = skip_values.reshape(rows_here, seq_here, fresh_pairs, pair_width).transpose(0, 2, 1, 3)
    value_rows = jnp.concatenate([fresh, reused], axis=1)
    flat_shape = (rows_here * pair_count, seq_here, pair_width)
    q_items, k_items, v_items = (
        lax.all_to_all(
            queries.reshape(flat_shape), "head", split_axis=0, concat_axis=1, tiled=True
        ),
        lax.all_to_all(
            key_rows.reshape(flat_shape), "head", split_axis=0, concat_axis=1, tiled=True
        ),
        lax.all_to_all(
            value_rows.reshape(flat_shape), "head", split_axis=0, concat_axis=1, tiled=True
        ),
    )
    seg_rows, mask_rows = (
        lax.all_gather(segments, "head", axis=1, tiled=True),
        lax.all_gather(token_mask, "head", axis=1, tiled=True),
    )
    item_count = q_items.shape[0]
    length = q_items.shape[1]
    item_row = (lax.axis_index("head") * item_count + jnp.arange(item_count)) // pair_count
    picker = (item_row[:, None] == jnp.arange(rows_here)[None, :]).astype(jnp.int32)
    seg_items = jnp.sum(picker[:, :, None] * seg_rows[None], axis=1)
    mask_items = jnp.sum(picker[:, :, None] * mask_rows[None], axis=1)
    q_split = split_pairs(q_items)
    k_split = split_pairs(k_items)
    v_split = split_pairs(v_items)
    block_count = length // QBLOCK
    mixed_blocks = []
    log_sums = []
    for block_id in range(block_count):
        q_start = block_id * QBLOCK
        k_end = q_start + QBLOCK
        scores = block_scores(
            q_split[:, q_start:k_end],
            k_split[:, :k_end],
            seg_items,
            mask_items,
            q_start,
            k_end,
            factor,
        )
        row_max = jnp.max(scores, axis=-1, keepdims=True)
        exp_scores = jnp.exp(scores - row_max)
        row_sum = jnp.sum(exp_scores, axis=-1, keepdims=True)
        soft_probs = (exp_scores / row_sum).astype(jnp.bfloat16)
        mixed = jnp.einsum(
            "ihqk,ikhc->iqhc", soft_probs, v_split[:, :k_end], preferred_element_type=jnp.float32
        )
        mixed_blocks.append(mixed.astype(jnp.bfloat16).reshape(item_count, QBLOCK, pair_width))
        log_sums.append(row_max + jnp.log(row_sum))
    mixed_items = jnp.concatenate(mixed_blocks, axis=1)
    mixed_rows = lax.all_to_all(
        mixed_items, "head", split_axis=1, concat_axis=0, tiled=True
    ).reshape(rows_here, pair_count, seq_here, pair_width)
    w_out_pairs = w_out.reshape(pair_count, pair_width, width)
    attended = jnp.einsum(
        "rpsc,pcd->rsd", mixed_rows, w_out_pairs, preferred_element_type=jnp.float32
    ) + out_bias.astype(jnp.float32)
    middle = tokens_f + attended
    normed_mid, second_back = jax.vjp(
        layer_norm, middle, mlp_gain.astype(jnp.float32), mlp_shift.astype(jnp.float32)
    )
    normed_two = normed_mid.astype(jnp.bfloat16)
    hidden = jnp.einsum(
        "rsd,df->rsf", normed_two, w_up, preferred_element_type=jnp.float32
    ) + up_bias.astype(jnp.float32)
    active_f, gelu_back = jax.vjp(gelu_tanh, hidden)
    active = active_f.astype(jnp.bfloat16)
    result = (
        middle
        + jnp.einsum("rsf,fd->rsd", active, w_down, preferred_element_type=jnp.float32)
        + down_bias.astype(jnp.float32)
    )
    layer_out = result.astype(jnp.bfloat16)
    g_down = jnp.einsum("rsf,rsd->fd", active, cotangent, preferred_element_type=jnp.float32)
    g_down_bias = jnp.sum(cotangent, axis=(0, 1), dtype=jnp.float32)
    d_active = jnp.einsum("rsd,fd->rsf", cotangent, w_down, preferred_element_type=jnp.float32)
    d_hidden = gelu_back(d_active)[0].astype(jnp.bfloat16)
    g_up_bias = jnp.sum(d_hidden, axis=(0, 1), dtype=jnp.float32)
    g_up = jnp.einsum("rsd,rsf->df", normed_two, d_hidden, preferred_element_type=jnp.float32)
    d_normed_two = jnp.einsum("rsf,df->rsd", d_hidden, w_up, preferred_element_type=jnp.float32)
    d_mid_norm, g_mlp_gain, g_mlp_shift = second_back(d_normed_two)
    d_middle = cotangent.astype(jnp.float32) + d_mid_norm
    d_att = d_middle.astype(jnp.bfloat16)
    g_out_bias = jnp.sum(d_att, axis=(0, 1), dtype=jnp.float32)
    g_out = jnp.einsum(
        "rpsc,rsd->pcd", mixed_rows, d_att, preferred_element_type=jnp.float32
    ).reshape(width, width)
    d_mixed = (
        jnp.einsum("rsd,pcd->rpsc", d_att, w_out_pairs, preferred_element_type=jnp.float32)
        .astype(jnp.bfloat16)
        .reshape(flat_shape)
    )
    d_items = lax.all_to_all(d_mixed, "head", split_axis=0, concat_axis=1, tiled=True)
    d_split = split_pairs(d_items)
    dk_total = jnp.zeros((item_count, length, 2, HDIM), jnp.float32)
    dv_total = jnp.zeros((item_count, length, 2, HDIM), jnp.float32)
    dq_blocks = []
    for block_id in range(block_count):
        q_start = block_id * QBLOCK
        k_end = q_start + QBLOCK
        scores = block_scores(
            q_split[:, q_start:k_end],
            k_split[:, :k_end],
            seg_items,
            mask_items,
            q_start,
            k_end,
            factor,
        )
        soft = jnp.exp(scores - log_sums[block_id])
        d_block = d_split[:, q_start:k_end]
        d_probs = jnp.einsum(
            "iqhc,ikhc->ihqk", d_block, v_split[:, :k_end], preferred_element_type=jnp.float32
        )
        delta = jnp.sum(d_probs * soft, axis=-1, keepdims=True)
        d_raw = (soft * (d_probs - delta) * factor).astype(jnp.bfloat16)
        dq_blocks.append(
            jnp.einsum(
                "ihqk,ikhc->iqhc", d_raw, k_split[:, :k_end], preferred_element_type=jnp.float32
            )
        )
        dk_total = dk_total.at[:, :k_end].add(
            jnp.einsum(
                "ihqk,iqhc->ikhc",
                d_raw,
                q_split[:, q_start:k_end],
                preferred_element_type=jnp.float32,
            )
        )
        dv_total = dv_total.at[:, :k_end].add(
            jnp.einsum(
                "ihqk,iqhc->ikhc",
                soft.astype(jnp.bfloat16),
                d_block,
                preferred_element_type=jnp.float32,
            )
        )
    item_shape = (item_count, length, pair_width)
    dq_items = jnp.concatenate(dq_blocks, axis=1).astype(jnp.bfloat16).reshape(item_shape)
    dk_items = dk_total.astype(jnp.bfloat16).reshape(item_shape)
    dv_items = dv_total.astype(jnp.bfloat16).reshape(item_shape)
    dq_rows, dk_rows, dv_rows = (
        lax.all_to_all(dq_items, "head", split_axis=1, concat_axis=0, tiled=True),
        lax.all_to_all(dk_items, "head", split_axis=1, concat_axis=0, tiled=True),
        lax.all_to_all(dv_items, "head", split_axis=1, concat_axis=0, tiled=True),
    )
    row_shape = (rows_here, pair_count, seq_here, pair_width)
    dq_rows = dq_rows.reshape(row_shape)
    dk_rows = dk_rows.reshape(row_shape)
    dv_rows = dv_rows.reshape(row_shape)
    grad_skip = (
        dv_rows[:, fresh_pairs:]
        .transpose(0, 2, 1, 3)
        .reshape(rows_here, seq_here, fresh_pairs * pair_width)
        .astype(jnp.float32)
    )
    d_project = jnp.concatenate([dq_rows, dk_rows, dv_rows[:, :fresh_pairs]], axis=1)
    g_qkv = jnp.einsum(
        "rsd,rpsc->dpc", normed, d_project, preferred_element_type=jnp.float32
    ).reshape(width, -1)
    g_q_bias = jnp.sum(dq_rows, axis=(0, 2), dtype=jnp.float32).reshape(-1)
    g_v_bias = jnp.sum(dv_rows[:, :fresh_pairs], axis=(0, 2), dtype=jnp.float32).reshape(-1)
    d_normed = jnp.einsum("rpsc,dpc->rsd", d_project, w_pairs, preferred_element_type=jnp.float32)
    d_tok_norm, g_attn_gain, g_attn_shift = first_back(d_normed)
    grad_tokens = d_middle + d_tok_norm
    small_sums = lax.psum(
        (
            g_attn_gain,
            g_attn_shift,
            g_q_bias,
            g_v_bias,
            g_out_bias,
            g_mlp_gain,
            g_mlp_shift,
            g_up_bias,
            g_down_bias,
        ),
        ("seq", "head"),
    )
    shards = (
        lax.psum_scatter(g_qkv.astype(jnp.bfloat16), "seq", scatter_dimension=0, tiled=True).astype(
            jnp.float32
        ),
        lax.psum_scatter(g_out.astype(jnp.bfloat16), "seq", scatter_dimension=0, tiled=True).astype(
            jnp.float32
        ),
        lax.psum_scatter(g_up.astype(jnp.bfloat16), "seq", scatter_dimension=0, tiled=True).astype(
            jnp.float32
        ),
        lax.psum_scatter(
            g_down.astype(jnp.bfloat16), "seq", scatter_dimension=0, tiled=True
        ).astype(jnp.float32),
    )
    reduced = (
        lax.psum(shards[0].astype(jnp.bfloat16), "head").astype(jnp.float32),
        lax.psum(shards[1].astype(jnp.bfloat16), "head").astype(jnp.float32),
        lax.psum(shards[2].astype(jnp.bfloat16), "head").astype(jnp.float32),
        lax.psum(shards[3].astype(jnp.bfloat16), "head").astype(jnp.float32),
    )
    return (
        layer_out,
        grad_tokens,
        grad_skip,
        small_sums[0],
        small_sums[1],
        reduced[0],
        small_sums[2],
        small_sums[3],
        reduced[1],
        small_sums[4],
        small_sums[5],
        small_sums[6],
        reduced[2],
        small_sums[7],
        reduced[3],
        small_sums[8],
    )


def pick(array, index):
    return lax.dynamic_index_in_dim(array, index, 0, keepdims=False)


def gate(first, second):
    return lax.optimization_barrier((first, second))


def after(value, *others):
    return lax.optimization_barrier((value, *others))[0]


def add_up(parts):
    total = parts[0].astype(F32)
    for part in parts[1:]:
        total = total + part.astype(F32)
    return total.astype(BF16)


def across_cores(array):
    return lax.ppermute(array, "seq", [(i, i ^ 1) for i in range(8)])


def group_swap(array, core_zero, core_one):
    pairs = [(4 * s + z, 4 * s + (z ^ (core_one if s & 1 else core_zero))) for s in range(8) for z in range(4)]
    return lax.ppermute(array, ("seq", "head"), pairs)


def near_swap(array):
    return group_swap(array, 1, 3)


def far_swap(array):
    return group_swap(array, 3, 1)


def across_swap(array):
    return group_swap(array, 2, 2)


def plane_swap(array, core_zero, core_one):
    return lax.ppermute(array, "seq", [(s, s ^ (core_one if s & 1 else core_zero)) for s in range(8)])


def first_hop(array):
    return plane_swap(array, 2, 4)


def second_hop(array):
    return plane_swap(array, 4, 2)


def plane_away(pairs):
    return jnp.concatenate([add_up([a[:2], b[:2]]) for a, b in pairs], axis=1)


def plane_stay(pairs):
    return jnp.concatenate([add_up([a[2:], b[2:]]) for a, b in pairs], axis=1)


def group_first(blocks, me, core):
    near, far = 1 + 2 * core, 3 - 2 * core
    take = lambda d: pick(blocks, me ^ d)
    return jnp.stack([take(near), take(2)]), jnp.stack([take(0), take(far)])


def by_owner(own, far, near, me, core):
    one, three = jnp.where(core == 0, near[0], far), jnp.where(core == 0, far, near[0])
    by_distance = [own, one, near[1], three]
    return [lax.select_n(me, *(by_distance[q ^ m] for m in range(4))) for q in range(4)]


def fits(sizes):
    return sizes == (8, 4)


def row_body(
    tokens,
    skip_values,
    segments,
    token_mask,
    attn_gain,
    attn_shift,
    w_qkv,
    q_bias,
    v_bias,
    w_out,
    out_bias,
    mlp_gain,
    mlp_shift,
    w_up,
    up_bias,
    w_down,
    down_bias,
    cotangent,
):
    me = lax.axis_index("head")
    seq = lax.axis_index("seq")
    core, plane = seq & 1, seq >> 1
    near, far = 1 + 2 * core, 3 - 2 * core
    at = jnp.stack([me, core, plane]).astype(jnp.int32)
    rows, part, width = tokens.shape
    length = rows * part
    fresh = width // 2
    ff = w_up.shape[1]
    strip = width // 8
    up_row = up_bias.astype(F32).reshape(1, ff)
    vecs = jnp.stack([attn_gain, attn_shift, out_bias, mlp_gain, mlp_shift, down_bias, down_bias, down_bias]).astype(F32)
    qkv_bias = jnp.concatenate([q_bias, jnp.zeros_like(q_bias), v_bias]).astype(F32)
    scale = jnp.where(jnp.arange(w_qkv.shape[1]) < width, Q_SCALE, 1.0).astype(F32)
    affine = jnp.stack([qkv_bias, scale])

    def forward(array, got):
        return jnp.stack([array, got[1]])

    code = (segments * 2 + token_mask).astype(BF16)
    code = jnp.broadcast_to(jnp.pad(code, ((0, 0), (0, width - part)))[:, None], (rows, CODE_ROWS, width))
    tokens_at = lambda d: jnp.concatenate([pick(tokens, me ^ d), pick(code, me ^ d)])
    pro = lambda way, piece, so_far: project(at, way, piece, vecs, w_qkv, affine, length, so_far)
    near_x = tokens_at(near)
    far_x = after(tokens_at(far), near_x)
    across_x = after(tokens_at(2), far_x)
    near_x, far_x, across_x = near_swap(near_x), far_swap(far_x), across_swap(across_x)
    so_far = pro(0, tokens_at(0), ())
    so_far = pro(1, near_x, so_far)
    so_far = pro(2, far_x, so_far)
    (across_x, so_far), (skip_values, cotangent) = gate((across_x, so_far), (skip_values, cotangent))
    skip_across = across_swap(pick(skip_values, me ^ 2))
    skip_near = near_swap(pick(skip_values, me ^ near))
    skip_far = far_swap(pick(skip_values, me ^ far))
    dy_across = across_swap(pick(cotangent, me ^ 2))
    dy_three = group_swap(pick(cotangent, me ^ 3), 3, 3)
    x, normed, proj, code_row = pro(3, across_x, so_far)
    skip = [pick(skip_values, me), skip_near, skip_far, skip_across]

    from_a = attend(at, code_row, proj, [proj], 0, 6, 12, 3, "attend_a")
    (o_a, lse_a, skip), cotangent = gate((*from_a, skip), cotangent)
    dy_one = group_swap(pick(cotangent, me ^ 1), 1, 1)
    o_b, lse_b = attend(at, code_row, proj, skip, 3, 9, 0, 3, "attend_b")
    dy = [pick(cotangent, me), dy_one, dy_across, dy_three]
    fed = feed(at, x, o_a, o_b, dy, w_out, vecs, w_up, up_row, w_down)
    y_own, y_away, y_far, down_send, down_keep, up_send, up_keep, g_up_bias, d_att, d_o, mlp_sums, out_send, out_keep = fed
    down_got = across_cores(down_send)
    up_got = across_cores(up_send)
    y_got = near_swap(y_away)
    out_got = across_cores(out_send)
    from_b = attend_back(
        at, code_row, proj, skip, o_b, d_o, lse_b, normed, w_qkv, 3, 3, 0, None, None, "attend_back_b"
    )
    from_b, (down_got, up_got, y_got, out_got) = gate(from_b, (down_got, up_got, y_got, out_got))
    b_send, b_keep, b_bias, s_own, s_away, s_far, d_normed = from_b
    lines = lambda v: v.reshape(4, -1, strip, width)
    big_pairs = [(up_got, up_keep), (lines(down_got), lines(down_keep))]
    big_away = plane_away(big_pairs)
    y_last = forward(y_far, y_got)
    (d_normed, s_away, b_send), (big_away, y_last) = gate((d_normed, s_away, b_send), (big_away, y_last))
    big_got = first_hop(big_away)
    y_last = far_swap(y_last)
    s_got = near_swap(s_away)
    b_got = across_cores(b_send)
    from_a = attend_back(
        at, code_row, proj, [proj], o_a, d_o, lse_a, normed, w_qkv, 0, 3, 0, d_normed,
        [x, vecs, d_att, mlp_sums, g_up_bias, b_bias], "attend_back_a"
    )
    from_a, (big_got, y_last, s_got, b_got) = gate(from_a, (big_got, y_last, s_got, b_got))
    a_send, a_keep, x_own, x_away, x_far, packed = from_a

    units = lambda v: v.reshape(4, -1, strip, PAIR)

    s_last = far_swap(forward(s_far, s_got))
    x_near = near_swap(x_away[0])
    x_far = far_swap(x_far)
    a_got = across_cores(a_send)
    big_half = add_up([big_got, plane_stay(big_pairs)])
    big_got = second_hop(big_half[0])
    layer_out = settle(at, [y_own, (y_got, 0), (y_last, 0), (y_last, 1)], BF16, "settle_out")
    (big_got, a_got, packed, x_away), (layer_out, s_last, x_near, x_far) = gate(
        (big_got, a_got, packed, x_away), (layer_out, s_last, x_near, x_far)
    )

    x_across = across_swap(x_away[1])
    grad_skip = settle(at, [s_own, (s_got, 0), (s_last, 0), (s_last, 1)], F32, "settle_skip")
    rest_pairs = [(out_got, out_keep), (units(b_got), units(b_keep)), (units(a_got), units(a_keep))]
    rest_got = first_hop(plane_away(rest_pairs))
    small_got = group_swap(packed, 1, 1)
    big = add_up([big_got, big_half[1]]).reshape(2, 4, strip, width).transpose(1, 0, 2, 3)
    big_send, big_keep = group_first(big, me, core)
    big_got = near_swap(big_send)
    (rest_got, packed), (small_got, grad_skip) = gate((rest_got, packed), (small_got, grad_skip))

    packed = packed + small_got
    small_got = group_swap(packed, 3, 3)
    rest_half = add_up([rest_got, plane_stay(rest_pairs)])
    rest_got = second_hop(rest_half[0])
    (rest_got, big_got), (x_across, small_got) = gate((rest_got, big_got), (x_across, small_got))
    rest = add_up([rest_got, rest_half[1]]).reshape(-1, 4, strip // 4, PAIR).transpose(1, 0, 2, 3)
    rest_send, rest_keep = group_first(rest, me, core)
    rest_got = near_swap(rest_send)
    grad_tokens = settle(at, [x_own, x_near, x_far, x_across], F32, "settle_tokens")

    big_sum = add_up([big_got, big_keep])
    big_got = far_swap(big_sum[1])
    packed = packed + after(small_got, big_sum)
    small_got = across_cores(packed)
    rest_sum = add_up([after(rest_got, big_sum, grad_tokens), rest_keep])
    rest_got = far_swap(rest_sum[1])
    big_own = add_up([after(big_got, rest_sum), big_sum[0]])
    big_far = far_swap(big_own)
    packed = packed + after(small_got, big_own)
    small_got = plane_swap(packed, 2, 2)
    rest_own = add_up([after(rest_got, big_own), rest_sum[0]])
    rest_far = far_swap(rest_own)
    big_far = jnp.stack([big_own, big_far])
    big_near = near_swap(big_far)
    packed = packed + after(small_got, rest_own)
    small_got = plane_swap(packed, 4, 4)
    rest_near = near_swap(jnp.stack([rest_own, after(rest_far, big_far)]))
    packed = (packed + small_got).reshape(-1)

    rest = jnp.concatenate(by_owner(rest_own, rest_far, rest_near, me, core), axis=1).astype(F32)
    big = by_owner(big_own, big_far[1], big_near, me, core)
    r_up = jnp.concatenate([q[0] for q in big], axis=1).astype(F32)
    r_down = jnp.concatenate([q[1] for q in big], axis=0).astype(F32)
    count = width // PAIR
    r_out = jnp.concatenate([rest[u] for u in range(count)], axis=1)
    unit_of = lambda p, n: rest[count + (p - count // 2) * 2 + n] if p >= count // 2 else rest[2 * count + 3 * p + n]
    order = [unit_of(p, n) for n in range(2) for p in range(count)] + [unit_of(p, 2) for p in range(count // 2)]
    r_qkv = jnp.concatenate(order, axis=1)
    sums = []
    for size in (width, width, width, fresh, width, width, width, ff, width):
        sums.append(packed[:size])
        packed = packed[size:]
    return (
        layer_out,
        grad_tokens,
        grad_skip,
        sums[0],
        sums[1],
        r_qkv,
        sums[2],
        sums[3],
        r_out,
        sums[4],
        sums[5],
        sums[6],
        r_up,
        sums[7],
        r_down,
        sums[8],
    )


def solution(mesh):
    sizes = (mesh.shape["seq"], mesh.shape["head"])
    return jax.shard_map(
        row_body if fits(sizes) else spread_body,
        mesh=mesh,
        in_specs=(
            P("seq", "head", None),
            P("seq", "head", None),
            P("seq", "head"),
            P("seq", "head"),
            P(),
            P(),
            P(),
            P(),
            P(),
            P(),
            P(),
            P(),
            P(),
            P(),
            P(),
            P(),
            P(),
            P("seq", "head", None),
        ),
        out_specs=(
            P("seq", "head", None),
            P("seq", "head", None),
            P("seq", "head", None),
            P(),
            P(),
            P("seq", None),
            P(),
            P(),
            P("seq", None),
            P(),
            P(),
            P(),
            P("seq", None),
            P(),
            P("seq", None),
            P(),
        ),
        check_vma=False,
    )
```

```python
import functools

import jax
import jax.numpy as jnp
from jax import lax
from jax.experimental import pallas as pl
from jax.experimental.pallas import tpu as pltpu
from jax.sharding import PartitionSpec as P

HDIM = 64
PAIR = 2 * HDIM
BLK = 256
LN2 = 0.6931471805599453
LOG2E = 1.4426950408889634
Q_SCALE = LOG2E * HDIM**-0.5
BF16 = jnp.bfloat16
F32 = jnp.float32
VMEM_BYTES = 56 << 20
CODE_ROWS = 8
GAIN_ROWS, Q_ROWS, V_ROWS, SUM_ROWS = 6, 12, 18, 72
ATTN_GAIN, ATTN_SHIFT, OUT_BIAS, MLP_GAIN, MLP_SHIFT, DOWN_BIAS = (slice(n, n + 1) for n in range(6))


def dot(left, right, left_dim, right_dim):
    return lax.dot_general(
        left, right, (((left_dim,), (right_dim,)), ((), ())), preferred_element_type=F32
    )


def nn(left, right):
    return dot(left, right, 1, 0)


def nt(left, right):
    return dot(left, right, 1, 1)


def tn(left, right):
    return dot(left, right, 0, 0)


def call(kernel, name, grid, in_specs, out_specs, out_shape, scratch=(), flops=0, moved=0, aliases=None):
    return pl.pallas_call(
        kernel,
        name=name,
        grid_spec=pltpu.PrefetchScalarGridSpec(
            num_scalar_prefetch=1,
            grid=grid,
            in_specs=in_specs,
            out_specs=out_specs,
            scratch_shapes=list(scratch),
        ),
        out_shape=out_shape,
        input_output_aliases=aliases or {},
        cost_estimate=pl.CostEstimate(flops=flops, bytes_accessed=moved, transcendentals=0),
        compiler_params=pltpu.CompilerParams(vmem_limit_bytes=VMEM_BYTES),
    )


def shape(dims, dtype=BF16):
    return jax.ShapeDtypeStruct(dims, dtype)


def whole(dims):
    return pl.BlockSpec(dims, lambda *_: (0,) * len(dims))


def once(dims):
    return pl.BlockSpec(dims, lambda *_: (0,) * len(dims), pipeline_mode=pl.Buffered(1))


def standardize(values):
    center = values - jnp.mean(values, axis=1, keepdims=True)
    rate = lax.rsqrt(jnp.mean(center * center, axis=1, keepdims=True) + EPSILON)
    return center * rate, rate


def standardize_back(grad, unit, rate):
    mean_grad = jnp.mean(grad, axis=1, keepdims=True)
    mean_dot = jnp.mean(grad * unit, axis=1, keepdims=True)
    return rate * (grad - mean_grad - unit * mean_dot)


def column_sums(values):
    return jnp.sum(values, axis=0, keepdims=True)


def ways(core):
    return 0, 1 + 2 * core, 3 - 2 * core, 2


def block_rows(place, d, size):
    return pl.ds(pl.multiple_of((place ^ d) * size, size), size)


def each_way(at_ref, refs):
    return [(block_rows(at_ref[0], d, ref.shape[0]), ref) for d, ref in zip(ways(at_ref[1]), refs)]


def deal_out(at_ref, source_ref, own_ref, away_ref, far_ref):
    place, part = at_ref[0], own_ref.shape[0]
    own, near, far, across = (source_ref[block_rows(place, d, part), :] for d in ways(at_ref[1]))
    own_ref[...] = own.astype(own_ref.dtype)
    away_ref[0] = near.astype(own_ref.dtype)
    away_ref[1] = across.astype(own_ref.dtype)
    far_ref[...] = far.astype(own_ref.dtype)


def piece_specs(pieces, rows, cols, at=lambda *index: (0, 0)):
    specs, arrays = [], []
    for piece in pieces:
        if isinstance(piece, tuple):
            array, number = piece
            specs.append(pl.BlockSpec((None, rows, cols), lambda *index, n=number: (n,) + at(*index)))
        else:
            array = piece
            specs.append(pl.BlockSpec((rows, cols), at))
        arrays.append(array)
    return specs, arrays


def project_kernel(at_ref, x_ref, vec_ref, w_ref, affine_ref, *refs):
    row_ref, normed_ref, proj_ref, code_ref = refs[-4:]
    part = row_ref.shape[0]
    tokens = x_ref[:part, :]
    unit, _ = standardize(tokens.astype(F32))
    normed = (unit * vec_ref[ATTN_GAIN] + vec_ref[ATTN_SHIFT]).astype(BF16)
    row_ref[...] = tokens
    normed_ref[...] = normed
    proj_ref[...] = ((nn(normed, w_ref[...]) + affine_ref[0:1, :]) * affine_ref[1:2, :]).astype(BF16)
    code_ref[...] = x_ref[part : part + CODE_ROWS, :part].astype(F32)[:8].astype(jnp.int32)


def project(at, way, piece, vecs, w, affine, length, so_far):
    part, width = length // 4, piece.shape[1]
    cols = w.shape[1]
    place = lambda at: at[0] ^ ways(at[1])[way]
    block = lambda n: pl.BlockSpec((part, n), lambda i, at: (place(at), 0))
    held = [pl.BlockSpec(memory_space=pl.ANY)] * len(so_far)
    return call(
        project_kernel,
        "project",
        (1,),
        [whole((part + CODE_ROWS, width)), whole(vecs.shape), whole((width, cols)), whole(affine.shape)] + held,
        [block(width), block(width), block(cols), pl.BlockSpec((8, part), lambda i, at: (0, place(at)))],
        [shape((length, width)), shape((length, width)), shape((length, cols)), shape((8, length), jnp.int32)],
        flops=2 * part * width * cols,
        moved=2 * (part * (3 * width + cols) + width * cols),
        aliases={5 + n: n for n in range(len(so_far))},
    )(at, piece, vecs, w, affine, *so_far)


def fill_bias(code_ref, bias_ref):
    length = code_ref.shape[1]
    code = code_ref[0:1, :]
    column = jnp.transpose(jnp.broadcast_to(code, (128, length)))
    for i in range(length // BLK):
        q_doc = column[i * BLK : (i + 1) * BLK, :1] >> 1
        for j in range(i + 1):
            k_code = code[:, j * BLK : (j + 1) * BLK]
            same = q_doc == (k_code >> 1)
            real = (k_code & 1) == 1
            if i == j:
                row_at = lax.broadcasted_iota(jnp.int32, (BLK, BLK), 0)
                col_at = lax.broadcasted_iota(jnp.int32, (BLK, BLK), 1)
                allowed = same & (col_at <= row_at) & (real | (col_at == row_at))
            else:
                allowed = same & real
            bias_ref[i * BLK : (i + 1) * BLK, j * BLK : (j + 1) * BLK] = jnp.where(allowed, 0.0, MASKED)


def halves(pair, other):
    first = lax.broadcasted_iota(jnp.int32, pair.shape, 1) < HDIM
    return jnp.where(first, pair, other), jnp.where(first, other, pair)


def gather_values(me_ref, v_refs, value_ref):
    if len(v_refs) == 1:
        return v_refs[0][...]
    for rows, ref in each_way(me_ref, v_refs):
        value_ref[rows, :] = ref[...]
    return value_ref[...]


def forward_kernel(count, me_ref, code_ref, q_ref, k_ref, *refs):
    v_refs, (o_ref, lse_ref, bias_ref, value_ref) = refs[:count], refs[count:]

    @pl.when(pl.program_id(0) == 0)
    def _():
        fill_bias(code_ref, bias_ref)

    length = q_ref.shape[0]
    v_pair = gather_values(me_ref, v_refs, value_ref)
    k_pair = k_ref[...]
    keys = halves(k_pair, jnp.zeros_like(k_pair))
    vals = halves(v_pair, jnp.ones_like(v_pair))
    first = lax.broadcasted_iota(jnp.int32, (BLK, PAIR), 1) < HDIM
    for i in range(length // BLK):
        end = (i + 1) * BLK
        rows = slice(i * BLK, end)
        q = q_ref[rows, :]
        outs, lses = [], []
        for h in range(2):
            scores = nt(q, keys[h][:end]) + bias_ref[rows, :end]
            top = jnp.max(scores, axis=1, keepdims=True)
            weights = jnp.exp2(scores - top).astype(BF16)
            mixed = nn(weights, vals[h][:end])
            total = pltpu.roll(mixed, HDIM, 1)
            outs.append(mixed / total)
            lses.append(top + jnp.log2(total))
        o_ref[rows, :] = jnp.where(first, outs[0], outs[1]).astype(BF16)
        lse_ref[rows, :] = jnp.where(first, lses[0], lses[1])


def backward_kernel(count, first_call, last_call, split, me_ref, code_ref, q_ref, k_ref, *refs):
    refs = list(refs)
    take = lambda n: [refs.pop(0) for _ in range(n)]
    v_refs = take(count)
    o_ref, do_ref, lse_ref, normed_ref = take(4)
    w_refs = take(2 if split else 3)
    before_ref = None if first_call else take(1)[0]
    if last_call:
        x_ref, vec_ref, d_att_ref, mlp_sums_ref, up_sums_ref, other_sums_ref = take(6)
    send_ref, keep_ref = take(2)
    bias_sums_ref = None if last_call else take(1)[0]
    piece_refs = take(3) if split else []
    if last_call:
        *y_refs, packed_ref = take(4)
    else:
        (after_ref,) = take(1)
    bias_ref, value_ref, dkt_ref, dvt_ref, d_ref, w_ref, acc_ref, stage_ref = refs
    step = pl.program_id(0)
    lane = lambda n: slice(n * PAIR, (n + 1) * PAIR)

    @pl.when(step == 0)
    def _():
        fill_bias(code_ref, bias_ref)
        acc_ref[...] = jnp.zeros_like(acc_ref) if first_call else before_ref[...]

    length = q_ref.shape[0]
    v_pair = gather_values(me_ref, v_refs, value_ref)
    k_pair = k_ref[...]
    zero = jnp.zeros_like(k_pair)
    keys = halves(k_pair, zero)
    vals = halves(v_pair, zero)
    first = lax.broadcasted_iota(jnp.int32, (BLK, PAIR), 1) < HDIM
    blocks = length // BLK
    for i in reversed(range(blocks)):
        end = (i + 1) * BLK
        rows = slice(i * BLK, end)
        q, do = q_ref[rows, :], do_ref[rows, :]
        q_t, do_t = jnp.transpose(q), jnp.transpose(do)
        prod = do.astype(F32) * o_ref[rows, :].astype(F32)
        dq = None
        for h in range(2):
            head = slice(h * HDIM, (h + 1) * HDIM)
            lse = lse_ref[rows, h * HDIM : h * HDIM + 1]
            mine = first if h == 0 else ~first
            delta = jnp.sum(jnp.where(mine, prod, 0.0), axis=1, keepdims=True)
            probs = jnp.exp2(nt(q, keys[h][:end]) + bias_ref[rows, :end] - lse)
            d_scores = (probs * (nt(do, vals[h][:end]) - delta)).astype(BF16)
            part = nn(d_scores, keys[h][:end])
            dq = part if dq is None else dq + part
            dv = nn(do_t[head], probs.astype(BF16))
            dk = nn(q_t[head], d_scores)
            if i == blocks - 1:
                dvt_ref[head, :] = dv
                dkt_ref[head, :] = dk
            else:
                dvt_ref[head, :end] += dv
                dkt_ref[head, :end] += dk
        d_ref[rows, lane(0)] = (dq * HDIM**-0.5).astype(BF16)
    d_ref[:, lane(1)] = jnp.transpose(dkt_ref[...] * LN2).astype(BF16)
    dv = jnp.transpose(dvt_ref[...]).astype(BF16)
    if split:
        value_ref[...] = dv
        deal_out(me_ref, value_ref, *piece_refs)
    else:
        d_ref[:, lane(2)] = dv
    for n, ref in enumerate(w_refs):
        w_ref[:, lane(n)] = ref[...]
    grad = d_ref[...]
    sums = column_sums(grad.astype(F32))
    if last_call:
        packed_ref[pl.ds(Q_ROWS + step, 1), :] = sums[:, lane(0)]
        packed_ref[pl.ds(V_ROWS + step, 1), :] = sums[:, lane(2)]
    else:
        bias_sums_ref[0] = sums
    acc_ref[...] += nt(grad, w_ref[...])
    store_units(tn(normed_ref[...], grad), me_ref, stage_ref, send_ref, keep_ref, (0,))

    @pl.when(step == pl.num_programs(0) - 1)
    def _():
        if last_call:
            total = acc_ref[...]
            unit, rate = standardize(x_ref[...].astype(F32))
            rows_of = lambda ref, row: [ref[row : row + 1, lane(n)] for n in range(ref.shape[1] // PAIR)]
            for first_row, vector in ((0, column_sums(total * unit)), (GAIN_ROWS, column_sums(total))):
                for n in range(GAIN_ROWS):
                    packed_ref[first_row + n : first_row + n + 1, :] = vector[:, lane(n)]
            others = [other_sums_ref[p, :, lane(0)] for p in range(other_sums_ref.shape[0])]
            tail_rows = rows_of(mlp_sums_ref, 2) + rows_of(mlp_sums_ref, 0) + rows_of(mlp_sums_ref, 1)
            tail_rows += rows_of(up_sums_ref, 0) + rows_of(mlp_sums_ref, 3)
            for first_row, values in ((Q_ROWS + len(others), others), (V_ROWS + len(others), tail_rows)):
                for n, value in enumerate(values):
                    packed_ref[first_row + n : first_row + n + 1, :] = value
            acc_ref[...] = d_att_ref[...].astype(F32) + standardize_back(total * vec_ref[ATTN_GAIN], unit, rate)
            deal_out(me_ref, acc_ref, *y_refs)
        else:
            after_ref[...] = acc_ref[...]


def pair_specs(length, offset):
    return pl.BlockSpec((length, PAIR), lambda p, me: (0, p + offset))


def value_specs(values, length, offset):
    if len(values) == 1:
        return [pair_specs(length, offset)], values
    return piece_specs(values, length // 4, PAIR, lambda p, me: (0, p))


def attend(me, code, proj, values, q_at, k_at, v_at, pairs, name):
    length = proj.shape[0]
    v_specs, v_arrays = value_specs(values, length, v_at)
    return call(
        functools.partial(forward_kernel, len(values)),
        name,
        (pairs,),
        [whole((8, length)), pair_specs(length, q_at), pair_specs(length, k_at)]
        + v_specs,
        [pair_specs(length, 0)] * 2,
        [shape((length, pairs * PAIR)), shape((length, pairs * PAIR), F32)],
        [pltpu.VMEM((length, length), F32), pltpu.VMEM((length, PAIR), BF16)],
        flops=pairs * 24 * length * length * PAIR,
        moved=pairs * length * PAIR * 12,
    )(me, code, proj, proj, *v_arrays)


def attend_back(at, code, proj, values, o, do, lse, normed, w, pair, pairs, o_at, before, last, name):
    length, width = normed.shape
    count = width // PAIR
    split = len(values) > 1
    units = 2 if split else 3
    cols = units * PAIR
    strip, part = width // 8, length // 4
    full = once((length, width))
    v_specs, v_arrays = value_specs(values, length, 2 * count + pair)
    w_spec = lambda offset: pl.BlockSpec((width, PAIR), lambda p, at: (0, p + offset))
    grads = pl.BlockSpec((4, 1, units, strip, PAIR), lambda p, at: (0, p, 0, 0, 0))
    in_specs = (
        [whole((8, length)), pair_specs(length, pair), pair_specs(length, count + pair)]
        + v_specs
        + [pair_specs(length, o_at), pair_specs(length, pair), pair_specs(length, o_at), full]
        + [w_spec(n * count + pair) for n in range(units)]
    )
    args = [code, proj, proj, *v_arrays, o, do, lse, normed] + [w] * units
    out_specs = [grads, grads]
    out_shape = [shape((4, pairs, units, strip, PAIR))] * 2
    if last is None:
        out_specs.append(pl.BlockSpec((1, 1, cols), lambda p, at: (p, 0, 0)))
        out_shape.append(shape((pairs, 1, cols), F32))
    if before is not None:
        in_specs.append(full)
        args.append(before)
    if last is not None:
        in_specs += [full, once(last[1].shape), full] + [once(v.shape) for v in last[3:]]
        args += last
    if split:
        one = pl.BlockSpec((part, PAIR), lambda p, at: (0, p))
        out_specs += [one, pl.BlockSpec((2, part, PAIR), lambda p, at: (0, 0, p)), one]
        out_shape += [shape((part, pairs * PAIR)), shape((2, part, pairs * PAIR)), shape((part, pairs * PAIR))]
    if last is not None:
        out_specs += [once((part, width)), once((2, part, width)), once((part, width)), once((SUM_ROWS, PAIR))]
        out_shape += [shape((part, width)), shape((2, part, width)), shape((part, width)), shape((SUM_ROWS, PAIR), F32)]
    else:
        out_specs.append(full)
        out_shape.append(shape((length, width), F32))
    return call(
        functools.partial(backward_kernel, len(values), before is None, last is not None, split),
        name,
        (pairs,),
        in_specs,
        out_specs,
        out_shape,
        [
            pltpu.VMEM((length, length), F32),
            pltpu.VMEM((length, PAIR), BF16),
            pltpu.VMEM((PAIR, length), F32),
            pltpu.VMEM((PAIR, length), F32),
            pltpu.VMEM((length, cols), BF16),
            pltpu.VMEM((width, cols), BF16),
            pltpu.VMEM((length, width), F32),
            pltpu.VMEM((4, 2, strip, cols), BF16),
        ],
        flops=pairs * (30 * length * length * PAIR + 4 * length * width * cols),
        moved=pairs * length * PAIR * 18 + 12 * length * width,
    )(at, *args)


GELU_A = 0.7978845608028654
GELU_B = 0.044715


def plane_order(core):
    return 3, 1 + core, 2 - core, 0


def plane_place(chip, core):
    return jnp.where(chip == 3, 0, jnp.where(chip == 0, 3, jnp.where(chip == 1 + core, 1, 2)))


def split_store(grad, at_ref, stage_ref, send_ref, keep_ref, lead):
    core, chip = at_ref[1], at_ref[2]
    stage_ref[...] = grad.astype(BF16).reshape(stage_ref.shape)
    for j, (theirs, mine) in enumerate(zip(plane_order(1 - core), plane_order(core))):
        send_ref[(j,) + lead] = stage_ref[chip ^ theirs, 1 - core]
        keep_ref[(j,) + lead] = stage_ref[chip ^ mine, core]


def store_units(grad, at_ref, stage_ref, send_ref, keep_ref, lead):
    core, chip = at_ref[1], at_ref[2]
    stage_ref[...] = grad.astype(BF16).reshape(stage_ref.shape)
    for u in range(stage_ref.shape[3] // PAIR):
        lanes = slice(u * PAIR, (u + 1) * PAIR)
        for j, (theirs, mine) in enumerate(zip(plane_order(1 - core), plane_order(core))):
            send_ref[(j,) + lead + (u,)] = stage_ref[chip ^ theirs, 1 - core, :, lanes]
            keep_ref[(j,) + lead + (u,)] = stage_ref[chip ^ mine, core, :, lanes]


def feed_kernel(
    at_ref, x_ref, oa_ref, ob_ref, d0_ref, d1_ref, d2_ref, d3_ref, wo_ref, vec_ref,
    wu_ref, ub_ref, wd_ref,
    y_own_ref, y_away_ref, y_far_ref, down_send_ref, down_keep_ref, up_send_ref, up_keep_ref, up_bias_ref,
    d_att_ref, d_o_ref, sums_ref, out_send_ref, out_keep_ref,
    dy_ref, middle_ref, normed_ref, y_ref, acc_ref, down_stage_ref, up_stage_ref, out_stage_ref,
):
    step = pl.program_id(0)
    core = at_ref[1]

    @pl.when(step == 0)
    def _():
        for d, ref in enumerate((d0_ref, d1_ref, d2_ref, d3_ref)):
            dy_ref[block_rows(at_ref[0], d, ref.shape[0]), :] = ref[...]
        half = oa_ref.shape[1]
        middle = (
            x_ref[...].astype(F32)
            + nn(oa_ref[...], wo_ref[:half, :])
            + nn(ob_ref[...], wo_ref[half:, :])
            + vec_ref[OUT_BIAS]
        )
        middle_ref[...] = middle
        unit, _ = standardize(middle)
        normed_ref[...] = (unit * vec_ref[MLP_GAIN] + vec_ref[MLP_SHIFT]).astype(BF16)
        y_ref[...] = middle + vec_ref[DOWN_BIAS]
        acc_ref[...] = jnp.zeros_like(acc_ref)

    dy = dy_ref[...]
    pre = nn(normed_ref[...], wu_ref[...]) + ub_ref[...]
    d_act = nt(dy, wd_ref[...])
    square = pre * pre
    curve = jnp.tanh(pre * (GELU_A + (GELU_A * GELU_B) * square))
    half_up = 0.5 + 0.5 * curve
    act = (pre * half_up).astype(BF16)
    bend = (0.5 * GELU_A) + (1.5 * GELU_A * GELU_B) * square
    d_pre = (d_act * (half_up + pre * bend * (1.0 - curve * curve))).astype(BF16)
    y_ref[...] += nn(act, wd_ref[...])
    down_stage_ref[...] = tn(act, dy).astype(BF16).reshape(down_stage_ref.shape)
    down_send_ref[0] = down_stage_ref[1 - core]
    down_keep_ref[0] = down_stage_ref[core]
    up_bias_ref[...] = column_sums(d_pre.astype(F32))
    acc_ref[...] += nt(d_pre, wu_ref[...])
    split_store(tn(normed_ref[...], d_pre), at_ref, up_stage_ref, up_send_ref, up_keep_ref, (0,))

    @pl.when(step == pl.num_programs(0) - 1)
    def _():
        deal_out(at_ref, y_ref, y_own_ref, y_away_ref, y_far_ref)
        total = acc_ref[...]
        unit, rate = standardize(middle_ref[...])
        dy_f = dy_ref[...].astype(F32)
        sums_ref[0:1, :] = column_sums(total * unit)
        sums_ref[1:2, :] = column_sums(total)
        d_att = (dy_f + standardize_back(total * vec_ref[MLP_GAIN], unit, rate)).astype(BF16)
        d_att_ref[...] = d_att
        sums_ref[2:3, :] = column_sums(d_att.astype(F32))
        sums_ref[3:4, :] = column_sums(dy_f)
        d_o_ref[...] = nt(d_att, wo_ref[...]).astype(BF16)
        grad = jnp.concatenate([tn(oa_ref[...], d_att), tn(ob_ref[...], d_att)], axis=0)
        store_units(grad, at_ref, out_stage_ref, out_send_ref, out_keep_ref, ())


def feed(at, x, o_a, o_b, dy_pieces, w_out, vecs, w_up, up_bias, w_down):
    length, width = x.shape
    ff = w_up.shape[1]
    part = length // 4
    strip, shard, chunk, units = width // 8, ff // 8, ff // 4, width // PAIR
    down_send = pl.BlockSpec((1, shard, width), lambda c, at: (plane_place(c ^ at[2], 1 - at[1]), 0, 0))
    down_keep = pl.BlockSpec((1, shard, width), lambda c, at: (plane_place(c ^ at[2], at[1]), 0, 0))
    up = pl.BlockSpec((4, 1, strip, chunk), lambda c, at: (0, c, 0, 0))
    cols = pl.BlockSpec((1, chunk), lambda c, at: (0, c))
    full = once((length, width))
    dy_specs, dy_arrays = piece_specs(dy_pieces, part, width)
    return call(
        feed_kernel,
        "feed",
        (4,),
        [full, once(o_a.shape), once(o_b.shape)] + dy_specs + [once((width, width)), once(vecs.shape)]
        + [
            pl.BlockSpec((width, chunk), lambda c, at: (0, c)),
            cols,
            pl.BlockSpec((chunk, width), lambda c, at: (c, 0)),
        ],
        [once((part, width)), once((2, part, width)), once((part, width)), down_send, down_keep, up, up, cols, full, full, once((8, width)), once((4, units, strip, PAIR)), once((4, units, strip, PAIR))],
        [shape((part, width)), shape((2, part, width)), shape((part, width))]
        + [shape((4, shard, width))] * 2
        + [shape((4, 4, strip, chunk))] * 2
        + [shape((1, ff), F32), shape((length, width)), shape((length, width)), shape((8, width), F32)]
        + [shape((4, units, strip, PAIR))] * 2,
        [
            pltpu.VMEM((length, width), BF16),
            pltpu.VMEM((length, width), F32),
            pltpu.VMEM((length, width), BF16),
            pltpu.VMEM((length, width), F32),
            pltpu.VMEM((length, width), F32),
            pltpu.VMEM((2, shard, width), BF16),
            pltpu.VMEM((4, 2, strip, chunk), BF16),
            pltpu.VMEM((4, 2, strip, width), BF16),
        ],
        flops=2 * length * width * (6 * ff + 3 * width),
        moved=2 * (length * width * 7 + 4 * width * ff + 3 * width * width),
    )(at, x, o_a, o_b, *dy_arrays, w_out, vecs, w_up, up_bias, w_down)


def settle_kernel(at_ref, *refs):
    out_ref = refs[-1]
    for d, ref in zip(ways(at_ref[1]), refs[:-1]):
        out_ref[at_ref[0] ^ d] = ref[...].astype(out_ref.dtype)


def settle(at, pieces, dtype, name):
    part, width = pieces[0].shape
    rows = part // 2
    specs, arrays = piece_specs(pieces, rows, width, lambda i, at: (i, 0))
    return call(
        settle_kernel,
        name,
        (2,),
        specs,
        pl.BlockSpec((4, rows, width), lambda i, at: (0, i, 0)),
        shape((4, part, width), dtype),
        moved=4 * part * width * 6,
    )(at, *arrays)


QBLOCK = 512


EPSILON = 1e-05
MASKED = -1e30


def layer_norm(inputs, norm_gain, norm_shift):
    center = inputs - jnp.mean(inputs, axis=-1, keepdims=True)
    spread = jnp.mean(center * center, axis=-1, keepdims=True)
    return center * lax.rsqrt(spread + EPSILON) * norm_gain + norm_shift


def gelu_tanh(inputs):
    return jax.nn.gelu(inputs, approximate=True)


def split_pairs(array):
    return array.reshape(array.shape[0], array.shape[1], 2, array.shape[2] // 2)


def block_scores(q_block, k_block, seg_items, mask_items, q_start, k_end, factor):
    raw = jnp.einsum("iqhc,ikhc->ihqk", q_block, k_block, preferred_element_type=jnp.float32)
    q_pos = q_start + jnp.arange(q_block.shape[1])
    k_pos = jnp.arange(k_end)
    causal = k_pos[None, :] <= q_pos[:, None]
    diagonal = k_pos[None, :] == q_pos[:, None]
    same_doc = (
        seg_items[:, q_start : q_start + q_block.shape[1], None] == seg_items[:, None, :k_end]
    )
    allowed = same_doc & causal[None] & ((mask_items[:, None, :k_end] == 1) | diagonal[None])
    return jnp.where(allowed[:, None], raw * factor, MASKED)


def spread_body(
    tokens,
    skip_values,
    segments,
    token_mask,
    attn_gain,
    attn_shift,
    w_qkv,
    q_bias,
    v_bias,
    w_out,
    out_bias,
    mlp_gain,
    mlp_shift,
    w_up,
    up_bias,
    w_down,
    down_bias,
    cotangent,
):
    rows_here, seq_here, width = tokens.shape
    pair_width = 2 * HDIM
    pair_count = width // pair_width
    fresh_pairs = pair_count // 2
    factor = float(HDIM) ** (-0.5)
    tokens_f = tokens.astype(jnp.float32)
    normed_f, first_back = jax.vjp(
        layer_norm, tokens_f, attn_gain.astype(jnp.float32), attn_shift.astype(jnp.float32)
    )
    normed = normed_f.astype(jnp.bfloat16)
    w_pairs = w_qkv.reshape(width, 2 * pair_count + fresh_pairs, pair_width)
    project = jnp.einsum("rsd,dpc->rpsc", normed, w_pairs, preferred_element_type=jnp.float32)
    queries = (
        project[:, :pair_count] + q_bias.astype(jnp.float32).reshape(1, pair_count, 1, pair_width)
    ).astype(jnp.bfloat16)
    key_rows = project[:, pair_count : 2 * pair_count].astype(jnp.bfloat16)
    fresh = (
        project[:, 2 * pair_count :]
        + v_bias.astype(jnp.float32).reshape(1, fresh_pairs, 1, pair_width)
    ).astype(jnp.bfloat16)
    reused = skip_values.reshape(rows_here, seq_here, fresh_pairs, pair_width).transpose(0, 2, 1, 3)
    value_rows = jnp.concatenate([fresh, reused], axis=1)
    flat_shape = (rows_here * pair_count, seq_here, pair_width)
    q_items, k_items, v_items = (
        lax.all_to_all(
            queries.reshape(flat_shape), "head", split_axis=0, concat_axis=1, tiled=True
        ),
        lax.all_to_all(
            key_rows.reshape(flat_shape), "head", split_axis=0, concat_axis=1, tiled=True
        ),
        lax.all_to_all(
            value_rows.reshape(flat_shape), "head", split_axis=0, concat_axis=1, tiled=True
        ),
    )
    seg_rows, mask_rows = (
        lax.all_gather(segments, "head", axis=1, tiled=True),
        lax.all_gather(token_mask, "head", axis=1, tiled=True),
    )
    item_count = q_items.shape[0]
    length = q_items.shape[1]
    item_row = (lax.axis_index("head") * item_count + jnp.arange(item_count)) // pair_count
    picker = (item_row[:, None] == jnp.arange(rows_here)[None, :]).astype(jnp.int32)
    seg_items = jnp.sum(picker[:, :, None] * seg_rows[None], axis=1)
    mask_items = jnp.sum(picker[:, :, None] * mask_rows[None], axis=1)
    q_split = split_pairs(q_items)
    k_split = split_pairs(k_items)
    v_split = split_pairs(v_items)
    block_count = length // QBLOCK
    mixed_blocks = []
    log_sums = []
    for block_id in range(block_count):
        q_start = block_id * QBLOCK
        k_end = q_start + QBLOCK
        scores = block_scores(
            q_split[:, q_start:k_end],
            k_split[:, :k_end],
            seg_items,
            mask_items,
            q_start,
            k_end,
            factor,
        )
        row_max = jnp.max(scores, axis=-1, keepdims=True)
        exp_scores = jnp.exp(scores - row_max)
        row_sum = jnp.sum(exp_scores, axis=-1, keepdims=True)
        soft_probs = (exp_scores / row_sum).astype(jnp.bfloat16)
        mixed = jnp.einsum(
            "ihqk,ikhc->iqhc", soft_probs, v_split[:, :k_end], preferred_element_type=jnp.float32
        )
        mixed_blocks.append(mixed.astype(jnp.bfloat16).reshape(item_count, QBLOCK, pair_width))
        log_sums.append(row_max + jnp.log(row_sum))
    mixed_items = jnp.concatenate(mixed_blocks, axis=1)
    mixed_rows = lax.all_to_all(
        mixed_items, "head", split_axis=1, concat_axis=0, tiled=True
    ).reshape(rows_here, pair_count, seq_here, pair_width)
    w_out_pairs = w_out.reshape(pair_count, pair_width, width)
    attended = jnp.einsum(
        "rpsc,pcd->rsd", mixed_rows, w_out_pairs, preferred_element_type=jnp.float32
    ) + out_bias.astype(jnp.float32)
    middle = tokens_f + attended
    normed_mid, second_back = jax.vjp(
        layer_norm, middle, mlp_gain.astype(jnp.float32), mlp_shift.astype(jnp.float32)
    )
    normed_two = normed_mid.astype(jnp.bfloat16)
    hidden = jnp.einsum(
        "rsd,df->rsf", normed_two, w_up, preferred_element_type=jnp.float32
    ) + up_bias.astype(jnp.float32)
    active_f, gelu_back = jax.vjp(gelu_tanh, hidden)
    active = active_f.astype(jnp.bfloat16)
    result = (
        middle
        + jnp.einsum("rsf,fd->rsd", active, w_down, preferred_element_type=jnp.float32)
        + down_bias.astype(jnp.float32)
    )
    layer_out = result.astype(jnp.bfloat16)
    g_down = jnp.einsum("rsf,rsd->fd", active, cotangent, preferred_element_type=jnp.float32)
    g_down_bias = jnp.sum(cotangent, axis=(0, 1), dtype=jnp.float32)
    d_active = jnp.einsum("rsd,fd->rsf", cotangent, w_down, preferred_element_type=jnp.float32)
    d_hidden = gelu_back(d_active)[0].astype(jnp.bfloat16)
    g_up_bias = jnp.sum(d_hidden, axis=(0, 1), dtype=jnp.float32)
    g_up = jnp.einsum("rsd,rsf->df", normed_two, d_hidden, preferred_element_type=jnp.float32)
    d_normed_two = jnp.einsum("rsf,df->rsd", d_hidden, w_up, preferred_element_type=jnp.float32)
    d_mid_norm, g_mlp_gain, g_mlp_shift = second_back(d_normed_two)
    d_middle = cotangent.astype(jnp.float32) + d_mid_norm
    d_att = d_middle.astype(jnp.bfloat16)
    g_out_bias = jnp.sum(d_att, axis=(0, 1), dtype=jnp.float32)
    g_out = jnp.einsum(
        "rpsc,rsd->pcd", mixed_rows, d_att, preferred_element_type=jnp.float32
    ).reshape(width, width)
    d_mixed = (
        jnp.einsum("rsd,pcd->rpsc", d_att, w_out_pairs, preferred_element_type=jnp.float32)
        .astype(jnp.bfloat16)
        .reshape(flat_shape)
    )
    d_items = lax.all_to_all(d_mixed, "head", split_axis=0, concat_axis=1, tiled=True)
    d_split = split_pairs(d_items)
    dk_total = jnp.zeros((item_count, length, 2, HDIM), jnp.float32)
    dv_total = jnp.zeros((item_count, length, 2, HDIM), jnp.float32)
    dq_blocks = []
    for block_id in range(block_count):
        q_start = block_id * QBLOCK
        k_end = q_start + QBLOCK
        scores = block_scores(
            q_split[:, q_start:k_end],
            k_split[:, :k_end],
            seg_items,
            mask_items,
            q_start,
            k_end,
            factor,
        )
        soft = jnp.exp(scores - log_sums[block_id])
        d_block = d_split[:, q_start:k_end]
        d_probs = jnp.einsum(
            "iqhc,ikhc->ihqk", d_block, v_split[:, :k_end], preferred_element_type=jnp.float32
        )
        delta = jnp.sum(d_probs * soft, axis=-1, keepdims=True)
        d_raw = (soft * (d_probs - delta) * factor).astype(jnp.bfloat16)
        dq_blocks.append(
            jnp.einsum(
                "ihqk,ikhc->iqhc", d_raw, k_split[:, :k_end], preferred_element_type=jnp.float32
            )
        )
        dk_total = dk_total.at[:, :k_end].add(
            jnp.einsum(
                "ihqk,iqhc->ikhc",
                d_raw,
                q_split[:, q_start:k_end],
                preferred_element_type=jnp.float32,
            )
        )
        dv_total = dv_total.at[:, :k_end].add(
            jnp.einsum(
                "ihqk,iqhc->ikhc",
                soft.astype(jnp.bfloat16),
                d_block,
                preferred_element_type=jnp.float32,
            )
        )
    item_shape = (item_count, length, pair_width)
    dq_items = jnp.concatenate(dq_blocks, axis=1).astype(jnp.bfloat16).reshape(item_shape)
    dk_items = dk_total.astype(jnp.bfloat16).reshape(item_shape)
    dv_items = dv_total.astype(jnp.bfloat16).reshape(item_shape)
    dq_rows, dk_rows, dv_rows = (
        lax.all_to_all(dq_items, "head", split_axis=1, concat_axis=0, tiled=True),
        lax.all_to_all(dk_items, "head", split_axis=1, concat_axis=0, tiled=True),
        lax.all_to_all(dv_items, "head", split_axis=1, concat_axis=0, tiled=True),
    )
    row_shape = (rows_here, pair_count, seq_here, pair_width)
    dq_rows = dq_rows.reshape(row_shape)
    dk_rows = dk_rows.reshape(row_shape)
    dv_rows = dv_rows.reshape(row_shape)
    grad_skip = (
        dv_rows[:, fresh_pairs:]
        .transpose(0, 2, 1, 3)
        .reshape(rows_here, seq_here, fresh_pairs * pair_width)
        .astype(jnp.float32)
    )
    d_project = jnp.concatenate([dq_rows, dk_rows, dv_rows[:, :fresh_pairs]], axis=1)
    g_qkv = jnp.einsum(
        "rsd,rpsc->dpc", normed, d_project, preferred_element_type=jnp.float32
    ).reshape(width, -1)
    g_q_bias = jnp.sum(dq_rows, axis=(0, 2), dtype=jnp.float32).reshape(-1)
    g_v_bias = jnp.sum(dv_rows[:, :fresh_pairs], axis=(0, 2), dtype=jnp.float32).reshape(-1)
    d_normed = jnp.einsum("rpsc,dpc->rsd", d_project, w_pairs, preferred_element_type=jnp.float32)
    d_tok_norm, g_attn_gain, g_attn_shift = first_back(d_normed)
    grad_tokens = d_middle + d_tok_norm
    small_sums = lax.psum(
        (
            g_attn_gain,
            g_attn_shift,
            g_q_bias,
            g_v_bias,
            g_out_bias,
            g_mlp_gain,
            g_mlp_shift,
            g_up_bias,
            g_down_bias,
        ),
        ("seq", "head"),
    )
    shards = (
        lax.psum_scatter(g_qkv.astype(jnp.bfloat16), "seq", scatter_dimension=0, tiled=True).astype(
            jnp.float32
        ),
        lax.psum_scatter(g_out.astype(jnp.bfloat16), "seq", scatter_dimension=0, tiled=True).astype(
            jnp.float32
        ),
        lax.psum_scatter(g_up.astype(jnp.bfloat16), "seq", scatter_dimension=0, tiled=True).astype(
            jnp.float32
        ),
        lax.psum_scatter(
            g_down.astype(jnp.bfloat16), "seq", scatter_dimension=0, tiled=True
        ).astype(jnp.float32),
    )
    reduced = (
        lax.psum(shards[0].astype(jnp.bfloat16), "head").astype(jnp.float32),
        lax.psum(shards[1].astype(jnp.bfloat16), "head").astype(jnp.float32),
        lax.psum(shards[2].astype(jnp.bfloat16), "head").astype(jnp.float32),
        lax.psum(shards[3].astype(jnp.bfloat16), "head").astype(jnp.float32),
    )
    return (
        layer_out,
        grad_tokens,
        grad_skip,
        small_sums[0],
        small_sums[1],
        reduced[0],
        small_sums[2],
        small_sums[3],
        reduced[1],
        small_sums[4],
        small_sums[5],
        small_sums[6],
        reduced[2],
        small_sums[7],
        reduced[3],
        small_sums[8],
    )


def pick(array, index):
    return lax.dynamic_index_in_dim(array, index, 0, keepdims=False)


def gate(first, second):
    return lax.optimization_barrier((first, second))


def after(value, *others):
    return lax.optimization_barrier((value, *others))[0]


def add_up(parts):
    total = parts[0].astype(F32)
    for part in parts[1:]:
        total = total + part.astype(F32)
    return total.astype(BF16)


def across_cores(array):
    return lax.ppermute(array, "seq", [(i, i ^ 1) for i in range(8)])


def group_swap(array, core_zero, core_one):
    pairs = [(4 * s + z, 4 * s + (z ^ (core_one if s & 1 else core_zero))) for s in range(8) for z in range(4)]
    return lax.ppermute(array, ("seq", "head"), pairs)


def near_swap(array):
    return group_swap(array, 1, 3)


def far_swap(array):
    return group_swap(array, 3, 1)


def across_swap(array):
    return group_swap(array, 2, 2)


def plane_swap(array, core_zero, core_one):
    return lax.ppermute(array, "seq", [(s, s ^ (core_one if s & 1 else core_zero)) for s in range(8)])


def first_hop(array):
    return plane_swap(array, 2, 4)


def second_hop(array):
    return plane_swap(array, 4, 2)


def plane_away(pairs):
    return jnp.concatenate([add_up([a[:2], b[:2]]) for a, b in pairs], axis=1)


def plane_stay(pairs):
    return jnp.concatenate([add_up([a[2:], b[2:]]) for a, b in pairs], axis=1)


def group_first(blocks, me, core):
    near, far = 1 + 2 * core, 3 - 2 * core
    take = lambda d: pick(blocks, me ^ d)
    return jnp.stack([take(near), take(2)]), jnp.stack([take(0), take(far)])


def by_owner(own, far, near, me, core):
    one, three = jnp.where(core == 0, near[0], far), jnp.where(core == 0, far, near[0])
    by_distance = [own, one, near[1], three]
    return [lax.select_n(me, *(by_distance[q ^ m] for m in range(4))) for q in range(4)]


def fits(sizes):
    return sizes == (8, 4)


def row_body(
    tokens,
    skip_values,
    segments,
    token_mask,
    attn_gain,
    attn_shift,
    w_qkv,
    q_bias,
    v_bias,
    w_out,
    out_bias,
    mlp_gain,
    mlp_shift,
    w_up,
    up_bias,
    w_down,
    down_bias,
    cotangent,
):
    me = lax.axis_index("head")
    seq = lax.axis_index("seq")
    core, plane = seq & 1, seq >> 1
    near, far = 1 + 2 * core, 3 - 2 * core
    at = jnp.stack([me, core, plane]).astype(jnp.int32)
    rows, part, width = tokens.shape
    length = rows * part
    fresh = width // 2
    ff = w_up.shape[1]
    strip = width // 8
    up_row = up_bias.astype(F32).reshape(1, ff)
    vecs = jnp.stack([attn_gain, attn_shift, out_bias, mlp_gain, mlp_shift, down_bias, down_bias, down_bias]).astype(F32)
    qkv_bias = jnp.concatenate([q_bias, jnp.zeros_like(q_bias), v_bias]).astype(F32)
    scale = jnp.where(jnp.arange(w_qkv.shape[1]) < width, Q_SCALE, 1.0).astype(F32)
    affine = jnp.stack([qkv_bias, scale])

    def forward(array, got):
        return jnp.stack([array, got[1]])

    code = (segments * 2 + token_mask).astype(BF16)
    code = jnp.broadcast_to(jnp.pad(code, ((0, 0), (0, width - part)))[:, None], (rows, CODE_ROWS, width))
    tokens_at = lambda d: jnp.concatenate([pick(tokens, me ^ d), pick(code, me ^ d)])
    pro = lambda way, piece, so_far: project(at, way, piece, vecs, w_qkv, affine, length, so_far)
    near_x = tokens_at(near)
    far_x = after(tokens_at(far), near_x)
    across_x = after(tokens_at(2), far_x)
    near_x, far_x, across_x = near_swap(near_x), far_swap(far_x), across_swap(across_x)
    so_far = pro(0, tokens_at(0), ())
    so_far = pro(1, near_x, so_far)
    so_far = pro(2, far_x, so_far)
    (across_x, so_far), (skip_values, cotangent) = gate((across_x, so_far), (skip_values, cotangent))
    skip_across = across_swap(pick(skip_values, me ^ 2))
    skip_near = near_swap(pick(skip_values, me ^ near))
    skip_far = far_swap(pick(skip_values, me ^ far))
    dy_across = across_swap(pick(cotangent, me ^ 2))
    dy_three = group_swap(pick(cotangent, me ^ 3), 3, 3)
    x, normed, proj, code_row = pro(3, across_x, so_far)
    skip = [pick(skip_values, me), skip_near, skip_far, skip_across]

    from_a = attend(at, code_row, proj, [proj], 0, 6, 12, 3, "attend_a")
    (o_a, lse_a, skip), cotangent = gate((*from_a, skip), cotangent)
    dy_one = group_swap(pick(cotangent, me ^ 1), 1, 1)
    o_b, lse_b = attend(at, code_row, proj, skip, 3, 9, 0, 3, "attend_b")
    dy = [pick(cotangent, me), dy_one, dy_across, dy_three]
    fed = feed(at, x, o_a, o_b, dy, w_out, vecs, w_up, up_row, w_down)
    y_own, y_away, y_far, down_send, down_keep, up_send, up_keep, g_up_bias, d_att, d_o, mlp_sums, out_send, out_keep = fed
    down_got = across_cores(down_send)
    up_got = across_cores(up_send)
    y_got = near_swap(y_away)
    out_got = across_cores(out_send)
    from_b = attend_back(
        at, code_row, proj, skip, o_b, d_o, lse_b, normed, w_qkv, 3, 3, 0, None, None, "attend_back_b"
    )
    from_b, (down_got, up_got, y_got, out_got) = gate(from_b, (down_got, up_got, y_got, out_got))
    b_send, b_keep, b_bias, s_own, s_away, s_far, d_normed = from_b
    lines = lambda v: v.reshape(4, -1, strip, width)
    big_pairs = [(up_got, up_keep), (lines(down_got), lines(down_keep))]
    big_away = plane_away(big_pairs)
    y_last = forward(y_far, y_got)
    (d_normed, s_away, b_send), (big_away, y_last) = gate((d_normed, s_away, b_send), (big_away, y_last))
    big_got = first_hop(big_away)
    y_last = far_swap(y_last)
    s_got = near_swap(s_away)
    b_got = across_cores(b_send)
    from_a = attend_back(
        at, code_row, proj, [proj], o_a, d_o, lse_a, normed, w_qkv, 0, 3, 0, d_normed,
        [x, vecs, d_att, mlp_sums, g_up_bias, b_bias], "attend_back_a"
    )
    from_a, (big_got, y_last, s_got, b_got) = gate(from_a, (big_got, y_last, s_got, b_got))
    a_send, a_keep, x_own, x_away, x_far, packed = from_a

    units = lambda v: v.reshape(4, -1, strip, PAIR)

    s_last = far_swap(forward(s_far, s_got))
    x_near = near_swap(x_away[0])
    x_far = far_swap(x_far)
    a_got = across_cores(a_send)
    big_half = add_up([big_got, plane_stay(big_pairs)])
    big_got = second_hop(big_half[0])
    layer_out = settle(at, [y_own, (y_got, 0), (y_last, 0), (y_last, 1)], BF16, "settle_out")
    (big_got, a_got, packed, x_away), (layer_out, s_last, x_near, x_far) = gate(
        (big_got, a_got, packed, x_away), (layer_out, s_last, x_near, x_far)
    )

    x_across = across_swap(x_away[1])
    grad_skip = settle(at, [s_own, (s_got, 0), (s_last, 0), (s_last, 1)], F32, "settle_skip")
    rest_pairs = [(out_got, out_keep), (units(b_got), units(b_keep)), (units(a_got), units(a_keep))]
    rest_got = first_hop(plane_away(rest_pairs))
    small_got = group_swap(packed, 1, 1)
    big = add_up([big_got, big_half[1]]).reshape(2, 4, strip, width).transpose(1, 0, 2, 3)
    big_send, big_keep = group_first(big, me, core)
    big_got = near_swap(big_send)
    (rest_got, packed), (small_got, grad_skip) = gate((rest_got, packed), (small_got, grad_skip))

    packed = packed + small_got
    small_got = group_swap(packed, 3, 3)
    rest_half = add_up([rest_got, plane_stay(rest_pairs)])
    rest_got = second_hop(rest_half[0])
    (rest_got, big_got), (x_across, small_got) = gate((rest_got, big_got), (x_across, small_got))
    rest = add_up([rest_got, rest_half[1]]).reshape(-1, 4, strip // 4, PAIR).transpose(1, 0, 2, 3)
    rest_send, rest_keep = group_first(rest, me, core)
    rest_got = near_swap(rest_send)
    grad_tokens = settle(at, [x_own, x_near, x_far, x_across], F32, "settle_tokens")

    big_sum = add_up([big_got, big_keep])
    big_got = far_swap(big_sum[1])
    packed = packed + after(small_got, big_sum)
    small_got = across_cores(packed)
    rest_sum = add_up([after(rest_got, big_sum, grad_tokens), rest_keep])
    rest_got = far_swap(rest_sum[1])
    big_own = add_up([after(big_got, rest_sum), big_sum[0]])
    big_far = far_swap(big_own)
    packed = packed + after(small_got, big_own)
    small_got = plane_swap(packed, 2, 2)
    rest_own = add_up([after(rest_got, big_own), rest_sum[0]])
    rest_far = far_swap(rest_own)
    big_far = jnp.stack([big_own, big_far])
    big_near = near_swap(big_far)
    packed = packed + after(small_got, rest_own)
    small_got = plane_swap(packed, 4, 4)
    rest_near = near_swap(jnp.stack([rest_own, after(rest_far, big_far)]))
    packed = (packed + small_got).reshape(-1)

    rest = jnp.concatenate(by_owner(rest_own, rest_far, rest_near, me, core), axis=1).astype(F32)
    big = by_owner(big_own, big_far[1], big_near, me, core)
    r_up = jnp.concatenate([q[0] for q in big], axis=1).astype(F32)
    r_down = jnp.concatenate([q[1] for q in big], axis=0).astype(F32)
    count = width // PAIR
    r_out = jnp.concatenate([rest[u] for u in range(count)], axis=1)
    unit_of = lambda p, n: rest[count + (p - count // 2) * 2 + n] if p >= count // 2 else rest[2 * count + 3 * p + n]
    order = [unit_of(p, n) for n in range(2) for p in range(count)] + [unit_of(p, 2) for p in range(count // 2)]
    r_qkv = jnp.concatenate(order, axis=1)
    sums = []
    for size in (width, width, width, fresh, width, width, width, ff, width):
        sums.append(packed[:size])
        packed = packed[size:]
    return (
        layer_out,
        grad_tokens,
        grad_skip,
        sums[0],
        sums[1],
        r_qkv,
        sums[2],
        sums[3],
        r_out,
        sums[4],
        sums[5],
        sums[6],
        r_up,
        sums[7],
        r_down,
        sums[8],
    )


def solution(mesh):
    sizes = (mesh.shape["seq"], mesh.shape["head"])
    return jax.shard_map(
        row_body if fits(sizes) else spread_body,
        mesh=mesh,
        in_specs=(
            P("seq", "head", None),
            P("seq", "head", None),
            P("seq", "head"),
            P("seq", "head"),
            P(),
            P(),
            P(),
            P(),
            P(),
            P(),
            P(),
            P(),
            P(),
            P(),
            P(),
            P(),
            P(),
            P("seq", "head", None),
        ),
        out_specs=(
            P("seq", "head", None),
            P("seq", "head", None),
            P("seq", "head", None),
            P(),
            P(),
            P("seq", None),
            P(),
            P(),
            P("seq", None),
            P(),
            P(),
            P(),
            P("seq", None),
            P(),
            P("seq", None),
            P(),
        ),
        check_vma=False,
    )
```
